32 devices in a mesh: blk: 8 (over y, x, core), sub: 4 (over z).
Axes of the slice: x: 2, y: 2, z: 4, core: 2. Of those that a mesh axis runs over, the one named last changes fastest.
Arguments:
- u_flow: float32 [16, 2048, 2048], P(None, 'blk', 'sub'), may hold values from -60 to 60
- v_flow: float32 [16, 2048, 2048], P(None, 'blk', 'sub'), may hold values from -60 to 60
- thickness: float32 [16], replicated, may hold values from 0.1 to 0.5
- depth_levels: int32 [2048, 2048], P('blk', 'sub'), may hold values from 1 to 16
- block_ocean: int32 [16, 16], replicated, may hold values from 0 to 1, as said below
- coef_x: float32 [2048, 2048], P('blk', 'sub'), may hold values from 0.2 to 1
- coef_y: float32 [2048, 2048], P('blk', 'sub'), may hold values from 0.2 to 1
- coef_xy: float32 [2048, 2048], P('blk', 'sub'), may hold values from 0.2 to 1
- coef_xm: float32 [2048, 2048], P('blk', 'sub'), may hold values from 0.2 to 1
- extra_diagonal: float32 [2048, 2048], P('blk', 'sub'), may hold values from 0.02 to 2
Outputs:
- surface_height: float32 [2048, 2048], P('blk', 'sub')
- residual: float32 [2048, 2048], P('blk', 'sub')
The draws below stay inside these ranges and needn't reach their ends.
Inputs may be any that keep to these rules, and one draw needn't show every extreme that they name: `block_ocean`: in every band of 256 rows of cells that one index of blk holds, exactly three quarters of the blocks are ocean blocks.
All inputs are finite; a program needn't handle non-finite values.
Results may differ from the reference program's by a relative error of at most 0.0003.
Values sent between devices are 32-bit elements; how exact they have to be, the bound alone decides.
No kernel may reach another device: no remote copies, remote signals or barrier semaphores. Data moves between devices by JAX's collectives and lax.ppermute only.
A program may use at most 128 MiB of HBM per device.

```python
import math
import jax
import jax.numpy as jnp

BLOCK = 128
LEV = 16
ITERS = 4
CX = 256
NX = 2048
NY = 2048
NBX = 16
NBY = 16


def flow_field(seeded):
    rising = 1.0 + 2.0 * jnp.arange(NX, dtype=jnp.float32) / max(NX - 1, 1)
    values = jnp.clip(jax.random.normal(seeded, (LEV, NX, NY), jnp.float32), -5.0, 5.0)
    return values * rising[None, :, None]


def draw_u_flow(key, part):
    return flow_field(jax.random.fold_in(key, 11))


def draw_v_flow(key, part):
    return flow_field(jax.random.fold_in(key, 23))


def draw_block_ocean(key, part):
    band_rows = CX // BLOCK
    band_size = band_rows * NBY
    band_count = NBX // band_rows
    centre_x = jax.random.randint(jax.random.fold_in(key, 31), (6,), 0, NBX)
    centre_y = jax.random.randint(jax.random.fold_in(key, 37), (6,), 0, NBY)
    grid_x = jnp.arange(NBX, dtype=jnp.int32)[:, None, None]
    grid_y = jnp.arange(NBY, dtype=jnp.int32)[None, :, None]
    distance = jnp.min((grid_x - centre_x[None, None, :]) ** 2 + (grid_y - centre_y[None, None, :]) ** 2, axis=2)
    bands = distance.reshape(band_count, band_size)
    shuffle = jax.random.permutation(jax.random.fold_in(key, 41), band_size)
    shuffled = bands[:, shuffle]
    order = jnp.argsort(shuffled, axis=1, stable=True)
    chosen = shuffle[order[:, :band_size // 4]]
    band_index = jnp.arange(band_count, dtype=jnp.int32)[:, None] * jnp.ones((1, band_size // 4), jnp.int32)
    land = jnp.zeros((band_count, band_size), jnp.int32).at[band_index, chosen].set(1)
    return (1 - land).reshape(NBX, NBY).astype(jnp.int32)


def with_ends(array, rng, least, largest):
    extent = array.shape
    spot = [jax.random.randint(jax.random.fold_in(rng, axis), (), 0, extent[axis]) for axis in range(len(extent))]
    array = array.at[tuple(spot)].set(least)
    longest = extent.index(max(extent))
    spot[longest] = (spot[longest] + 1) % extent[longest]
    return array.at[tuple(spot)].set(largest)


def level_of(rng, dims, cuts, least, largest):
    def one(axis_at, shards_of):
        draws = jax.random.uniform(jax.random.fold_in(jax.random.fold_in(rng, 6), axis_at), (shards_of,), jnp.float32, least / len(cuts), largest / len(cuts))
        return jnp.repeat(jnp.exp(draws), dims[axis_at] // shards_of).reshape((-1,) + (1,) * (len(dims) - axis_at - 1))

    gain = one(*cuts[0])
    for cut in cuts[1:]:
        gain = gain * one(*cut)
    return gain


def setup_inputs(seed: int = 0) -> dict:
    key_of = jax.random.split(jax.random.key(seed), 11)
    u_flow = draw_u_flow(jax.random.fold_in(key_of[10], 71), 0)
    v_flow = draw_v_flow(jax.random.fold_in(key_of[10], 71), 0)
    thickness = jnp.clip(jnp.exp(jax.random.uniform(key_of[2], (LEV,), jnp.float32, math.log(0.1), math.log(0.5))), 0.1, 0.5)
    depth_levels = with_ends(jax.random.randint(key_of[3], (NX, NY), 1, LEV + 1), jax.random.fold_in(key_of[3], 1), 1, LEV).astype(jnp.int32)
    block_ocean = draw_block_ocean(jax.random.fold_in(key_of[10], 71), 0)
    coef_x = jnp.clip(0.2 + 0.8 * jax.random.uniform(key_of[5], (NX, NY), jnp.float32) ** level_of(key_of[5], (NX, NY), ((0, 8), (1, 4)), -0.2, 0.2), 0.2, 1.0)
    coef_y = jnp.clip(0.2 + 0.8 * jax.random.uniform(key_of[6], (NX, NY), jnp.float32) ** level_of(key_of[6], (NX, NY), ((0, 8), (1, 4)), -0.2, 0.2), 0.2, 1.0)
    coef_xy = jnp.clip(0.2 + 0.8 * jax.random.uniform(key_of[7], (NX, NY), jnp.float32) ** level_of(key_of[7], (NX, NY), ((0, 8), (1, 4)), -0.2, 0.2), 0.2, 1.0)
    coef_xm = jnp.clip(0.2 + 0.8 * jax.random.uniform(key_of[8], (NX, NY), jnp.float32) ** level_of(key_of[8], (NX, NY), ((0, 8), (1, 4)), -0.2, 0.2), 0.2, 1.0)
    extra_diagonal = jnp.clip(jnp.exp(math.log(2.0) - 4.6051702 * jax.random.uniform(key_of[9], (NX, NY), jnp.float32) ** level_of(key_of[9], (NX, NY), ((0, 8), (1, 4)), -0.2, 0.2)), 0.02, 2.0)
    return {"u_flow": u_flow, "v_flow": v_flow, "thickness": thickness, "depth_levels": depth_levels, "block_ocean": block_ocean, "coef_x": coef_x, "coef_y": coef_y, "coef_xy": coef_xy, "coef_xm": coef_xm, "extra_diagonal": extra_diagonal}


OFFSETS = ((1, 0), (-1, 0), (0, 1), (0, -1), (1, 1), (-1, -1), (1, -1), (-1, 1))


def shifted(field, offset_x, offset_y):
    padded = jnp.pad(field, 1)
    row_count, col_count = field.shape
    return padded[1 + offset_x:1 + offset_x + row_count, 1 + offset_y:1 + offset_y + col_count]


def reference(u_flow, v_flow, thickness, depth_levels, block_ocean, coef_x, coef_y, coef_xy, coef_xm, extra_diagonal):
    ocean_mask = jnp.repeat(jnp.repeat(block_ocean, BLOCK, axis=0), BLOCK, axis=1).astype(jnp.float32)
    flux_u = jnp.zeros(depth_levels.shape, jnp.float32)
    flux_v = jnp.zeros(depth_levels.shape, jnp.float32)
    for level_index in range(LEV):
        active = (depth_levels > level_index).astype(jnp.float32) * thickness[level_index]
        flux_u = flux_u + active * u_flow[level_index]
        flux_v = flux_v + active * v_flow[level_index]
    flux_u = ocean_mask * flux_u
    flux_v = ocean_mask * flux_v
    forcing = ocean_mask * (0.5 * ((shifted(flux_u, 1, 0) - shifted(flux_u, -1, 0)) + (shifted(flux_v, 0, 1) - shifted(flux_v, 0, -1))))
    weights = [coef_x, shifted(coef_x, -1, 0), coef_y, shifted(coef_y, 0, -1),
               coef_xy, shifted(coef_xy, -1, -1), coef_xm, shifted(coef_xm, -1, 1)]
    center = extra_diagonal
    for weight in weights:
        center = center + weight
    inverse = 1.0 / center

    def operate(field):
        beside = jnp.zeros(field.shape, jnp.float32)
        for offset, weight in zip(OFFSETS, weights):
            beside = beside + weight * shifted(field, offset[0], offset[1])
        return ocean_mask * (center * field - beside)

    surface_height = jnp.zeros(forcing.shape, jnp.float32)
    residual = forcing
    search = jnp.zeros(forcing.shape, jnp.float32)
    search_image = jnp.zeros(forcing.shape, jnp.float32)
    rho_old = jnp.float32(1.0)
    sigma_value = jnp.float32(0.0)
    for iteration in range(ITERS):
        scaled = residual * inverse
        applied = operate(scaled)
        rho_now = jnp.sum(residual * scaled)
        curvature = jnp.sum(scaled * applied)
        beta_ratio = rho_now / rho_old
        sigma_value = curvature - beta_ratio * beta_ratio * sigma_value
        alpha_step = rho_now / sigma_value
        rho_old = rho_now
        search = scaled + beta_ratio * search
        search_image = applied + beta_ratio * search_image
        surface_height = surface_height + alpha_step * search
        residual = residual - alpha_step * search_image
    return surface_height, residual
```

```python
import functools

import jax
import jax.numpy as jnp
from jax import lax
from jax.experimental import pallas as pl
from jax.experimental.pallas import tpu as pltpu
from jax.sharding import PartitionSpec as P

BLOCK = 128
ITERS = 4
HALO = ITERS
LANES = 128
ROWS = 8
FIELDS = 8
CHUNK = 32
F32 = jnp.float32
VMEM = pl.BlockSpec(memory_space=pltpu.VMEM)
SMEM = pl.BlockSpec(memory_space=pltpu.SMEM)
HBM = pl.BlockSpec(memory_space=pltpu.HBM)
PAIRS = [(i, j) for i in range(ITERS) for j in range(i, ITERS + 1)]


def lane_of(shape):
    return lax.broadcasted_iota(jnp.int32, shape, len(shape) - 1)


def row_of(shape):
    return lax.broadcasted_iota(jnp.int32, shape, len(shape) - 2)


def left(value):
    return pltpu.roll(value, 1, 1)


def right(value):
    return pltpu.roll(value, value.shape[1] - 1, 1)


def ocean_at(ocean_ref, row, col):
    block_rows, block_cols = ocean_ref.shape
    inside = (row >= 0) & (row < block_rows) & (col >= 0) & (col < block_cols)
    entry = ocean_ref[jnp.clip(row, 0, block_rows - 1), jnp.clip(col, 0, block_cols - 1)]
    return jnp.where(inside & (entry == 1), 1.0, 0.0).astype(F32)


def flux_kernel(
    ids, thick, ocean, u_hbm, v_hbm, depth_hbm, cx_hbm, cy_hbm, cxy_hbm, cxm_hbm, ex_hbm,
    fp_ref, cp_ref, fue_ref, pack_a, pack_b,
    u_buf, v_buf, depth, cx, cy, cxy, cxm, ex, fu, fv, sems, coef_sem,
):
    levels, row_count, col_count = u_buf.shape
    tiles = col_count // LANES
    chunks = row_count // CHUNK
    quarter = row_count // 4
    blk, sub = ids[0], ids[1]
    coef_copies = [
        pltpu.make_async_copy(src, dst, coef_sem.at[i])
        for i, (src, dst) in enumerate(
            [(depth_hbm, depth), (cx_hbm, cx), (cy_hbm, cy), (cxy_hbm, cxy), (cxm_hbm, cxm), (ex_hbm, ex)]
        )
    ]

    def flow_copies(c):
        rows = pl.ds(c * CHUNK, CHUNK)
        return (
            pltpu.make_async_copy(u_hbm.at[:, rows, :], u_buf.at[:, rows, :], sems.at[0, c]),
            pltpu.make_async_copy(v_hbm.at[:, rows, :], v_buf.at[:, rows, :], sems.at[1, c]),
        )

    for copy in coef_copies:
        copy.start()
    for c in range(chunks):
        for copy in flow_copies(c):
            copy.start()
    for copy in coef_copies:
        copy.wait()

    row8 = row_of((ROWS, col_count))
    lane8 = lane_of((ROWS, col_count))

    def center_group(g, carry):
        above_x, above_xy, above_xm = carry
        rows = pl.ds(pl.multiple_of(g * ROWS, ROWS), ROWS)
        here_x, here_y, here_xy, here_xm = cx[rows], cy[rows], cxy[rows], cxm[rows]
        shift = lambda a, b: jnp.where(row8 == 0, pltpu.roll(a, 1, 0), pltpu.roll(b, 1, 0))
        total = ex[rows] + here_x
        total = total + shift(above_x, here_x)
        total = total + here_y
        total = total + jnp.where(lane8 == 0, 0.0, left(here_y))
        total = total + here_xy
        total = total + jnp.where(lane8 == 0, 0.0, left(shift(above_xy, here_xy)))
        total = total + here_xm
        total = total + jnp.where(lane8 == col_count - 1, 0.0, right(shift(above_xm, here_xm)))
        cp_ref[rows] = total
        return here_x, here_xy, here_xm

    zero = jnp.zeros((ROWS, col_count), F32)
    lax.fori_loop(0, row_count // ROWS, center_group, (zero, zero, zero))

    block_rows = row_count // BLOCK
    for c in range(chunks):
        for copy in flow_copies(c):
            copy.wait()
        block_row = blk * block_rows + c * CHUNK // BLOCK

        def sum_group(g, _, c=c, block_row=block_row):
            rows = pl.ds(pl.multiple_of(c * CHUNK + g * ROWS, ROWS), ROWS)
            for t in range(tiles):
                lanes = pl.ds(t * LANES, LANES)
                mask = ocean_at(ocean, block_row, sub * tiles + t)
                deep = depth[rows, lanes]
                total_u = jnp.zeros((ROWS, LANES), F32)
                total_v = total_u
                for k in range(levels):
                    active = jnp.where(deep > k, thick[k], 0.0)
                    total_u = total_u + active * u_buf[k, rows, lanes]
                    total_v = total_v + active * v_buf[k, rows, lanes]
                fu[rows, lanes] = mask * total_u
                fv[rows, lanes] = mask * total_v
            return 0

        lax.fori_loop(0, CHUNK // ROWS, sum_group, 0)

    even = (sub % 2) == 0
    lane1 = lane_of((ROWS, LANES))

    def force_group(k, g, _):
        base = k * quarter + g * ROWS
        rows = pl.ds(pl.multiple_of(base, ROWS), ROWS)
        here_u, here_v = fu[rows], fv[rows]
        before = fu[pl.ds(pl.multiple_of(jnp.maximum(base - ROWS, 0), ROWS), ROWS)]
        after = fu[pl.ds(pl.multiple_of(jnp.minimum(base + ROWS, row_count - ROWS), ROWS), ROWS)]
        first, final = base == 0, base == row_count - ROWS
        up = jnp.where(row8 == 0, jnp.where(first, 0.0, pltpu.roll(before, 1, 0)), pltpu.roll(here_u, 1, 0))
        down = jnp.where(
            row8 == ROWS - 1,
            jnp.where(final, 0.0, pltpu.roll(after, ROWS - 1, 0)),
            pltpu.roll(here_u, ROWS - 1, 0),
        )
        west = jnp.where(lane8 == 0, 0.0, left(here_v))
        east = jnp.where(lane8 == col_count - 1, 0.0, right(here_v))
        change = 0.5 * ((down - up) + (east - west))
        block_row = blk * block_rows + base // BLOCK
        mask = jnp.concatenate(
            [jnp.full((ROWS, LANES), ocean_at(ocean, block_row, sub * tiles + t), F32) for t in range(tiles)], axis=1
        )
        partial = mask * change
        fp_ref[rows] = partial
        fields = [partial, cx[rows], cy[rows], cxy[rows], cxm[rows], cp_ref[rows], here_v, here_u]
        to_west = jnp.zeros((ROWS, LANES), F32)
        to_east = to_west
        for f, field in enumerate(fields):
            at = 4 * f + 32 * k
            chosen = (lane1 >= at) & (lane1 < at + HALO)
            to_west = jnp.where(chosen, pltpu.roll(field[:, :LANES], at, 1), to_west)
            to_east = jnp.where(chosen, pltpu.roll(field[:, -LANES:], (at + HALO) % LANES, 1), to_east)
        at = 4 * 6 + 32 * k
        extra = pltpu.roll(fields[4][:, :LANES], (at + 1 - HALO) % LANES, 1)
        to_west = jnp.where(lane1 == at + 1, extra, to_west)
        extra = pltpu.roll(fields[3][:, -LANES:], (at + HALO + 1) % LANES, 1)
        to_east = jnp.where(lane1 == at, extra, to_east)
        packed = pl.ds(pl.multiple_of(g * ROWS, ROWS), ROWS)
        old_a = jnp.where(even, to_east, to_west)
        old_b = jnp.where(even, to_west, to_east)
        if k == 0:
            pack_a[packed] = old_a
            pack_b[packed] = old_b
        else:
            pack_a[packed] = pack_a[packed] + old_a
            pack_b[packed] = pack_b[packed] + old_b
        return 0

    for k in range(4):
        lax.fori_loop(0, quarter // ROWS, functools.partial(force_group, k), 0)
    fue_ref[0:ROWS] = fu[0:ROWS]
    fue_ref[ROWS : 2 * ROWS] = fu[row_count - ROWS : row_count]


def side_tiles(send_a, send_b, recv_a, recv_b, even, packed):
    own_a, own_b, got_a, got_b = send_a[packed], send_b[packed], recv_a[packed], recv_b[packed]
    pick = lambda a, b: jnp.where(even, a, b)
    return pick(own_b, own_a), pick(own_a, own_b), pick(got_b, got_a), pick(got_a, got_b)


def outer_tile(from_west, from_east, f, k):
    lane1 = lane_of(from_west.shape)
    at = 4 * f + 32 * k
    east = pltpu.roll(from_east, (-at) % LANES, 1)
    west = pltpu.roll(from_west, (LANES - HALO - at) % LANES, 1)
    tile = jnp.where(lane1 < HALO, east, jnp.where(lane1 >= LANES - HALO, west, 0.0))
    if f == 3:
        extra = pltpu.roll(from_west, (LANES - HALO - 1 - 4 * 6 - 32 * k) % LANES, 1)
        tile = jnp.where(lane1 == LANES - HALO - 1, extra, tile)
    if f == 4:
        extra = pltpu.roll(from_east, (HALO - 4 * 6 - 1 - 32 * k) % LANES, 1)
        tile = jnp.where(lane1 == HALO, extra, tile)
    return tile


def force_with_sides(partial, mask, sides, k):
    own_west, own_east, from_west, from_east = sides
    lane1 = lane_of(own_west.shape)
    first, last = 4 * 6 + 32 * k, 4 * 6 + 3 + 32 * k
    outer = outer_tile(from_west, from_east, 0, k)
    tail = pltpu.roll(own_east, (-last) % LANES, 1)
    head = pltpu.roll(own_west, (LANES - 1 - first) % LANES, 1)
    change = jnp.where(lane1 == 0, -tail, jnp.where(lane1 == LANES - 1, head, 0.0))
    outer = outer + 0.5 * mask[:, -LANES:] * change
    begin = partial[:, :LANES] - jnp.where(
        lane1 == 0, 0.5 * mask[:, :LANES] * pltpu.roll(from_west, (-last) % LANES, 1), 0.0
    )
    middle = partial[:, LANES:-LANES]
    end = partial[:, -LANES:] + jnp.where(
        lane1 == LANES - 1,
        0.5 * mask[:, -2 * LANES : -LANES] * pltpu.roll(from_east, (LANES - 1 - first) % LANES, 1),
        0.0,
    )
    return jnp.concatenate([begin, middle, end, outer], axis=1)


def mask_row(ocean, block_row, sub, tiles):
    lane1 = lane_of((1, LANES))
    parts = [jnp.full((1, LANES), ocean_at(ocean, block_row, sub * tiles + t), F32) for t in range(tiles)]
    east = ocean_at(ocean, block_row, (sub + 1) * tiles)
    west = ocean_at(ocean, block_row, sub * tiles - 1)
    parts.append(jnp.where(lane1 < LANES // 2, east, west))
    return jnp.concatenate(parts, axis=1)


def edge_kernel(ids, ocean, fp, cx, cy, cxy, cxm, cp, fue, send_a, send_b, recv_a, recv_b, rows_a, rows_b):
    row_count, col_count = fp.shape
    tiles = col_count // LANES
    block_rows = row_count // BLOCK
    blk, sub = ids[0], ids[1]
    even_sub, even_blk = (sub % 2) == 0, (blk % 2) == 0
    quarter = row_count // 4
    row8 = row_of((ROWS, col_count + LANES))
    lane8 = lane_of((ROWS, col_count + LANES))
    crosses_west = (lane8 == 0) | (lane8 == col_count)
    crosses_east = (lane8 == col_count - 1) | (lane8 == col_count + LANES - 1)
    results = []
    for top in (True, False):
        base = 0 if top else row_count - ROWS
        k = base // quarter
        rows = slice(base, base + ROWS)
        packed = slice(base % quarter, base % quarter + ROWS)
        sides = side_tiles(send_a, send_b, recv_a, recv_b, even_sub, packed)
        block_row = blk * block_rows + base // BLOCK
        mask = jnp.broadcast_to(mask_row(ocean, block_row, sub, tiles), (ROWS, col_count + LANES))
        fields = [force_with_sides(fp[rows], mask, sides, k)]
        for f, field in enumerate([cx, cy, cxy, cxm, cp]):
            fields.append(jnp.concatenate([field[rows], outer_tile(sides[2], sides[3], f + 1, k)], axis=1))
        flux = jnp.concatenate(
            [fue[0:ROWS] if top else fue[ROWS : 2 * ROWS], outer_tile(sides[2], sides[3], 7, k)], axis=1
        )
        if top:
            fields[1] = jnp.where(row8 == 3, pltpu.roll(flux, 3, 0), fields[1])
            half = lambda v: v
        else:
            side = jnp.where(crosses_west, left(fields[2]) + left(pltpu.roll(fields[3], 1, 0)), 0.0)
            side = side + jnp.where(crosses_east, right(pltpu.roll(fields[4], 1, 0)), 0.0)
            fields[5] = fields[5] + jnp.where(row8 == 4, side, 0.0)
            fields[2] = jnp.where(row8 == 4, pltpu.roll(flux, 5, 0), fields[2])
            half = lambda v: pltpu.roll(v, 4, 0)
        pieces = []
        for pair in range(3):
            one, two = half(fields[2 * pair]), half(fields[2 * pair + 1])
            pieces.append(jnp.where(row8 < 4, one, pltpu.roll(two, 4, 0)))
        results.append(pieces)
    for pair in range(3):
        rows = slice(pair * ROWS, (pair + 1) * ROWS)
        rows_a[rows] = jnp.where(even_blk, results[1][pair], results[0][pair])
        rows_b[rows] = jnp.where(even_blk, results[0][pair], results[1][pair])


def basis_kernel(
    ids, ocean, fp, cx, cy, cxy, cxm, cp, fue, send_a, send_b, recv_a, recv_b, rows_a, rows_b,
    c0, c1, c2, c3, c4, center_ref, gram_ref,
    wx, wy, wxy, wxm, nx, nxy, nxm, inv, v0, v1, v2, v3,
):
    row_count, col_count = fp.shape
    tiles = col_count // LANES
    wide = col_count + LANES
    block_rows = row_count // BLOCK
    quarter = row_count // 4
    groups = row_count // ROWS
    blk, sub = ids[0], ids[1]
    even_sub, even_blk = (sub % 2) == 0, (blk % 2) == 0
    row8 = row_of((ROWS, wide))
    lane8 = lane_of((ROWS, wide))

    def at(g):
        return pl.ds(pl.multiple_of(g * ROWS, ROWS), ROWS)

    pick = lambda flag, a, b: jnp.where(flag, a, b)
    pieces = []
    for pair in range(3):
        rows = slice(pair * ROWS, (pair + 1) * ROWS)
        below = pick(even_blk, rows_a[rows], rows_b[rows])
        above = pick(even_blk, rows_b[rows], rows_a[rows])
        pieces.append(jnp.where(row8 < 4, below, pltpu.roll(above, 4, 0)))
        pieces.append(jnp.where(row8 < 4, pltpu.roll(below, 4, 0), above))
    force_out, x_out, y_out, xy_out, xm_out, center_out = pieces
    flux_below = x_out[3:4]
    flux_above = y_out[4:5]
    for k in range(4):

        def widen(g, _, k=k):
            group = k * (quarter // ROWS) + g
            rows = at(group)
            sides = side_tiles(send_a, send_b, recv_a, recv_b, even_sub, at(g))
            for f, (own, ring) in enumerate([(cx, wx), (cy, wy), (cxy, wxy), (cxm, wxm), (cp, inv)]):
                ring[at(group + 1)] = jnp.concatenate(
                    [own[rows], outer_tile(sides[2], sides[3], f + 1, k)], axis=1
                )
            mask = jnp.broadcast_to(
                mask_row(ocean, blk * block_rows + group * ROWS // BLOCK, sub, tiles), (ROWS, wide)
            )
            v0[at(group + 1)] = force_with_sides(fp[rows], mask, sides, k)
            return 0

        lax.fori_loop(0, quarter // ROWS, widen, 0)

    for ring, out in [(wx, x_out), (wy, y_out), (wxy, xy_out), (wxm, xm_out)]:
        ring[at(groups + 1)] = out
        ring[at(0)] = out

    packed_first = slice(0, ROWS)
    packed_last = slice(quarter - ROWS, quarter)
    sides_first = side_tiles(send_a, send_b, recv_a, recv_b, even_sub, packed_first)
    sides_last = side_tiles(send_a, send_b, recv_a, recv_b, even_sub, packed_last)
    flux_first = jnp.concatenate([fue[0:1], outer_tile(sides_first[2], sides_first[3], 7, 0)[0:1]], axis=1)
    flux_last = jnp.concatenate(
        [fue[2 * ROWS - 1 : 2 * ROWS], outer_tile(sides_last[2], sides_last[3], 7, 3)[ROWS - 1 : ROWS]], axis=1
    )
    mask_first = mask_row(ocean, blk * block_rows, sub, tiles)
    mask_last = mask_row(ocean, (blk + 1) * block_rows - 1, sub, tiles)
    mask_below = mask_row(ocean, (blk + 1) * block_rows, sub, tiles)
    mask_above = mask_row(ocean, blk * block_rows - 1, sub, tiles)
    v0[at(1)] = v0[at(1)] - jnp.where(row8 == 0, 0.5 * mask_first * flux_above, 0.0)
    v0[at(groups)] = v0[at(groups)] + jnp.where(row8 == ROWS - 1, 0.5 * mask_last * flux_below, 0.0)
    force_out = force_out - jnp.where(row8 == 0, 0.5 * mask_below * flux_last, 0.0)
    force_out = force_out + jnp.where(row8 == ROWS - 1, 0.5 * mask_above * flux_first, 0.0)
    v0[at(groups + 1)] = force_out
    inv[at(groups + 1)] = center_out

    crosses_west = (lane8 == 0) | (lane8 == col_count)
    crosses_east = (lane8 == col_count - 1) | (lane8 == wide - 1)

    def scale(g, _):
        ring = at(g + 1)
        before = at(g)
        shift = lambda ref: jnp.where(row8 == 0, pltpu.roll(ref[before], 1, 0), pltpu.roll(ref[ring], 1, 0))
        up_x, up_xy, up_xm = shift(wx), shift(wxy), shift(wxm)
        nx[ring] = up_x
        nxy[ring] = up_xy
        nxm[ring] = up_xm
        crosses_row = (row8 == 0) & ((g == 0) | (g == groups))
        total = inv[ring]
        total = total + jnp.where(crosses_row, up_x, 0.0)
        open_row = (row8 != 4) | (g < groups)
        total = total + jnp.where(open_row & crosses_west, left(wy[ring]), 0.0)
        total = total + jnp.where(crosses_row | (open_row & crosses_west), left(up_xy), 0.0)
        total = total + jnp.where(crosses_row | (open_row & crosses_east), right(up_xm), 0.0)
        own_row = blk * block_rows + g * ROWS // BLOCK
        own = mask_row(ocean, own_row, sub, tiles)
        mask = jnp.where(g == groups, jnp.where(row8 < 4, mask_below, mask_above), own)
        inverse = jnp.where(mask > 0.0, 1.0 / jnp.where(mask > 0.0, total, 1.0), 0.0)
        inv[ring] = inverse
        scaled = v0[ring] * inverse
        v0[ring] = scaled

        @pl.when(g < groups)
        def _():
            center_ref[at(g)] = total[:, :col_count]
            c0[at(g)] = scaled[:, :col_count]

        return 0

    lax.fori_loop(0, groups + 1, scale, 0)

    def wrap(ref):
        ref[at(0)] = ref[at(groups + 1)]
        ref[at(groups + 2)] = ref[at(1)]

    def spread(source, g):
        ring = at(g + 1)
        here, before, after = source[ring], source[at(g)], source[at(g + 2)]
        up = jnp.where(row8 == 0, pltpu.roll(before, 1, 0), pltpu.roll(here, 1, 0))
        down = jnp.where(row8 == ROWS - 1, pltpu.roll(after, ROWS - 1, 0), pltpu.roll(here, ROWS - 1, 0))
        side = wy[ring]
        total = wx[ring] * down + nx[ring] * up
        total = total + side * right(here)
        total = total + wxy[ring] * right(down) + wxm[ring] * left(down)
        total = total + left(side * here + nxy[ring] * up)
        total = total + right(nxm[ring] * up)
        return inv[ring] * total, here

    def step(source, target, out, subtract):
        def body(g, _):
            moved, here = spread(source, g)
            result = here - moved if subtract else moved
            target[at(g + 1)] = result

            @pl.when(g < groups)
            def _():
                out[at(g)] = result[:, :col_count]

            return 0

        lax.fori_loop(0, groups + 1, body, 0)
        wrap(target)

    wrap(v0)
    step(v0, v1, c1, True)
    step(v1, v2, c2, False)
    step(v2, v3, c3, False)

    def last(g, sums):
        moved, here = spread(v3, g)
        rows = at(g)
        final = moved[:, :col_count]
        c4[rows] = final
        basis = [c0[rows], c1[rows], c2[rows], here[:, :col_count], final]
        center = center_ref[rows]
        weighted = [center * b for b in basis]
        new = []
        for (i, j), total in zip(PAIRS, sums):
            product = basis[i] * weighted[j]
            part = product[:, :LANES]
            for t in range(1, tiles):
                part = part + product[:, t * LANES : (t + 1) * LANES]
            new.append(total + part)
        return tuple(new)

    empty = tuple(jnp.zeros((ROWS, LANES), F32) for _ in PAIRS)
    sums = lax.fori_loop(0, groups, last, empty)
    lane1 = lane_of((1, LANES))
    packed = jnp.zeros((1, LANES), F32)
    for index, total in enumerate(sums):
        packed = jnp.where(lane1 == index, jnp.sum(jnp.sum(total, axis=0, keepdims=True), axis=1, keepdims=True), packed)
    gram_ref[...] = jnp.broadcast_to(packed, gram_ref.shape)


def finish_kernel(gram_ref, c0, c1, c2, c3, c4, center_ref, height_ref, residual_ref):
    lane1 = lane_of((1, LANES))
    entries = jnp.sum(gram_ref[...], axis=0, keepdims=True)
    size = ITERS + 1
    gram = {}
    for index, (i, j) in enumerate(PAIRS):
        entry = jnp.sum(jnp.where(lane1 == index, entries, 0.0), axis=1, keepdims=True)
        gram[i, j] = entry
        gram[j, i] = entry
    zero = jnp.zeros((1, 1), F32)
    one = jnp.ones((1, 1), F32)

    def image(coefs):
        result = [zero, coefs[0] + coefs[1]]
        for j in range(2, size):
            own = coefs[j] if j < size - 1 else zero
            result.append(own - coefs[j - 1])
        return result

    def form(one_side, products):
        total = zero
        for a, b in zip(one_side, products):
            total = total + a * b
        return total

    scaled = [one] + [zero] * (size - 1)
    search = [zero] * size
    height = [zero] * size
    rho_old, sigma = one, zero
    for iteration in range(ITERS):
        limit = iteration + 1
        products = []
        for j in range(size):
            total = zero
            for i in range(limit):
                total = total + scaled[i] * gram[i, j]
            products.append(total)
        rho = form(scaled[:limit], products)
        curvature = form(image(scaled)[: limit + 1], products)
        beta = rho / rho_old
        sigma = curvature - beta * beta * sigma
        alpha = rho / sigma
        rho_old = rho
        search = [s + beta * q for s, q in zip(scaled, search)]
        height = [h + alpha * q for h, q in zip(height, search)]
        scaled = [s - alpha * q for s, q in zip(scaled, image(search))]

    def combine(g, _):
        rows = pl.ds(pl.multiple_of(g * ROWS, ROWS), ROWS)
        basis = [ref[rows] for ref in (c0, c1, c2, c3, c4)]
        total = height[0] * basis[0]
        for j in range(1, size - 1):
            total = total + height[j] * basis[j]
        height_ref[rows] = total
        total = scaled[0] * basis[0]
        for j in range(1, size):
            total = total + scaled[j] * basis[j]
        residual_ref[rows] = center_ref[rows] * total
        return 0

    lax.fori_loop(0, c0.shape[0] // ROWS, combine, 0)


def swap(value, axis, parity):
    peers = lax.axis_size(axis)
    pairs = []
    for i in range(parity, peers - 1, 2):
        pairs += [(i, i + 1), (i + 1, i)]
    return lax.ppermute(value, axis, pairs)


def body(u_flow, v_flow, thickness, depth_levels, block_ocean, coef_x, coef_y, coef_xy, coef_xm, extra_diagonal):
    levels, row_count, col_count = u_flow.shape
    wide = col_count + LANES
    plane = jax.ShapeDtypeStruct((row_count, col_count), F32)
    strip = jax.ShapeDtypeStruct((row_count // 4, LANES), F32)
    ids = jnp.stack([lax.axis_index("blk"), lax.axis_index("sub")]).astype(jnp.int32)
    flow = pltpu.VMEM((levels, row_count, col_count), F32)
    field = pltpu.VMEM((row_count, col_count), F32)
    fp, cp, fue, send_a, send_b = pl.pallas_call(
        flux_kernel,
        out_shape=(plane, plane, jax.ShapeDtypeStruct((2 * ROWS, col_count), F32), strip, strip),
        in_specs=[SMEM, SMEM, SMEM] + [HBM] * 8,
        out_specs=(VMEM,) * 5,
        scratch_shapes=[flow, flow, pltpu.VMEM((row_count, col_count), jnp.int32)]
        + [field] * 7
        + [pltpu.SemaphoreType.DMA((2, row_count // CHUNK)), pltpu.SemaphoreType.DMA((6,))],
        compiler_params=pltpu.CompilerParams(vmem_limit_bytes=40 << 20),
        name="flux",
    )(ids, thickness, block_ocean, u_flow, v_flow, depth_levels, coef_x, coef_y, coef_xy, coef_xm, extra_diagonal)
    recv_a, recv_b = swap(send_a, "sub", 0), swap(send_b, "sub", 1)
    edge = jax.ShapeDtypeStruct((3 * ROWS, wide), F32)
    edge_a, edge_b = pl.pallas_call(
        edge_kernel,
        out_shape=(edge, edge),
        in_specs=[SMEM, SMEM] + [VMEM] * 11,
        out_specs=(VMEM,) * 2,
        compiler_params=pltpu.CompilerParams(vmem_limit_bytes=16 << 20),
        name="edge",
    )(ids, block_ocean, fp, coef_x, coef_y, coef_xy, coef_xm, cp, fue, send_a, send_b, recv_a, recv_b)
    rows_a, rows_b = swap(edge_a, "blk", 0), swap(edge_b, "blk", 1)
    devices = lax.axis_size("blk") * lax.axis_size("sub")
    ring = pltpu.VMEM((row_count + 3 * ROWS, wide), F32)
    *basis, center, gram = pl.pallas_call(
        basis_kernel,
        out_shape=(plane,) * 6 + (jax.ShapeDtypeStruct((devices, LANES), F32),),
        in_specs=[SMEM, SMEM] + [VMEM] * 13,
        out_specs=(VMEM,) * 7,
        scratch_shapes=[ring] * 12,
        compiler_params=pltpu.CompilerParams(vmem_limit_bytes=32 << 20),
        name="basis",
    )(
        ids, block_ocean, fp, coef_x, coef_y, coef_xy, coef_xm, cp, fue,
        send_a, send_b, recv_a, recv_b, rows_a, rows_b,
    )
    gram = lax.all_to_all(gram, ("blk", "sub"), 0, 0, tiled=True)
    return pl.pallas_call(
        finish_kernel,
        out_shape=(plane, plane),
        in_specs=[VMEM] * 7,
        out_specs=(VMEM,) * 2,
        compiler_params=pltpu.CompilerParams(vmem_limit_bytes=16 << 20),
        name="finish",
    )(gram, *basis, center)


def solution(mesh):
    placed = (
        P(None, "blk", "sub"),
        P(None, "blk", "sub"),
        P(),
        P("blk", "sub"),
        P(),
        P("blk", "sub"),
        P("blk", "sub"),
        P("blk", "sub"),
        P("blk", "sub"),
        P("blk", "sub"),
    )
    return jax.shard_map(
        body,
        mesh=mesh,
        in_specs=placed,
        out_specs=(P("blk", "sub"), P("blk", "sub")),
        check_vma=False,
    )
```

```python
import functools

import jax
import jax.numpy as jnp
from jax import lax
from jax.experimental import pallas as pl
from jax.experimental.pallas import tpu as pltpu
from jax.sharding import PartitionSpec as P

BLOCK = 128
ITERS = 4
HALO = ITERS
LANES = 128
ROWS = 8
CHUNK = 32
AHEAD = 3
UNROLL = 4
F32 = jnp.float32
FLUX_LIMIT = 40 << 20
VMEM = pl.BlockSpec(memory_space=pltpu.VMEM)
SMEM = pl.BlockSpec(memory_space=pltpu.SMEM)
HBM = pl.BlockSpec(memory_space=pltpu.HBM)
PAIRS = [(i, j) for i in range(ITERS) for j in range(i, ITERS + 1)]


def lane_of(shape):
    return lax.broadcasted_iota(jnp.int32, shape, len(shape) - 1)


def row_of(shape):
    return lax.broadcasted_iota(jnp.int32, shape, len(shape) - 2)


def shifted_rows(before, here):
    return jnp.where(row_of(here.shape) == 0, before, here)


def left(value):
    return pltpu.roll(value, 1, 1)


def right(value):
    return pltpu.roll(value, value.shape[1] - 1, 1)


def down(value):
    return pltpu.roll(value, 1, 0)


def two_sum(a, b):
    total = a + b
    other = total - a
    return total, (a - (total - other)) + (b - other)


def ocean_at(ocean_ref, row, col):
    block_rows, block_cols = ocean_ref.shape
    inside = (row >= 0) & (row < block_rows) & (col >= 0) & (col < block_cols)
    entry = ocean_ref[jnp.clip(row, 0, block_rows - 1), jnp.clip(col, 0, block_cols - 1)]
    return jnp.where(inside & (entry == 1), 1.0, 0.0).astype(F32)


def flux_kernel(
    ids, thick, ocean, u_hbm, v_hbm, depth_hbm, cx_hbm, cy_hbm, cxy_hbm, cxm_hbm, ex_hbm,
    fp_ref, cp_ref, edge_ref, pack_a, pack_b, ax, ay, axy, axm, inv, c0,
    u_buf, v_buf, depth, ex, fu, fv, masks, sems, coef_sem,
):
    levels, row_count, col_count = u_buf.shape
    tiles = col_count // LANES
    chunks = row_count // CHUNK
    groups = row_count // ROWS
    steps = CHUNK // ROWS
    blk, sub = ids[0], ids[1]
    block_rows = row_count // BLOCK
    own = (pl.ds(0, row_count), pl.ds(0, col_count))
    coef_copies = [
        pltpu.make_async_copy(src, dst, coef_sem.at[i])
        for i, (src, dst) in enumerate(
            [
                (depth_hbm, depth), (ex_hbm, ex), (cx_hbm, ax.at[own]), (cy_hbm, ay.at[own]),
                (cxy_hbm, axy.at[own]), (cxm_hbm, axm.at[own]),
            ]
        )
    ]

    def flow_copies(c):
        rows = pl.ds(pl.multiple_of(c * CHUNK, CHUNK), CHUNK)
        return (
            pltpu.make_async_copy(u_hbm.at[:, rows, :], u_buf.at[:, rows, :], sems.at[0, c]),
            pltpu.make_async_copy(v_hbm.at[:, rows, :], v_buf.at[:, rows, :], sems.at[1, c]),
        )

    coef_copies[0].start()
    for copy in flow_copies(0):
        copy.start()
    for copy in coef_copies[1:]:
        copy.start()
    for c in range(1, AHEAD):
        for copy in flow_copies(c):
            copy.start()
    for b in range(block_rows):
        for t in range(tiles):
            masks[pl.ds(b * ROWS, ROWS), pl.ds(t * LANES, LANES)] = jnp.full(
                (ROWS, LANES), ocean_at(ocean, blk * block_rows + b, sub * tiles + t), F32
            )
    coef_copies[0].wait()

    row8 = row_of((ROWS, col_count))
    lane8 = lane_of((ROWS, col_count))
    lane1 = lane_of((ROWS, LANES))
    cols = pl.ds(0, col_count)
    even = (sub % 2) == 0

    def at(g):
        return pl.ds(pl.multiple_of(g * ROWS, ROWS), ROWS)

    def west_of(value):
        return jnp.where(lane8 == 0, 0.0, left(value))

    def east_of(value):
        return jnp.where(lane8 == col_count - 1, 0.0, right(value))

    def rolled_fields(rows):
        return [
            down(v) for v in (ax[rows, cols], west_of(axy[rows, cols]), east_of(axm[rows, cols]), fu[rows])
        ]

    def mask_at(g):
        return pl.ds(pl.multiple_of(g * ROWS // BLOCK * ROWS, ROWS), ROWS)

    def sum_group(g):
        rows = at(g)
        for t in range(tiles):
            lanes = pl.ds(t * LANES, LANES)
            mask = masks[mask_at(g), lanes]
            deep = depth[rows, lanes]
            total_u = jnp.zeros((ROWS, LANES), F32)
            total_v = total_u
            for k in range(levels):
                active = jnp.where(deep > k, thick[k], 0.0)
                total_u = total_u + active * u_buf[k, rows, lanes]
                total_v = total_v + active * v_buf[k, rows, lanes]
            fu[rows, lanes] = mask * total_u
            fv[rows, lanes] = mask * total_v

    def group_work(g, k, before):
        rows = at(g)
        here_x, here_y, here_xy, here_xm = ax[rows, cols], ay[rows, cols], axy[rows, cols], axm[rows, cols]
        here_u, here_v = fu[rows], fv[rows]
        west_xy, east_xm, west_y = west_of(here_xy), east_of(here_xm), west_of(here_y)
        rolled = [down(v) for v in (here_x, west_xy, east_xm, here_u)]
        up_x, up_west, up_east, up_u = [shifted_rows(a, b) for a, b in zip(before, rolled)]
        total = ex[rows] + here_x
        total = total + up_x
        total = total + here_y
        total = total + west_y
        total = total + here_xy
        total = total + up_west
        total = total + here_xm
        total = total + up_east
        cp_ref[rows] = total
        after = fu[at(jnp.minimum(g + 1, groups - 1))]
        after = jnp.where(g + 1 < groups, pltpu.roll(after, ROWS - 1, 0), 0.0)
        below = jnp.where(row8 == ROWS - 1, after, pltpu.roll(here_u, ROWS - 1, 0))
        change = 0.5 * ((below - up_u) + (east_of(here_v) - west_of(here_v)))
        mask = masks[mask_at(g)]
        partial = mask * change
        inverse = mask * (1.0 / total)
        fp_ref[rows] = partial
        inv[rows, cols] = inverse
        c0[rows, cols] = partial * inverse
        fields = [partial, here_x, here_y, here_xy, here_xm, total, here_v, here_u]
        to_west = jnp.zeros((ROWS, LANES), F32)
        to_east = to_west
        for f, field in enumerate(fields):
            lane = 4 * f + 32 * k
            chosen = (lane1 >= lane) & (lane1 < lane + HALO)
            to_west = jnp.where(chosen, pltpu.roll(field[:, :LANES], lane, 1), to_west)
            to_east = jnp.where(chosen, pltpu.roll(field[:, -LANES:], (lane + HALO) % LANES, 1), to_east)
        lane = 4 * 6 + 32 * k
        extra = pltpu.roll(here_xm[:, :LANES], (lane + 1 - HALO) % LANES, 1)
        to_west = jnp.where(lane1 == lane + 1, extra, to_west)
        extra = pltpu.roll(here_xy[:, -LANES:], (lane + HALO + 1) % LANES, 1)
        to_east = jnp.where(lane1 == lane, extra, to_east)
        packed = at(g // 4)
        for_a = jnp.where(even, to_east, to_west)
        for_b = jnp.where(even, to_west, to_east)
        if k == 0:
            pack_a[packed] = for_a
            pack_b[packed] = for_b
        else:
            pack_a[packed] = pack_a[packed] + for_a
            pack_b[packed] = pack_b[packed] + for_b
        return rolled

    def work_from(g, k):
        before = rolled_fields(at(jnp.maximum(g - 1, 0)))
        return group_work(g, k, [jnp.where(g > 0, b, 0.0) for b in before])

    def chunk(c, _):
        for copy in flow_copies(c):
            copy.wait()

        @pl.when(c + AHEAD < chunks)
        def _():
            for copy in flow_copies(c + AHEAD):
                copy.start()

        lax.fori_loop(0, steps, lambda i, _: (sum_group(c * steps + i), 0)[1], 0)

        @pl.when(c == 0)
        def _():
            for copy in coef_copies[1:]:
                copy.wait()

        @pl.when(c > 0)
        def _():
            work_from(c * steps - 1, 3)

        carry = work_from(c * steps, 0)
        for k in range(1, steps - 1):
            carry = group_work(c * steps + k, k, carry)
        return 0

    lax.fori_loop(0, chunks, chunk, 0)
    work_from(groups - 1, 3)
    for side, base in enumerate((0, row_count - ROWS)):
        rows = pl.ds(base, ROWS)
        for f, field in enumerate(
            [fp_ref[rows], ax[rows, cols], ay[rows, cols], axy[rows, cols], axm[rows, cols], cp_ref[rows], fu[rows]]
        ):
            edge_ref[pl.ds((side * 7 + f) * ROWS, ROWS)] = field


def side_tiles(send_a, send_b, recv_a, recv_b, even, packed):
    own_a, own_b, got_a, got_b = send_a[packed], send_b[packed], recv_a[packed], recv_b[packed]
    pick = lambda a, b: jnp.where(even, a, b)
    return pick(own_b, own_a), pick(own_a, own_b), pick(got_b, got_a), pick(got_a, got_b)


def outer_tile(from_west, from_east, f, k):
    lane1 = lane_of(from_west.shape)
    at = 4 * f + 32 * k
    east = pltpu.roll(from_east, (-at) % LANES, 1)
    west = pltpu.roll(from_west, (LANES - HALO - at) % LANES, 1)
    tile = jnp.where(lane1 < HALO, east, jnp.where(lane1 >= LANES - HALO, west, 0.0))
    if f == 3:
        extra = pltpu.roll(from_west, (LANES - HALO - 1 - 4 * 6 - 32 * k) % LANES, 1)
        tile = jnp.where(lane1 == LANES - HALO - 1, extra, tile)
    if f == 4:
        extra = pltpu.roll(from_east, (HALO - 4 * 6 - 1 - 32 * k) % LANES, 1)
        tile = jnp.where(lane1 == HALO, extra, tile)
    return tile


def force_with_sides(partial, mask, sides, k):
    own_west, own_east, from_west, from_east = sides
    lane1 = lane_of(own_west.shape)
    first, last = 4 * 6 + 32 * k, 4 * 6 + 3 + 32 * k
    outer = outer_tile(from_west, from_east, 0, k)
    tail = pltpu.roll(own_east, (-last) % LANES, 1)
    head = pltpu.roll(own_west, (LANES - 1 - first) % LANES, 1)
    change = jnp.where(lane1 == 0, -tail, jnp.where(lane1 == LANES - 1, head, 0.0))
    outer = outer + 0.5 * mask[:, -LANES:] * change
    begin = partial[:, :LANES] - jnp.where(
        lane1 == 0, 0.5 * mask[:, :LANES] * pltpu.roll(from_west, (-last) % LANES, 1), 0.0
    )
    middle = partial[:, LANES:-LANES]
    end = partial[:, -LANES:] + jnp.where(
        lane1 == LANES - 1,
        0.5 * mask[:, -2 * LANES : -LANES] * pltpu.roll(from_east, (LANES - 1 - first) % LANES, 1),
        0.0,
    )
    return jnp.concatenate([begin, middle, end, outer], axis=1)


def mask_row(ocean, block_row, sub, tiles):
    lane1 = lane_of((1, LANES))
    parts = [jnp.full((1, LANES), ocean_at(ocean, block_row, sub * tiles + t), F32) for t in range(tiles)]
    east = ocean_at(ocean, block_row, (sub + 1) * tiles)
    west = ocean_at(ocean, block_row, sub * tiles - 1)
    parts.append(jnp.where(lane1 < LANES // 2, east, west))
    return jnp.concatenate(parts, axis=1)


def edge_kernel(ids, ocean, edges, send_a, send_b, recv_a, recv_b, rows_a, rows_b, *, row_count):
    col_count = edges.shape[1]
    tiles = col_count // LANES
    block_rows = row_count // BLOCK
    blk, sub = ids[0], ids[1]
    even_sub, even_blk = (sub % 2) == 0, (blk % 2) == 0
    shape = (ROWS, col_count + LANES)
    row8, lane8 = row_of(shape), lane_of(shape)
    crosses_west = (lane8 == 0) | (lane8 == col_count)
    crosses_east = (lane8 == col_count - 1) | (lane8 == col_count + LANES - 1)
    strips = row_count // (4 * ROWS)
    results = []
    for side, top in enumerate((True, False)):
        k = 0 if top else 3
        packed = pl.ds(0 if top else (strips - 1) * ROWS, ROWS)
        rows = [edges[pl.ds((side * 7 + f) * ROWS, ROWS)] for f in range(7)]
        sides = side_tiles(send_a, send_b, recv_a, recv_b, even_sub, packed)
        block_row = blk * block_rows + (0 if top else block_rows - 1)
        mask = jnp.broadcast_to(mask_row(ocean, block_row, sub, tiles), shape)
        fields = [force_with_sides(rows[0], mask, sides, k)]
        for f in range(1, 6):
            fields.append(jnp.concatenate([rows[f], outer_tile(sides[2], sides[3], f, k)], axis=1))
        flux = jnp.concatenate([rows[6], outer_tile(sides[2], sides[3], 7, k)], axis=1)
        if top:
            fields[1] = jnp.where(row8 == 3, pltpu.roll(flux, 3, 0), fields[1])
            half = lambda v: v
        else:
            extra = jnp.where(crosses_west, left(fields[2]) + left(down(fields[3])), 0.0)
            extra = extra + jnp.where(crosses_east, right(down(fields[4])), 0.0)
            fields[5] = fields[5] + jnp.where(row8 == 4, extra, 0.0)
            fields[2] = jnp.where(row8 == 4, pltpu.roll(flux, 5, 0), fields[2])
            half = lambda v: pltpu.roll(v, 4, 0)
        pieces = []
        for pair in range(3):
            one, two = half(fields[2 * pair]), half(fields[2 * pair + 1])
            pieces.append(jnp.where(row8 < 4, one, pltpu.roll(two, 4, 0)))
        results.append(pieces)
    for pair in range(3):
        rows = slice(pair * ROWS, (pair + 1) * ROWS)
        rows_a[rows] = jnp.where(even_blk, results[1][pair], results[0][pair])
        rows_b[rows] = jnp.where(even_blk, results[0][pair], results[1][pair])


def prepare_kernel(ax, ay, axy, axm, bly, nx, nxy, nxm, lxy, rxm):
    row_count, wide = ax.shape[0] - ROWS, ax.shape[1]
    cols = pl.ds(0, wide - LANES)
    lane8 = lane_of((ROWS, wide - LANES))
    end = lane8 == wide - LANES - 1

    def body(g, before):
        rows = pl.ds(pl.multiple_of(g * ROWS, ROWS), ROWS)
        here_xy, here_xm = axy[rows, cols], axm[rows, cols]
        bly[rows, cols] = jnp.where(lane8 == 0, 0.0, left(ay[rows, cols]))
        lxy[rows, cols] = jnp.where(lane8 == 0, 0.0, left(here_xy))
        rxm[rows, cols] = jnp.where(end, 0.0, right(here_xm))
        rolled = tuple(down(v) for v in (ax[rows, cols], here_xy, here_xm))
        for ring, a, b in zip((nx, nxy, nxm), before, rolled):
            ring[rows, cols] = shifted_rows(a, b)
        return rolled

    zero = jnp.zeros(lane8.shape, F32)
    lax.fori_loop(0, row_count // ROWS, body, (zero, zero, zero), unroll=4)


def widen_kernel(
    ids, ocean, fp, send_a, send_b, recv_a, recv_b,
    ax_in, ay_in, bly_in, nx_in, nxy_in, nxm_in, lxy_in, rxm_in, inv_in, c0_in, center_in,
    outer_center, ax, ay, bly, nx, nxy, nxm, lxy, rxm, inv, c0, center,
):
    row_count, col_count = fp.shape
    tiles = col_count // LANES
    block_rows = row_count // BLOCK
    groups = row_count // ROWS
    blk, sub = ids[0], ids[1]
    even_sub = (sub % 2) == 0
    lane1 = lane_of((ROWS, LANES))
    first, last, outer = pl.ds(0, LANES), pl.ds(col_count - LANES, LANES), pl.ds(col_count, LANES)
    west_edge, east_edge = lane1 == 0, lane1 == LANES - 1

    def at(g):
        return pl.ds(pl.multiple_of(g * ROWS, ROWS), ROWS)

    def widen(p, before):
        sides = side_tiles(send_a, send_b, recv_a, recv_b, even_sub, at(p))
        own_west, own_east, from_west, from_east = sides
        for k in range(4):
            g = 4 * p + k
            rows = at(g)
            new_f, new_x, new_y, new_xy, new_xm, new_c = [outer_tile(from_west, from_east, f, k) for f in range(6)]
            end_y = pltpu.roll(own_east, (-(4 * 2 + 3 + 32 * k)) % LANES, 1)
            end_xy = pltpu.roll(own_east, (-(4 * 3 + 3 + 32 * k)) % LANES, 1)
            begin_xm = pltpu.roll(own_west, (LANES - 1 - 4 * 4 - 32 * k) % LANES, 1)
            left_y, left_xy, right_xm = left(new_y), left(new_xy), right(new_xm)
            outer_y = jnp.where(west_edge, end_y, left_y)
            outer_xy = jnp.where(west_edge, end_xy, left_xy)
            outer_xm = jnp.where(east_edge, begin_xm, right_xm)
            rolled = [down(v) for v in (new_x, new_xy, new_xm, outer_xy, outer_xm, left_xy, right_xm)]
            up_x, up_xy, up_xm, up_outer_xy, up_outer_xm, up_left, up_right = [
                shifted_rows(a, b) for a, b in zip(before, rolled)
            ]
            before = rolled
            ax[rows, outer] = new_x
            ay[rows, outer] = new_y
            bly[rows, outer] = outer_y
            lxy[rows, outer] = outer_xy
            rxm[rows, outer] = outer_xm
            nx[rows, outer] = up_x
            nxy[rows, outer] = up_xy
            nxm[rows, outer] = up_xm
            bly[rows, first] = jnp.where(west_edge, left_y, bly[rows, first])
            lxy[rows, first] = jnp.where(west_edge, left_xy, lxy[rows, first])
            rxm[rows, last] = jnp.where(east_edge, right_xm, rxm[rows, last])
            center_first = center[rows, first] + jnp.where(west_edge, left_y + up_left, 0.0)
            center_last = center[rows, last] + jnp.where(east_edge, up_right, 0.0)
            center_outer = new_c + jnp.where(west_edge, outer_y + up_outer_xy, 0.0)
            center_outer = center_outer + jnp.where(east_edge, up_outer_xm, 0.0)
            center[rows, first] = center_first
            center[rows, last] = center_last
            outer_center[rows] = center_outer
            block_row = blk * block_rows + g * ROWS // BLOCK
            mask_first = ocean_at(ocean, block_row, sub * tiles)
            mask_last = ocean_at(ocean, block_row, (sub + 1) * tiles - 1)
            mask_outer = jnp.where(
                lane1 < LANES // 2,
                ocean_at(ocean, block_row, (sub + 1) * tiles),
                ocean_at(ocean, block_row, sub * tiles - 1),
            )
            near, far = 4 * 6 + 32 * k, 4 * 6 + 3 + 32 * k
            tail = pltpu.roll(own_east, (-far) % LANES, 1)
            begin = pltpu.roll(own_west, (LANES - 1 - near) % LANES, 1)
            from_w = pltpu.roll(from_west, (-far) % LANES, 1)
            from_e = pltpu.roll(from_east, (LANES - 1 - near) % LANES, 1)
            force_first = fp[rows, first] - jnp.where(west_edge, (0.5 * mask_first) * from_w, 0.0)
            force_last = fp[rows, last] + jnp.where(east_edge, (0.5 * mask_last) * from_e, 0.0)
            change = jnp.where(west_edge, -tail, jnp.where(east_edge, begin, 0.0))
            force_outer = new_f + 0.5 * mask_outer * change
            inverse_first = mask_first * (1.0 / center_first)
            inverse_last = mask_last * (1.0 / center_last)
            inverse_outer = jnp.where(mask_outer > 0.0, 1.0 / jnp.where(center_outer > 0.0, center_outer, 1.0), 0.0)
            inv[rows, first] = inverse_first
            inv[rows, last] = inverse_last
            inv[rows, outer] = inverse_outer
            c0[rows, first] = force_first * inverse_first
            c0[rows, last] = force_last * inverse_last
            c0[rows, outer] = force_outer * inverse_outer
        return tuple(before)

    zero = jnp.zeros((ROWS, LANES), F32)
    lax.fori_loop(0, groups // 4, widen, (zero,) * 7)


def basis_kernel(
    ids, ocean, outer_center, edges, send_a, send_b, recv_a, recv_b, rows_a, rows_b,
    ax_in, ay_in, bly_in, nx_in, nxy_in, nxm_in, lxy_in, rxm_in, inv_in, c0_in, center_in,
    c1, c2, c3, c4, gram_ref, ax, ay, bly, nx, nxy, nxm, lxy, rxm, inv, c0, center,
):
    row_count, col_count = center.shape
    tiles = col_count // LANES
    wide = col_count + LANES
    block_rows = row_count // BLOCK
    groups = row_count // ROWS
    blk, sub = ids[0], ids[1]
    even_sub, even_blk = (sub % 2) == 0, (blk % 2) == 0
    row8, lane8 = row_of((ROWS, wide)), lane_of((ROWS, wide))
    row1, lane1 = row_of((ROWS, LANES)), lane_of((ROWS, LANES))
    first, last, outer = pl.ds(0, LANES), pl.ds(col_count - LANES, LANES), pl.ds(col_count, LANES)
    west_edge, east_edge = lane1 == 0, lane1 == LANES - 1

    def at(g):
        return pl.ds(pl.multiple_of(g * ROWS, ROWS), ROWS)

    pieces = []
    for pair in range(3):
        rows = slice(pair * ROWS, (pair + 1) * ROWS)
        below = jnp.where(even_blk, rows_a[rows], rows_b[rows])
        above = jnp.where(even_blk, rows_b[rows], rows_a[rows])
        pieces.append(jnp.where(row8 < 4, below, pltpu.roll(above, 4, 0)))
        pieces.append(jnp.where(row8 < 4, pltpu.roll(below, 4, 0), above))
    out_f, out_x, out_y, out_xy, out_xm, out_c = pieces
    flux_below, flux_above = out_x[3:4], out_y[4:5]

    def mask_of(block_row):
        return jnp.broadcast_to(mask_row(ocean, block_row, sub, tiles), (ROWS, wide))

    def edge_group(side, k):
        strip = 0 if side == 0 else groups // 4 - 1
        sides = side_tiles(send_a, send_b, recv_a, recv_b, even_sub, at(strip))
        get = lambda f: edges[pl.ds((side * 7 + f) * ROWS, ROWS)]
        full = [
            jnp.concatenate([get(e), outer_tile(sides[2], sides[3], f, k)], axis=1)
            for e, f in ((1, 1), (3, 3), (4, 4), (6, 7))
        ]
        mask = mask_of(blk * block_rows + (0 if side == 0 else block_rows - 1))
        return full, mask, force_with_sides(get(0), mask, sides, k)

    (_, _, _, flux_first), mask_first, force_first = edge_group(0, 0)
    (x_last, xy_last, xm_last, flux_last), mask_last, force_last = edge_group(1, 3)
    mask_below, mask_above = mask_of((blk + 1) * block_rows), mask_of(blk * block_rows - 1)

    def inverse_of(mask, total):
        return jnp.where(mask > 0.0, 1.0 / jnp.where(total > 0.0, total, 1.0), 0.0)

    head = row8 == 0
    own_first = pl.ds(0, ROWS)
    up = []
    for ring, out in ((nx, out_x), (nxy, out_xy), (nxm, out_xm)):
        moved = jnp.where(head, down(out), ring[own_first])
        ring[own_first] = moved
        up.append(moved)
    total = jnp.concatenate([center[own_first], outer_center[own_first]], axis=1)
    total = total + jnp.where(head, up[0] + left(up[1]) + right(up[2]), 0.0)
    center[own_first] = total[:, :col_count]
    inverse = inverse_of(mask_first, total)
    inv[own_first] = inverse
    c0[own_first] = inverse * (force_first - jnp.where(head, 0.5 * mask_first * flux_above, 0.0))
    own_last = pl.ds(row_count - ROWS, ROWS)
    c0[own_last] = inv[own_last] * (
        force_last + jnp.where(row8 == ROWS - 1, 0.5 * mask_last * flux_below, 0.0)
    )
    ring_rows = pl.ds(row_count, ROWS)
    up = [
        jnp.where(head, down(before), down(out))
        for before, out in ((x_last, out_x), (xy_last, out_xy), (xm_last, out_xm))
    ]
    left_y = left(out_y)
    for ring, value in (
        (ax, out_x), (ay, out_y), (bly, left_y), (nx, up[0]), (nxy, up[1]), (nxm, up[2]),
        (lxy, left(out_xy)), (rxm, right(out_xm)),
    ):
        ring[ring_rows] = value
    crosses_west = (row8 != 4) & ((lane8 == 0) | (lane8 == col_count))
    crosses_east = (row8 != 4) & ((lane8 == col_count - 1) | (lane8 == wide - 1))
    total = out_c + jnp.where(head, up[0], 0.0)
    total = total + jnp.where(crosses_west, left_y, 0.0)
    total = total + jnp.where(head | crosses_west, left(up[1]), 0.0)
    total = total + jnp.where(head | crosses_east, right(up[2]), 0.0)
    inverse = inverse_of(jnp.where(row8 < 4, mask_below, mask_above), total)
    out_f = out_f - jnp.where(head, 0.5 * mask_below * flux_last[ROWS - 1 : ROWS], 0.0)
    out_f = out_f + jnp.where(row8 == ROWS - 1, 0.5 * mask_above * flux_first[0:1], 0.0)
    inv[ring_rows] = inverse
    c0[ring_rows] = inverse * out_f

    def sides_of(source, g, width):
        value = source[at(g)]
        return left(value)[:, :width], right(value)[:, :width]

    def terms(source, g, width, turned):
        rows, cols = at(g), pl.ds(0, width)
        west, east = turned
        here = source[rows, cols]
        same = ay[rows, cols] * east + bly[rows, cols] * west
        after = ax[rows, cols] * here + lxy[rows, cols] * west + rxm[rows, cols] * east
        before = nx[rows, cols] * here + nxy[rows, cols] * east + nxm[rows, cols] * west
        return same, down(after), pltpu.roll(before, ROWS - 1, 0)

    def sweep(source, count, width, finish):
        ring_turned, turned, following = [sides_of(source, g, width) for g in (groups, 0, 1)]
        _, ring_after, _ = terms(source, groups, width, ring_turned)
        same, after, own_first = terms(source, 0, width, turned)
        tail = row_of((ROWS, width)) == ROWS - 1

        def body(g, carry):
            partial, own, previous, turned = carry
            following = sides_of(source, jnp.minimum(g + 1, groups), width)
            same, after, later = terms(source, g, width, turned)
            finish(g - 1, partial + jnp.where(tail, later, own))
            return same + shifted_rows(previous, after), later, after, following

        carry = (same + shifted_rows(ring_after, after), own_first, after, following)
        partial, own, _, turned = lax.fori_loop(1, count, body, carry, unroll=UNROLL)
        if count > groups:
            later = own_first
        else:
            later = terms(source, groups, width, turned)[2]
        finish(count - 1, partial + jnp.where(tail, later, own))

    def step(source, target, subtract):
        def finish(g, total):
            rows = at(g)
            moved = inv[rows] * total
            target[rows] = source[rows] - moved if subtract else moved

        sweep(source, groups + 1, wide, finish)

    step(c0, c1, True)
    step(c1, c2, False)
    step(c2, c3, False)

    cols = pl.ds(0, col_count)

    def last_finish(g, total):
        c4[at(g)] = inv[at(g), cols] * total

    sweep(c3, groups, col_count, last_finish)

    def add_products(g, sums):
        rows = at(g)
        basis = [ref[rows, cols] for ref in (c0, c1, c2, c3)] + [c4[rows]]
        weight = center[rows]
        weighted = [weight * b for b in basis]
        new = []
        for (i, j), total in zip(PAIRS, sums):
            product = basis[i] * weighted[j]
            part = product[:, :LANES]
            for t in range(1, tiles):
                part = part + product[:, t * LANES : (t + 1) * LANES]
            new.append(total + part)
        return tuple(new)

    zero = jnp.zeros((ROWS, LANES), F32)
    sums = lax.fori_loop(0, groups, add_products, tuple(zero for _ in PAIRS), unroll=2)

    count = len(PAIRS)
    high = jnp.zeros((2 * ROWS, LANES), F32)
    low = high
    place = row_of((2 * ROWS, LANES))
    for index, total in enumerate(sums):
        error = jnp.zeros_like(total)
        for shift in (4, 2, 1):
            total, rounding = two_sum(total, pltpu.roll(total, shift, 0))
            error = error + pltpu.roll(error, shift, 0) + rounding
        high = jnp.where(place == index, total[0:1], high)
        low = jnp.where(place == index, error[0:1], low)
    for shift in (64, 32, 16, 8, 4, 2, 1):
        high, rounding = two_sum(high, pltpu.roll(high, shift, 1))
        low = low + pltpu.roll(low, shift, 1) + rounding
    lane2 = lane_of((2 * ROWS, LANES))
    packed = jnp.where(lane2 == place, high, jnp.where(lane2 == place + LANES // 2, low, 0.0))
    gram_ref[...] = jnp.broadcast_to(jnp.sum(packed, axis=0, keepdims=True), gram_ref.shape)


def finish_kernel(gram_ref, c0, c1, c2, c3, c4, center_ref, height_ref, residual_ref):
    lane1 = lane_of((1, LANES))
    high = gram_ref[...]
    low = jnp.zeros_like(high)
    while high.shape[0] > 1:
        half = high.shape[0] // 2
        high, rounding = two_sum(high[:half], high[half:])
        low = low[:half] + low[half:] + rounding
    entries = high + (low + pltpu.roll(high, LANES // 2, 1))
    size = ITERS + 1
    gram = {}
    for index, (i, j) in enumerate(PAIRS):
        entry = jnp.sum(jnp.where(lane1 == index, entries, 0.0), axis=1, keepdims=True)
        gram[i, j] = entry
        gram[j, i] = entry
    zero = jnp.zeros((1, 1), F32)
    one = jnp.ones((1, 1), F32)

    def image(coefs):
        result = [zero, coefs[0] + coefs[1]]
        for j in range(2, size):
            own = coefs[j] if j < size - 1 else zero
            result.append(own - coefs[j - 1])
        return result

    def form(one_side, products):
        total = zero
        for a, b in zip(one_side, products):
            total = total + a * b
        return total

    scaled = [one] + [zero] * (size - 1)
    search = [zero] * size
    height = [zero] * size
    rho_old, sigma = one, zero
    for iteration in range(ITERS):
        limit = iteration + 1
        products = []
        for j in range(size):
            total = zero
            for i in range(limit):
                total = total + scaled[i] * gram[i, j]
            products.append(total)
        rho = form(scaled[:limit], products)
        curvature = form(image(scaled)[: limit + 1], products)
        beta = rho / rho_old
        sigma = curvature - beta * beta * sigma
        alpha = rho / sigma
        rho_old = rho
        search = [s + beta * q for s, q in zip(scaled, search)]
        height = [h + alpha * q for h, q in zip(height, search)]
        scaled = [s - alpha * q for s, q in zip(scaled, image(search))]

    def combine(g, _):
        rows = pl.ds(pl.multiple_of(g * ROWS, ROWS), ROWS)
        cols = pl.ds(0, center_ref.shape[1])
        basis = [ref[rows, cols] for ref in (c0, c1, c2, c3, c4)]
        total = height[0] * basis[0]
        for j in range(1, size - 1):
            total = total + height[j] * basis[j]
        height_ref[rows] = total
        total = scaled[0] * basis[0]
        for j in range(1, size):
            total = total + scaled[j] * basis[j]
        residual_ref[rows] = center_ref[rows] * total
        return 0

    lax.fori_loop(0, center_ref.shape[0] // ROWS, combine, 0, unroll=2)


def swap(value, axis, parity):
    peers = lax.axis_size(axis)
    pairs = []
    for i in range(parity, peers - 1, 2):
        pairs += [(i, i + 1), (i + 1, i)]
    return lax.ppermute(value, axis, pairs)


def body(u_flow, v_flow, thickness, depth_levels, block_ocean, coef_x, coef_y, coef_xy, coef_xm, extra_diagonal):
    levels, row_count, col_count = u_flow.shape
    wide = col_count + LANES
    shape = lambda *dims: pltpu.VMEM(dims, F32)
    final = jax.ShapeDtypeStruct((row_count, col_count), F32)
    far = lambda array: pltpu.with_memory_space_constraint(array, pltpu.HBM)
    plane = shape(row_count, col_count)
    ring = shape(row_count + ROWS, wide)
    strip = shape(row_count // 4, LANES)
    ids = jnp.stack([lax.axis_index("blk"), lax.axis_index("sub")]).astype(jnp.int32)
    flow = pltpu.VMEM((levels, row_count, col_count), F32)
    field = pltpu.VMEM((row_count, col_count), F32)
    fp, cp, edges, send_a, send_b, *rings = pl.pallas_call(
        flux_kernel,
        out_shape=(plane, plane, shape(14 * ROWS, col_count), strip, strip) + (ring,) * 6,
        in_specs=[SMEM, SMEM, SMEM] + [HBM] * 8,
        out_specs=(VMEM,) * 11,
        scratch_shapes=[flow, flow, pltpu.VMEM((row_count, col_count), jnp.int32)]
        + [field] * 3
        + [pltpu.VMEM((row_count // BLOCK * ROWS, col_count), F32)]
        + [pltpu.SemaphoreType.DMA((2, row_count // CHUNK)), pltpu.SemaphoreType.DMA((6,))],
        compiler_params=pltpu.CompilerParams(vmem_limit_bytes=FLUX_LIMIT),
        name="flux",
    )(
        ids, thickness, block_ocean,
        *[far(a) for a in (u_flow, v_flow, depth_levels, coef_x, coef_y, coef_xy, coef_xm, extra_diagonal)],
    )
    recv_a, recv_b = swap(send_a, "sub", 0), swap(send_b, "sub", 1)
    ax, ay, axy, axm, inv, c0 = rings
    moved = pl.pallas_call(
        prepare_kernel,
        out_shape=(ring,) * 6,
        in_specs=[VMEM] * 4,
        out_specs=(VMEM,) * 6,
        compiler_params=pltpu.CompilerParams(vmem_limit_bytes=8 << 20),
        cost_estimate=pl.CostEstimate(flops=10 << 20, bytes_accessed=4 << 20, transcendentals=0),
        name="prepare",
    )(ax, ay, axy, axm)
    edge = shape(3 * ROWS, wide)
    edge_a, edge_b = pl.pallas_call(
        functools.partial(edge_kernel, row_count=row_count),
        out_shape=(edge, edge),
        in_specs=[SMEM, SMEM] + [VMEM] * 5,
        out_specs=(VMEM,) * 2,
        compiler_params=pltpu.CompilerParams(vmem_limit_bytes=8 << 20),
        name="edge",
    )(ids, block_ocean, edges, send_a, send_b, recv_a, recv_b)
    rows_a, rows_b = swap(edge_a, "blk", 0), swap(edge_b, "blk", 1)
    outer_center, *rings = pl.pallas_call(
        widen_kernel,
        out_shape=(shape(row_count, LANES),) + (ring,) * 10 + (plane,),
        in_specs=[SMEM, SMEM] + [VMEM] * 16,
        out_specs=(VMEM,) * 12,
        input_output_aliases={7 + i: 1 + i for i in range(11)},
        compiler_params=pltpu.CompilerParams(vmem_limit_bytes=8 << 20),
        cost_estimate=pl.CostEstimate(flops=10 << 20, bytes_accessed=4 << 20, transcendentals=0),
        name="widen",
    )(ids, block_ocean, fp, send_a, send_b, recv_a, recv_b, ax, ay, *moved, inv, c0, cp)
    devices = lax.axis_size("blk") * lax.axis_size("sub")
    c1, c2, c3, c4, gram, *rest = pl.pallas_call(
        basis_kernel,
        out_shape=(ring, ring, ring, plane, shape(devices, LANES)) + (ring,) * 10 + (plane,),
        in_specs=[SMEM, SMEM] + [VMEM] * 19,
        out_specs=(VMEM,) * 16,
        input_output_aliases={10 + i: 5 + i for i in range(11)},
        compiler_params=pltpu.CompilerParams(vmem_limit_bytes=8 << 20),
        name="basis",
    )(ids, block_ocean, outer_center, edges, send_a, send_b, recv_a, recv_b, rows_a, rows_b, *rings)
    c0, center = rest[-2], rest[-1]
    gram = lax.all_to_all(gram, ("blk", "sub"), 0, 0, tiled=True)
    return pl.pallas_call(
        finish_kernel,
        out_shape=(final, final),
        in_specs=[VMEM] * 7,
        out_specs=(VMEM,) * 2,
        compiler_params=pltpu.CompilerParams(vmem_limit_bytes=8 << 20),
        name="finish",
    )(gram, c0, c1, c2, c3, c4, center)


def solution(mesh):
    placed = (
        P(None, "blk", "sub"),
        P(None, "blk", "sub"),
        P(),
        P("blk", "sub"),
        P(),
        P("blk", "sub"),
        P("blk", "sub"),
        P("blk", "sub"),
        P("blk", "sub"),
        P("blk", "sub"),
    )
    return jax.shard_map(
        body,
        mesh=mesh,
        in_specs=placed,
        out_specs=(P("blk", "sub"), P("blk", "sub")),
        check_vma=False,
    )
```

```python
import functools

import jax
import jax.numpy as jnp
from jax import lax
from jax.experimental import pallas as pl
from jax.experimental.pallas import tpu as pltpu
from jax.sharding import PartitionSpec as P

BLOCK = 128
ITERS = 4
HALO = ITERS
LANES = 128
ROWS = 8
CHUNK = 32
AHEAD = 3
UNROLL = 8
F32 = jnp.float32
FLUX_LIMIT = 40 << 20
VMEM = pl.BlockSpec(memory_space=pltpu.VMEM)
HBM = pl.BlockSpec(memory_space=pltpu.HBM)
PAIRS = [(i, j) for i in range(ITERS) for j in range(i, ITERS + 1)]


def lane_of(shape):
    return lax.broadcasted_iota(jnp.int32, shape, len(shape) - 1)


def row_of(shape):
    return lax.broadcasted_iota(jnp.int32, shape, len(shape) - 2)


def shifted_rows(before, here):
    return jnp.where(row_of(here.shape) == 0, before, here)


def left(value):
    return pltpu.roll(value, 1, 1)


def right(value):
    return pltpu.roll(value, value.shape[1] - 1, 1)


def down(value):
    return pltpu.roll(value, 1, 0)


def two_sum(a, b):
    total = a + b
    other = total - a
    return total, (a - (total - other)) + (b - other)


def ocean_at(ocean_ref, row, col):
    block_rows, block_cols = ocean_ref.shape
    inside = (row >= 0) & (row < block_rows) & (col >= 0) & (col < block_cols)
    entry = ocean_ref[jnp.clip(row, 0, block_rows - 1), jnp.clip(col, 0, block_cols - 1)]
    return jnp.where(inside & (entry == 1), 1.0, 0.0).astype(F32)


def flux_kernel(
    thick_hbm, ocean_hbm, u_hbm, v_hbm, depth_hbm, cx_hbm, cy_hbm, cxy_hbm, cxm_hbm, ex_hbm,
    fp_ref, cp_ref, edge_ref, pack_a, pack_b, ax, ay, axy, axm, inv, c0, masks,
    u_buf, v_buf, depth, ex, fu, fv, thick, ocean, sems, coef_sem, small_sem,
):
    levels, row_count, col_count = u_buf.shape
    tiles = col_count // LANES
    chunks = row_count // CHUNK
    groups = row_count // ROWS
    steps = CHUNK // ROWS
    blk, sub = own_place()
    block_rows = row_count // BLOCK
    own = (pl.ds(0, row_count), pl.ds(0, col_count))
    coef_copies = [
        pltpu.make_async_copy(src, dst, coef_sem.at[i])
        for i, (src, dst) in enumerate(
            [
                (depth_hbm, depth), (ex_hbm, ex), (cx_hbm, ax.at[own]), (cy_hbm, ay.at[own]),
                (cxy_hbm, axy.at[own]), (cxm_hbm, axm.at[own]),
            ]
        )
    ]

    def flow_copies(c):
        rows = pl.ds(pl.multiple_of(c * CHUNK, CHUNK), CHUNK)
        return (
            pltpu.make_async_copy(u_hbm.at[:, rows, :], u_buf.at[:, rows, :], sems.at[0, c]),
            pltpu.make_async_copy(v_hbm.at[:, rows, :], v_buf.at[:, rows, :], sems.at[1, c]),
        )

    small_copies = [
        pltpu.make_async_copy(src, dst, small_sem.at[i])
        for i, (src, dst) in enumerate([(thick_hbm, thick), (ocean_hbm, ocean)])
    ]
    for copy in small_copies:
        copy.start()
    coef_copies[0].start()
    for copy in flow_copies(0):
        copy.start()
    for copy in coef_copies[1:]:
        copy.start()
    for c in range(1, AHEAD):
        for copy in flow_copies(c):
            copy.start()
    for copy in small_copies:
        copy.wait()
    for place in range(block_rows + 2):
        block_row = blk * block_rows + (place if place <= block_rows else -1)
        masks[mask_group(place)] = jnp.broadcast_to(
            mask_row(ocean, block_row, sub, tiles), (ROWS, col_count + LANES)
        )
    coef_copies[0].wait()

    row8 = row_of((ROWS, col_count))
    lane8 = lane_of((ROWS, col_count))
    lane1 = lane_of((ROWS, LANES))
    cols = pl.ds(0, col_count)
    even = (sub % 2) == 0

    def at(g):
        return pl.ds(pl.multiple_of(g * ROWS, ROWS), ROWS)

    def west_of(value):
        return jnp.where(lane8 == 0, 0.0, left(value))

    def east_of(value):
        return jnp.where(lane8 == col_count - 1, 0.0, right(value))

    def rolled_fields(rows):
        return [
            down(v) for v in (ax[rows, cols], west_of(axy[rows, cols]), east_of(axm[rows, cols]), fu[rows])
        ]

    def sum_group(g):
        rows = at(g)
        for t in range(tiles):
            lanes = pl.ds(t * LANES, LANES)
            mask = masks[mask_group(g * ROWS // BLOCK), lanes]
            deep = depth[rows, lanes]
            total_u = jnp.zeros((ROWS, LANES), F32)
            total_v = total_u
            for k in range(levels):
                active = jnp.where(deep > k, thick[k], 0.0)
                total_u = total_u + active * u_buf[k, rows, lanes]
                total_v = total_v + active * v_buf[k, rows, lanes]
            fu[rows, lanes] = mask * total_u
            fv[rows, lanes] = mask * total_v

    def group_work(g, k, before):
        rows = at(g)
        here_x, here_y, here_xy, here_xm = ax[rows, cols], ay[rows, cols], axy[rows, cols], axm[rows, cols]
        here_u, here_v = fu[rows], fv[rows]
        west_xy, east_xm, west_y = west_of(here_xy), east_of(here_xm), west_of(here_y)
        rolled = [down(v) for v in (here_x, west_xy, east_xm, here_u)]
        up_x, up_west, up_east, up_u = [shifted_rows(a, b) for a, b in zip(before, rolled)]
        total = ex[rows] + here_x
        total = total + up_x
        total = total + here_y
        total = total + west_y
        total = total + here_xy
        total = total + up_west
        total = total + here_xm
        total = total + up_east
        cp_ref[rows] = total
        after = fu[at(jnp.minimum(g + 1, groups - 1))]
        after = jnp.where(g + 1 < groups, pltpu.roll(after, ROWS - 1, 0), 0.0)
        below = jnp.where(row8 == ROWS - 1, after, pltpu.roll(here_u, ROWS - 1, 0))
        change = 0.5 * ((below - up_u) + (east_of(here_v) - west_of(here_v)))
        mask = masks[mask_group(g * ROWS // BLOCK), cols]
        partial = mask * change
        inverse = mask * (1.0 / total)
        fp_ref[rows] = partial
        inv[rows, cols] = inverse
        c0[rows, cols] = partial * inverse
        fields = [partial, here_x, here_y, here_xy, here_xm, total, here_v, here_u]
        to_west = jnp.zeros((ROWS, LANES), F32)
        to_east = to_west
        for f, field in enumerate(fields):
            lane = 4 * f + 32 * k
            chosen = (lane1 >= lane) & (lane1 < lane + HALO)
            to_west = jnp.where(chosen, pltpu.roll(field[:, :LANES], lane, 1), to_west)
            to_east = jnp.where(chosen, pltpu.roll(field[:, -LANES:], (lane + HALO) % LANES, 1), to_east)
        lane = 4 * 6 + 32 * k
        extra = pltpu.roll(here_xm[:, :LANES], (lane + 1 - HALO) % LANES, 1)
        to_west = jnp.where(lane1 == lane + 1, extra, to_west)
        extra = pltpu.roll(here_xy[:, -LANES:], (lane + HALO + 1) % LANES, 1)
        to_east = jnp.where(lane1 == lane, extra, to_east)
        packed = at(g // 4)
        for_a = jnp.where(even, to_east, to_west)
        for_b = jnp.where(even, to_west, to_east)
        if k == 0:
            pack_a[packed] = for_a
            pack_b[packed] = for_b
        else:
            pack_a[packed] = pack_a[packed] + for_a
            pack_b[packed] = pack_b[packed] + for_b
        return rolled

    def work_from(g, k):
        before = rolled_fields(at(jnp.maximum(g - 1, 0)))
        return group_work(g, k, [jnp.where(g > 0, b, 0.0) for b in before])

    def chunk(c, _):
        for copy in flow_copies(c):
            copy.wait()

        @pl.when(c + AHEAD < chunks)
        def _():
            for copy in flow_copies(c + AHEAD):
                copy.start()

        lax.fori_loop(0, steps, lambda i, _: (sum_group(c * steps + i), 0)[1], 0)

        @pl.when(c == 0)
        def _():
            for copy in coef_copies[1:]:
                copy.wait()

        @pl.when(c > 0)
        def _():
            work_from(c * steps - 1, 3)

        carry = work_from(c * steps, 0)
        for k in range(1, steps - 1):
            carry = group_work(c * steps + k, k, carry)
        return 0

    lax.fori_loop(0, chunks, chunk, 0)
    work_from(groups - 1, 3)
    for side, base in enumerate((0, row_count - ROWS)):
        rows = pl.ds(base, ROWS)
        for f, field in enumerate(
            [fp_ref[rows], ax[rows, cols], ay[rows, cols], axy[rows, cols], axm[rows, cols], cp_ref[rows], fu[rows]]
        ):
            edge_ref[pl.ds((side * 7 + f) * ROWS, ROWS)] = field


def side_tiles(send_a, send_b, recv_a, recv_b, even, packed):
    own_a, own_b, got_a, got_b = send_a[packed], send_b[packed], recv_a[packed], recv_b[packed]
    pick = lambda a, b: jnp.where(even, a, b)
    return pick(own_b, own_a), pick(own_a, own_b), pick(got_b, got_a), pick(got_a, got_b)


def outer_tile(from_west, from_east, f, k):
    lane1 = lane_of(from_west.shape)
    at = 4 * f + 32 * k
    east = pltpu.roll(from_east, (-at) % LANES, 1)
    west = pltpu.roll(from_west, (LANES - HALO - at) % LANES, 1)
    tile = jnp.where(lane1 < HALO, east, jnp.where(lane1 >= LANES - HALO, west, 0.0))
    if f == 3:
        extra = pltpu.roll(from_west, (LANES - HALO - 1 - 4 * 6 - 32 * k) % LANES, 1)
        tile = jnp.where(lane1 == LANES - HALO - 1, extra, tile)
    if f == 4:
        extra = pltpu.roll(from_east, (HALO - 4 * 6 - 1 - 32 * k) % LANES, 1)
        tile = jnp.where(lane1 == HALO, extra, tile)
    return tile


def force_with_sides(partial, mask, sides, k):
    own_west, own_east, from_west, from_east = sides
    lane1 = lane_of(own_west.shape)
    first, last = 4 * 6 + 32 * k, 4 * 6 + 3 + 32 * k
    outer = outer_tile(from_west, from_east, 0, k)
    tail = pltpu.roll(own_east, (-last) % LANES, 1)
    head = pltpu.roll(own_west, (LANES - 1 - first) % LANES, 1)
    change = jnp.where(lane1 == 0, -tail, jnp.where(lane1 == LANES - 1, head, 0.0))
    outer = outer + 0.5 * mask[:, -LANES:] * change
    begin = partial[:, :LANES] - jnp.where(
        lane1 == 0, 0.5 * mask[:, :LANES] * pltpu.roll(from_west, (-last) % LANES, 1), 0.0
    )
    middle = partial[:, LANES:-LANES]
    end = partial[:, -LANES:] + jnp.where(
        lane1 == LANES - 1,
        0.5 * mask[:, -2 * LANES : -LANES] * pltpu.roll(from_east, (LANES - 1 - first) % LANES, 1),
        0.0,
    )
    return jnp.concatenate([begin, middle, end, outer], axis=1)


def own_place():
    return lax.axis_index("blk"), lax.axis_index("sub")


def mask_group(block):
    if isinstance(block, int):
        return pl.ds(block * ROWS, ROWS)
    return pl.ds(pl.multiple_of(block * ROWS, ROWS), ROWS)


def mask_row(ocean, block_row, sub, tiles):
    lane1 = lane_of((1, LANES))
    parts = [jnp.full((1, LANES), ocean_at(ocean, block_row, sub * tiles + t), F32) for t in range(tiles)]
    east = ocean_at(ocean, block_row, (sub + 1) * tiles)
    west = ocean_at(ocean, block_row, sub * tiles - 1)
    parts.append(jnp.where(lane1 < LANES // 2, east, west))
    return jnp.concatenate(parts, axis=1)


def edge_kernel(masks, edges, send_a, send_b, recv_a, recv_b, _, rows_a, rows_b, *, row_count):
    col_count = edges.shape[1]
    tiles = col_count // LANES
    block_rows = row_count // BLOCK
    blk, sub = own_place()
    even_sub, even_blk = (sub % 2) == 0, (blk % 2) == 0
    shape = (ROWS, col_count + LANES)
    row8, lane8 = row_of(shape), lane_of(shape)
    crosses_west = (lane8 == 0) | (lane8 == col_count)
    crosses_east = (lane8 == col_count - 1) | (lane8 == col_count + LANES - 1)
    strips = row_count // (4 * ROWS)
    results = []
    for side, top in enumerate((True, False)):
        k = 0 if top else 3
        packed = pl.ds(0 if top else (strips - 1) * ROWS, ROWS)
        rows = [edges[pl.ds((side * 7 + f) * ROWS, ROWS)] for f in range(7)]
        sides = side_tiles(send_a, send_b, recv_a, recv_b, even_sub, packed)
        mask = masks[mask_group(0 if top else block_rows - 1)]
        fields = [force_with_sides(rows[0], mask, sides, k)]
        for f in range(1, 6):
            fields.append(jnp.concatenate([rows[f], outer_tile(sides[2], sides[3], f, k)], axis=1))
        flux = jnp.concatenate([rows[6], outer_tile(sides[2], sides[3], 7, k)], axis=1)
        if top:
            fields[1] = jnp.where(row8 == 3, pltpu.roll(flux, 3, 0), fields[1])
            half = lambda v: v
        else:
            extra = jnp.where(crosses_west, left(fields[2]) + left(down(fields[3])), 0.0)
            extra = extra + jnp.where(crosses_east, right(down(fields[4])), 0.0)
            fields[5] = fields[5] + jnp.where(row8 == 4, extra, 0.0)
            fields[2] = jnp.where(row8 == 4, pltpu.roll(flux, 5, 0), fields[2])
            half = lambda v: pltpu.roll(v, 4, 0)
        pieces = []
        for pair in range(3):
            one, two = half(fields[2 * pair]), half(fields[2 * pair + 1])
            pieces.append(jnp.where(row8 < 4, one, pltpu.roll(two, 4, 0)))
        results.append(pieces)
    for pair in range(3):
        rows = slice(pair * ROWS, (pair + 1) * ROWS)
        rows_a[rows] = jnp.where(even_blk, results[1][pair], results[0][pair])
        rows_b[rows] = jnp.where(even_blk, results[0][pair], results[1][pair])


def prepare_kernel(ax, ay, axy, axm, bly, nx, nxy, nxm, lxy, rxm):
    row_count, wide = ax.shape[0] - ROWS, ax.shape[1]
    cols = pl.ds(0, wide - LANES)
    lane8 = lane_of((ROWS, wide - LANES))
    end = lane8 == wide - LANES - 1

    def body(g, before):
        rows = pl.ds(pl.multiple_of(g * ROWS, ROWS), ROWS)
        here_xy, here_xm = axy[rows, cols], axm[rows, cols]
        bly[rows, cols] = jnp.where(lane8 == 0, 0.0, left(ay[rows, cols]))
        lxy[rows, cols] = jnp.where(lane8 == 0, 0.0, left(here_xy))
        rxm[rows, cols] = jnp.where(end, 0.0, right(here_xm))
        rolled = tuple(down(v) for v in (ax[rows, cols], here_xy, here_xm))
        for ring, a, b in zip((nx, nxy, nxm), before, rolled):
            ring[rows, cols] = shifted_rows(a, b)
        return rolled

    zero = jnp.zeros(lane8.shape, F32)
    lax.fori_loop(0, row_count // ROWS, body, (zero, zero, zero), unroll=4)


def widen_kernel(
    masks, fp, send_a, send_b, recv_a, recv_b,
    ax_in, ay_in, bly_in, nx_in, nxy_in, nxm_in, lxy_in, rxm_in, inv_in, c0_in, center_in,
    outer_center, ax, ay, bly, nx, nxy, nxm, lxy, rxm, inv, c0, center,
):
    row_count, col_count = fp.shape
    tiles = col_count // LANES
    block_rows = row_count // BLOCK
    groups = row_count // ROWS
    blk, sub = own_place()
    even_sub = (sub % 2) == 0
    lane1 = lane_of((ROWS, LANES))
    first, last, outer = pl.ds(0, LANES), pl.ds(col_count - LANES, LANES), pl.ds(col_count, LANES)
    west_edge, east_edge = lane1 == 0, lane1 == LANES - 1

    def at(g):
        return pl.ds(pl.multiple_of(g * ROWS, ROWS), ROWS)

    def widen(p, before):
        sides = side_tiles(send_a, send_b, recv_a, recv_b, even_sub, at(p))
        own_west, own_east, from_west, from_east = sides
        for k in range(4):
            g = 4 * p + k
            rows = at(g)
            new_f, new_x, new_y, new_xy, new_xm, new_c = [outer_tile(from_west, from_east, f, k) for f in range(6)]
            end_y = pltpu.roll(own_east, (-(4 * 2 + 3 + 32 * k)) % LANES, 1)
            end_xy = pltpu.roll(own_east, (-(4 * 3 + 3 + 32 * k)) % LANES, 1)
            begin_xm = pltpu.roll(own_west, (LANES - 1 - 4 * 4 - 32 * k) % LANES, 1)
            left_y, left_xy, right_xm = left(new_y), left(new_xy), right(new_xm)
            outer_y = jnp.where(west_edge, end_y, left_y)
            outer_xy = jnp.where(west_edge, end_xy, left_xy)
            outer_xm = jnp.where(east_edge, begin_xm, right_xm)
            rolled = [down(v) for v in (new_x, new_xy, new_xm, outer_xy, outer_xm, left_xy, right_xm)]
            up_x, up_xy, up_xm, up_outer_xy, up_outer_xm, up_left, up_right = [
                shifted_rows(a, b) for a, b in zip(before, rolled)
            ]
            before = rolled
            ax[rows, outer] = new_x
            ay[rows, outer] = new_y
            bly[rows, outer] = outer_y
            lxy[rows, outer] = outer_xy
            rxm[rows, outer] = outer_xm
            nx[rows, outer] = up_x
            nxy[rows, outer] = up_xy
            nxm[rows, outer] = up_xm
            bly[rows, first] = jnp.where(west_edge, left_y, bly[rows, first])
            lxy[rows, first] = jnp.where(west_edge, left_xy, lxy[rows, first])
            rxm[rows, last] = jnp.where(east_edge, right_xm, rxm[rows, last])
            center_first = center[rows, first] + jnp.where(west_edge, left_y + up_left, 0.0)
            center_last = center[rows, last] + jnp.where(east_edge, up_right, 0.0)
            center_outer = new_c + jnp.where(west_edge, outer_y + up_outer_xy, 0.0)
            center_outer = center_outer + jnp.where(east_edge, up_outer_xm, 0.0)
            center[rows, first] = center_first
            center[rows, last] = center_last
            outer_center[rows] = center_outer
            block = mask_group(g * ROWS // BLOCK)
            mask_first, mask_last, mask_outer = masks[block, first], masks[block, last], masks[block, outer]
            near, far = 4 * 6 + 32 * k, 4 * 6 + 3 + 32 * k
            tail = pltpu.roll(own_east, (-far) % LANES, 1)
            begin = pltpu.roll(own_west, (LANES - 1 - near) % LANES, 1)
            from_w = pltpu.roll(from_west, (-far) % LANES, 1)
            from_e = pltpu.roll(from_east, (LANES - 1 - near) % LANES, 1)
            force_first = fp[rows, first] - jnp.where(west_edge, (0.5 * mask_first) * from_w, 0.0)
            force_last = fp[rows, last] + jnp.where(east_edge, (0.5 * mask_last) * from_e, 0.0)
            change = jnp.where(west_edge, -tail, jnp.where(east_edge, begin, 0.0))
            force_outer = new_f + 0.5 * mask_outer * change
            inverse_first = mask_first * (1.0 / center_first)
            inverse_last = mask_last * (1.0 / center_last)
            inverse_outer = jnp.where(mask_outer > 0.0, 1.0 / jnp.where(center_outer > 0.0, center_outer, 1.0), 0.0)
            inv[rows, first] = inverse_first
            inv[rows, last] = inverse_last
            inv[rows, outer] = inverse_outer
            c0[rows, first] = force_first * inverse_first
            c0[rows, last] = force_last * inverse_last
            c0[rows, outer] = force_outer * inverse_outer
        return tuple(before)

    zero = jnp.zeros((ROWS, LANES), F32)
    lax.fori_loop(0, groups // 4, widen, (zero,) * 7)


def basis_kernel(
    masks, outer_center, edges, send_a, send_b, recv_a, recv_b, rows_a, rows_b,
    ax_in, ay_in, bly_in, nx_in, nxy_in, nxm_in, lxy_in, rxm_in, inv_in, c0_in, center_in,
    c1, c2, c3, c4, gram_ref, ax, ay, bly, nx, nxy, nxm, lxy, rxm, inv, c0, center,
):
    row_count, col_count = center.shape
    tiles = col_count // LANES
    wide = col_count + LANES
    block_rows = row_count // BLOCK
    groups = row_count // ROWS
    blk, sub = own_place()
    even_sub, even_blk = (sub % 2) == 0, (blk % 2) == 0
    row8, lane8 = row_of((ROWS, wide)), lane_of((ROWS, wide))
    row1, lane1 = row_of((ROWS, LANES)), lane_of((ROWS, LANES))
    first, last, outer = pl.ds(0, LANES), pl.ds(col_count - LANES, LANES), pl.ds(col_count, LANES)
    west_edge, east_edge = lane1 == 0, lane1 == LANES - 1

    def at(g):
        return pl.ds(pl.multiple_of(g * ROWS, ROWS), ROWS)

    pieces = []
    for pair in range(3):
        rows = slice(pair * ROWS, (pair + 1) * ROWS)
        below = jnp.where(even_blk, rows_a[rows], rows_b[rows])
        above = jnp.where(even_blk, rows_b[rows], rows_a[rows])
        pieces.append(jnp.where(row8 < 4, below, pltpu.roll(above, 4, 0)))
        pieces.append(jnp.where(row8 < 4, pltpu.roll(below, 4, 0), above))
    out_f, out_x, out_y, out_xy, out_xm, out_c = pieces
    flux_below, flux_above = out_x[3:4], out_y[4:5]

    def edge_group(side, k):
        strip = 0 if side == 0 else groups // 4 - 1
        sides = side_tiles(send_a, send_b, recv_a, recv_b, even_sub, at(strip))
        get = lambda f: edges[pl.ds((side * 7 + f) * ROWS, ROWS)]
        full = [
            jnp.concatenate([get(e), outer_tile(sides[2], sides[3], f, k)], axis=1)
            for e, f in ((1, 1), (3, 3), (4, 4), (6, 7))
        ]
        mask = masks[mask_group(0 if side == 0 else block_rows - 1)]
        return full, mask, force_with_sides(get(0), mask, sides, k)

    (_, _, _, flux_first), mask_first, force_first = edge_group(0, 0)
    (x_last, xy_last, xm_last, flux_last), mask_last, force_last = edge_group(1, 3)
    mask_below, mask_above = masks[mask_group(block_rows)], masks[mask_group(block_rows + 1)]

    def inverse_of(mask, total):
        return jnp.where(mask > 0.0, 1.0 / jnp.where(total > 0.0, total, 1.0), 0.0)

    head = row8 == 0
    own_first = pl.ds(0, ROWS)
    up = []
    for ring, out in ((nx, out_x), (nxy, out_xy), (nxm, out_xm)):
        moved = jnp.where(head, down(out), ring[own_first])
        ring[own_first] = moved
        up.append(moved)
    total = jnp.concatenate([center[own_first], outer_center[own_first]], axis=1)
    total = total + jnp.where(head, up[0] + left(up[1]) + right(up[2]), 0.0)
    center[own_first] = total[:, :col_count]
    inverse = inverse_of(mask_first, total)
    inv[own_first] = inverse
    c0[own_first] = inverse * (force_first - jnp.where(head, 0.5 * mask_first * flux_above, 0.0))
    own_last = pl.ds(row_count - ROWS, ROWS)
    c0[own_last] = inv[own_last] * (
        force_last + jnp.where(row8 == ROWS - 1, 0.5 * mask_last * flux_below, 0.0)
    )
    ring_rows = pl.ds(row_count, ROWS)
    up = [
        jnp.where(head, down(before), down(out))
        for before, out in ((x_last, out_x), (xy_last, out_xy), (xm_last, out_xm))
    ]
    left_y = left(out_y)
    for ring, value in (
        (ax, out_x), (ay, out_y), (bly, left_y), (nx, up[0]), (nxy, up[1]), (nxm, up[2]),
        (lxy, left(out_xy)), (rxm, right(out_xm)),
    ):
        ring[ring_rows] = value
    crosses_west = (row8 != 4) & ((lane8 == 0) | (lane8 == col_count))
    crosses_east = (row8 != 4) & ((lane8 == col_count - 1) | (lane8 == wide - 1))
    total = out_c + jnp.where(head, up[0], 0.0)
    total = total + jnp.where(crosses_west, left_y, 0.0)
    total = total + jnp.where(head | crosses_west, left(up[1]), 0.0)
    total = total + jnp.where(head | crosses_east, right(up[2]), 0.0)
    inverse = inverse_of(jnp.where(row8 < 4, mask_below, mask_above), total)
    out_f = out_f - jnp.where(head, 0.5 * mask_below * flux_last[ROWS - 1 : ROWS], 0.0)
    out_f = out_f + jnp.where(row8 == ROWS - 1, 0.5 * mask_above * flux_first[0:1], 0.0)
    inv[ring_rows] = inverse
    c0[ring_rows] = inverse * out_f

    def sides_of(source, g, width):
        value = source[at(g)]
        return left(value)[:, :width], right(value)[:, :width]

    def terms(source, g, width, turned):
        rows, cols = at(g), pl.ds(0, width)
        west, east = turned
        here = source[rows, cols]
        same = ay[rows, cols] * east + bly[rows, cols] * west
        after = ax[rows, cols] * here + lxy[rows, cols] * west + rxm[rows, cols] * east
        before = nx[rows, cols] * here + nxy[rows, cols] * east + nxm[rows, cols] * west
        return same, down(after), pltpu.roll(before, ROWS - 1, 0)

    def sweep(source, count, width, finish):
        ring_turned, turned, following = [sides_of(source, g, width) for g in (groups, 0, 1)]
        _, ring_after, _ = terms(source, groups, width, ring_turned)
        same, after, own_first = terms(source, 0, width, turned)
        tail = row_of((ROWS, width)) == ROWS - 1

        def body(g, carry):
            partial, own, previous, turned = carry
            following = sides_of(source, jnp.minimum(g + 1, groups), width)
            same, after, later = terms(source, g, width, turned)
            finish(g - 1, partial + jnp.where(tail, later, own))
            return same + shifted_rows(previous, after), later, after, following

        carry = (same + shifted_rows(ring_after, after), own_first, after, following)
        partial, own, _, turned = lax.fori_loop(1, count, body, carry, unroll=UNROLL)
        if count > groups:
            later = own_first
        else:
            later = terms(source, groups, width, turned)[2]
        finish(count - 1, partial + jnp.where(tail, later, own))

    def step(source, target, subtract):
        def finish(g, total):
            rows = at(g)
            moved = inv[rows] * total
            target[rows] = source[rows] - moved if subtract else moved

        sweep(source, groups + 1, wide, finish)

    step(c0, c1, True)
    step(c1, c2, False)
    step(c2, c3, False)

    cols = pl.ds(0, col_count)

    def last_finish(g, total):
        c4[at(g)] = inv[at(g), cols] * total

    sweep(c3, groups, col_count, last_finish)

    def add_products(g, sums):
        rows = at(g)
        basis = [ref[rows, cols] for ref in (c0, c1, c2, c3)] + [c4[rows]]
        weight = center[rows]
        weighted = [weight * b for b in basis]
        new = []
        for (i, j), total in zip(PAIRS, sums):
            product = basis[i] * weighted[j]
            part = product[:, :LANES]
            for t in range(1, tiles):
                part = part + product[:, t * LANES : (t + 1) * LANES]
            new.append(total + part)
        return tuple(new)

    zero = jnp.zeros((ROWS, LANES), F32)
    sums = lax.fori_loop(0, groups, add_products, tuple(zero for _ in PAIRS), unroll=2)

    count = len(PAIRS)
    high = jnp.zeros((2 * ROWS, LANES), F32)
    low = high
    place = row_of((2 * ROWS, LANES))
    for index, total in enumerate(sums):
        error = jnp.zeros_like(total)
        for shift in (4, 2, 1):
            total, rounding = two_sum(total, pltpu.roll(total, shift, 0))
            error = error + pltpu.roll(error, shift, 0) + rounding
        high = jnp.where(place == index, total[0:1], high)
        low = jnp.where(place == index, error[0:1], low)
    for shift in (64, 32, 16, 8, 4, 2, 1):
        high, rounding = two_sum(high, pltpu.roll(high, shift, 1))
        low = low + pltpu.roll(low, shift, 1) + rounding
    lane2 = lane_of((2 * ROWS, LANES))
    packed = jnp.where(lane2 == place, high, jnp.where(lane2 == place + LANES // 2, low, 0.0))
    gram_ref[...] = jnp.broadcast_to(jnp.sum(packed, axis=0, keepdims=True), gram_ref.shape)


def finish_kernel(gram_ref, c0, c1, c2, c3, c4, center_ref, height_ref, residual_ref):
    lane1 = lane_of((1, LANES))
    high = gram_ref[...]
    low = jnp.zeros_like(high)
    while high.shape[0] > 1:
        half = high.shape[0] // 2
        high, rounding = two_sum(high[:half], high[half:])
        low = low[:half] + low[half:] + rounding
    entries = high + (low + pltpu.roll(high, LANES // 2, 1))
    size = ITERS + 1
    gram = {}
    for index, (i, j) in enumerate(PAIRS):
        entry = jnp.sum(jnp.where(lane1 == index, entries, 0.0), axis=1, keepdims=True)
        gram[i, j] = entry
        gram[j, i] = entry
    zero = jnp.zeros((1, 1), F32)
    one = jnp.ones((1, 1), F32)

    def image(coefs):
        result = [zero, coefs[0] + coefs[1]]
        for j in range(2, size):
            own = coefs[j] if j < size - 1 else zero
            result.append(own - coefs[j - 1])
        return result

    def form(one_side, products):
        total = zero
        for a, b in zip(one_side, products):
            total = total + a * b
        return total

    scaled = [one] + [zero] * (size - 1)
    search = [zero] * size
    height = [zero] * size
    rho_old, sigma = one, zero
    for iteration in range(ITERS):
        limit = iteration + 1
        products = []
        for j in range(size):
            total = zero
            for i in range(limit):
                total = total + scaled[i] * gram[i, j]
            products.append(total)
        rho = form(scaled[:limit], products)
        curvature = form(image(scaled)[: limit + 1], products)
        beta = rho / rho_old
        sigma = curvature - beta * beta * sigma
        alpha = rho / sigma
        rho_old = rho
        search = [s + beta * q for s, q in zip(scaled, search)]
        height = [h + alpha * q for h, q in zip(height, search)]
        scaled = [s - alpha * q for s, q in zip(scaled, image(search))]

    def combine(g, _):
        rows = pl.ds(pl.multiple_of(g * ROWS, ROWS), ROWS)
        cols = pl.ds(0, center_ref.shape[1])
        basis = [ref[rows, cols] for ref in (c0, c1, c2, c3, c4)]
        total = height[0] * basis[0]
        for j in range(1, size - 1):
            total = total + height[j] * basis[j]
        height_ref[rows] = total
        total = scaled[0] * basis[0]
        for j in range(1, size):
            total = total + scaled[j] * basis[j]
        residual_ref[rows] = center_ref[rows] * total
        return 0

    lax.fori_loop(0, center_ref.shape[0] // ROWS, combine, 0, unroll=2)


def swap(value, axis, parity):
    peers = lax.axis_size(axis)
    pairs = []
    for i in range(parity, peers - 1, 2):
        pairs += [(i, i + 1), (i + 1, i)]
    return lax.ppermute(value, axis, pairs)


def body(u_flow, v_flow, thickness, depth_levels, block_ocean, coef_x, coef_y, coef_xy, coef_xm, extra_diagonal):
    levels, row_count, col_count = u_flow.shape
    wide = col_count + LANES
    shape = lambda *dims: pltpu.VMEM(dims, F32)
    final = jax.ShapeDtypeStruct((row_count, col_count), F32)
    far = lambda array: pltpu.with_memory_space_constraint(array, pltpu.HBM)
    plane = shape(row_count, col_count)
    ring = shape(row_count + ROWS, wide)
    strip = shape(row_count // 4, LANES)
    flow = pltpu.VMEM((levels, row_count, col_count), F32)
    field = pltpu.VMEM((row_count, col_count), F32)
    fp, cp, edges, send_a, send_b, *rings, masks = pl.pallas_call(
        flux_kernel,
        out_shape=(plane, plane, shape(14 * ROWS, col_count), strip, strip)
        + (ring,) * 6
        + (shape((row_count // BLOCK + 2) * ROWS, wide),),
        in_specs=[HBM] * 10,
        out_specs=(VMEM,) * 12,
        scratch_shapes=[flow, flow, pltpu.VMEM((row_count, col_count), jnp.int32)]
        + [field] * 3
        + [pltpu.SMEM(thickness.shape, F32), pltpu.SMEM(block_ocean.shape, jnp.int32)]
        + [pltpu.SemaphoreType.DMA((2, row_count // CHUNK)), pltpu.SemaphoreType.DMA((6,)), pltpu.SemaphoreType.DMA((2,))],
        compiler_params=pltpu.CompilerParams(vmem_limit_bytes=FLUX_LIMIT),
        name="flux",
    )(
        *[far(a) for a in (thickness, block_ocean, u_flow, v_flow, depth_levels, coef_x, coef_y, coef_xy, coef_xm, extra_diagonal)],
    )
    recv_a, recv_b = swap(send_a, "sub", 0), swap(send_b, "sub", 1)
    ax, ay, axy, axm, inv, c0 = rings
    moved = pl.pallas_call(
        prepare_kernel,
        out_shape=(ring,) * 6,
        in_specs=[VMEM] * 4,
        out_specs=(VMEM,) * 6,
        compiler_params=pltpu.CompilerParams(vmem_limit_bytes=8 << 20),
        cost_estimate=pl.CostEstimate(flops=10 << 20, bytes_accessed=4 << 20, transcendentals=0),
        name="prepare",
    )(ax, ay, axy, axm)
    edge = shape(3 * ROWS, wide)
    edge_a, edge_b = pl.pallas_call(
        functools.partial(edge_kernel, row_count=row_count),
        out_shape=(edge, edge),
        in_specs=[VMEM] * 7,
        out_specs=(VMEM,) * 2,
        compiler_params=pltpu.CompilerParams(vmem_limit_bytes=8 << 20),
        name="edge",
    )(masks, edges, send_a, send_b, recv_a, recv_b, moved[0])
    rows_a, rows_b = swap(edge_a, "blk", 0), swap(edge_b, "blk", 1)
    outer_center, *rings = pl.pallas_call(
        widen_kernel,
        out_shape=(shape(row_count, LANES),) + (ring,) * 10 + (plane,),
        in_specs=[VMEM] * 17,
        out_specs=(VMEM,) * 12,
        input_output_aliases={6 + i: 1 + i for i in range(11)},
        compiler_params=pltpu.CompilerParams(vmem_limit_bytes=8 << 20),
        cost_estimate=pl.CostEstimate(flops=10 << 20, bytes_accessed=4 << 20, transcendentals=0),
        name="widen",
    )(masks, fp, send_a, send_b, recv_a, recv_b, ax, ay, *moved, inv, c0, cp)
    devices = lax.axis_size("blk") * lax.axis_size("sub")
    c1, c2, c3, c4, gram, *rest = pl.pallas_call(
        basis_kernel,
        out_shape=(ring, ring, ring, plane, shape(devices, LANES)) + (ring,) * 10 + (plane,),
        in_specs=[VMEM] * 20,
        out_specs=(VMEM,) * 16,
        input_output_aliases={9 + i: 5 + i for i in range(11)},
        compiler_params=pltpu.CompilerParams(vmem_limit_bytes=8 << 20),
        name="basis",
    )(masks, outer_center, edges, send_a, send_b, recv_a, recv_b, rows_a, rows_b, *rings)
    c0, center = rest[-2], rest[-1]
    gram = lax.all_to_all(gram, ("blk", "sub"), 0, 0, tiled=True)
    return pl.pallas_call(
        finish_kernel,
        out_shape=(final, final),
        in_specs=[VMEM] * 7,
        out_specs=(VMEM,) * 2,
        compiler_params=pltpu.CompilerParams(vmem_limit_bytes=8 << 20),
        name="finish",
    )(gram, c0, c1, c2, c3, c4, center)


def solution(mesh):
    placed = (
        P(None, "blk", "sub"),
        P(None, "blk", "sub"),
        P(),
        P("blk", "sub"),
        P(),
        P("blk", "sub"),
        P("blk", "sub"),
        P("blk", "sub"),
        P("blk", "sub"),
        P("blk", "sub"),
    )
    return jax.shard_map(
        body,
        mesh=mesh,
        in_specs=placed,
        out_specs=(P("blk", "sub"), P("blk", "sub")),
        check_vma=False,
    )
```

```python
import functools

import jax
import jax.numpy as jnp
from jax import lax
from jax.experimental import pallas as pl
from jax.experimental.pallas import tpu as pltpu
from jax.sharding import PartitionSpec as P

BLOCK = 128
ITERS = 4
HALO = ITERS
LANES = 128
ROWS = 8
CHUNK = 32
PIECE = 16
AHEAD = 6
UNROLL = 8
PARTS = 4
F32 = jnp.float32
FLUX_LIMIT = 40 << 20
VMEM = pl.BlockSpec(memory_space=pltpu.VMEM)
HBM = pl.BlockSpec(memory_space=pltpu.HBM)
PAIRS = [(i, j) for i in range(ITERS) for j in range(i, ITERS + 1)]


def lane_of(shape):
    return lax.broadcasted_iota(jnp.int32, shape, len(shape) - 1)


def row_of(shape):
    return lax.broadcasted_iota(jnp.int32, shape, len(shape) - 2)


def shifted_rows(before, here):
    return jnp.where(row_of(here.shape) == 0, before, here)


def left(value):
    return pltpu.roll(value, 1, 1)


def right(value):
    return pltpu.roll(value, value.shape[1] - 1, 1)


def down(value):
    return pltpu.roll(value, 1, 0)


def two_sum(a, b):
    total = a + b
    other = total - a
    return total, (a - (total - other)) + (b - other)


def ocean_at(ocean_ref, row, col):
    block_rows, block_cols = ocean_ref.shape
    inside = (row >= 0) & (row < block_rows) & (col >= 0) & (col < block_cols)
    entry = ocean_ref[jnp.clip(row, 0, block_rows - 1), jnp.clip(col, 0, block_cols - 1)]
    return jnp.where(inside & (entry == 1), 1.0, 0.0).astype(F32)


def flux_kernel(
    thick_hbm, ocean_hbm, u_hbm, v_hbm, depth_hbm, cx_hbm, cy_hbm, cxy_hbm, cxm_hbm, ex_hbm,
    fp_ref, cp_ref, edge_ref, pack_a, pack_b, ax, ay, axy, axm, masks,
    u_buf, v_buf, depth, ex, fu, fv, thick, ocean, sems, coef_sem, small_sem,
):
    levels, row_count, col_count = u_buf.shape
    tiles = col_count // LANES
    chunks = row_count // CHUNK
    pieces = row_count // PIECE
    groups = row_count // ROWS
    steps = CHUNK // ROWS
    blk, sub = own_place()
    block_rows = row_count // BLOCK
    own = (pl.ds(0, row_count), pl.ds(0, col_count))
    coef_copies = [
        pltpu.make_async_copy(src, dst, coef_sem.at[i])
        for i, (src, dst) in enumerate(
            [
                (depth_hbm, depth), (ex_hbm, ex), (cx_hbm, ax.at[own]), (cy_hbm, ay.at[own]),
                (cxy_hbm, axy.at[own]), (cxm_hbm, axm.at[own]),
            ]
        )
    ]

    def flow_copies(c):
        rows = pl.ds(pl.multiple_of(c * PIECE, PIECE), PIECE)
        return (
            pltpu.make_async_copy(u_hbm.at[:, rows, :], u_buf.at[:, rows, :], sems.at[0, c]),
            pltpu.make_async_copy(v_hbm.at[:, rows, :], v_buf.at[:, rows, :], sems.at[1, c]),
        )

    small_copies = [
        pltpu.make_async_copy(src, dst, small_sem.at[i])
        for i, (src, dst) in enumerate([(thick_hbm, thick), (ocean_hbm, ocean)])
    ]
    for copy in small_copies:
        copy.start()
    coef_copies[0].start()
    for copy in flow_copies(0):
        copy.start()
    for copy in coef_copies[1:]:
        copy.start()
    for c in range(1, AHEAD):
        for copy in flow_copies(c):
            copy.start()
    for copy in small_copies:
        copy.wait()
    for place in range(block_rows + 2):
        block_row = blk * block_rows + (place if place <= block_rows else -1)
        masks[mask_group(place)] = jnp.broadcast_to(
            mask_row(ocean, block_row, sub, tiles), (ROWS, col_count + LANES)
        )
    coef_copies[0].wait()

    row8 = row_of((ROWS, col_count))
    lane8 = lane_of((ROWS, col_count))
    lane1 = lane_of((ROWS, LANES))
    cols = pl.ds(0, col_count)
    even = (sub % 2) == 0

    def at(g):
        return pl.ds(pl.multiple_of(g * ROWS, ROWS), ROWS)

    def west_of(value):
        return jnp.where(lane8 == 0, 0.0, left(value))

    def east_of(value):
        return jnp.where(lane8 == col_count - 1, 0.0, right(value))

    def rolled_fields(rows):
        return [
            down(v) for v in (ax[rows, cols], west_of(axy[rows, cols]), east_of(axm[rows, cols]), fu[rows])
        ]

    def sum_group(g):
        rows = at(g)
        for t in range(tiles):
            lanes = pl.ds(t * LANES, LANES)
            mask = masks[mask_group(g * ROWS // BLOCK), lanes]
            deep = depth[rows, lanes]
            total_u = jnp.zeros((ROWS, LANES), F32)
            total_v = total_u
            for k in range(levels):
                active = jnp.where(deep > k, thick[k], 0.0)
                total_u = total_u + active * u_buf[k, rows, lanes]
                total_v = total_v + active * v_buf[k, rows, lanes]
            fu[rows, lanes] = mask * total_u
            fv[rows, lanes] = mask * total_v

    def group_work(g, k, before):
        rows = at(g)
        here_x, here_y, here_xy, here_xm = ax[rows, cols], ay[rows, cols], axy[rows, cols], axm[rows, cols]
        here_u, here_v = fu[rows], fv[rows]
        west_xy, east_xm, west_y = west_of(here_xy), east_of(here_xm), west_of(here_y)
        rolled = [down(v) for v in (here_x, west_xy, east_xm, here_u)]
        up_x, up_west, up_east, up_u = [shifted_rows(a, b) for a, b in zip(before, rolled)]
        total = ex[rows] + here_x
        total = total + up_x
        total = total + here_y
        total = total + west_y
        total = total + here_xy
        total = total + up_west
        total = total + here_xm
        total = total + up_east
        cp_ref[rows] = total
        after = fu[at(jnp.minimum(g + 1, groups - 1))]
        after = jnp.where(g + 1 < groups, pltpu.roll(after, ROWS - 1, 0), 0.0)
        below = jnp.where(row8 == ROWS - 1, after, pltpu.roll(here_u, ROWS - 1, 0))
        change = 0.5 * ((below - up_u) + (east_of(here_v) - west_of(here_v)))
        mask = masks[mask_group(g * ROWS // BLOCK), cols]
        partial = mask * change
        fp_ref[rows] = partial
        fields = [partial, here_x, here_y, here_xy, here_xm, total, here_v, here_u]
        to_west = jnp.zeros((ROWS, LANES), F32)
        to_east = to_west
        for f, field in enumerate(fields):
            lane = 4 * f + 32 * k
            chosen = (lane1 >= lane) & (lane1 < lane + HALO)
            to_west = jnp.where(chosen, pltpu.roll(field[:, :LANES], lane, 1), to_west)
            to_east = jnp.where(chosen, pltpu.roll(field[:, -LANES:], (lane + HALO) % LANES, 1), to_east)
        lane = 4 * 6 + 32 * k
        extra = pltpu.roll(here_xm[:, :LANES], (lane + 1 - HALO) % LANES, 1)
        to_west = jnp.where(lane1 == lane + 1, extra, to_west)
        extra = pltpu.roll(here_xy[:, -LANES:], (lane + HALO + 1) % LANES, 1)
        to_east = jnp.where(lane1 == lane, extra, to_east)
        packed = at(g // 4)
        for_a = jnp.where(even, to_east, to_west)
        for_b = jnp.where(even, to_west, to_east)
        if k == 0:
            pack_a[packed] = for_a
            pack_b[packed] = for_b
        else:
            pack_a[packed] = pack_a[packed] + for_a
            pack_b[packed] = pack_b[packed] + for_b
        return rolled

    def work_from(g, k):
        before = rolled_fields(at(jnp.maximum(g - 1, 0)))
        return group_work(g, k, [jnp.where(g > 0, b, 0.0) for b in before])

    def chunk(c, _):
        def piece(i, _):
            p = c * (CHUNK // PIECE) + i
            for copy in flow_copies(p):
                copy.wait()

            @pl.when(p + AHEAD < pieces)
            def _():
                for copy in flow_copies(p + AHEAD):
                    copy.start()

            for j in range(PIECE // ROWS):
                sum_group(p * (PIECE // ROWS) + j)
            return 0

        lax.fori_loop(0, CHUNK // PIECE, piece, 0)

        @pl.when(c == 0)
        def _():
            for copy in coef_copies[1:]:
                copy.wait()

        @pl.when(c > 0)
        def _():
            work_from(c * steps - 1, 3)

        carry = work_from(c * steps, 0)
        for k in range(1, steps - 1):
            carry = group_work(c * steps + k, k, carry)
        return 0

    lax.fori_loop(0, chunks, chunk, 0)
    work_from(groups - 1, 3)
    for side, base in enumerate((0, row_count - ROWS)):
        rows = pl.ds(base, ROWS)
        for f, field in enumerate(
            [fp_ref[rows], ax[rows, cols], ay[rows, cols], axy[rows, cols], axm[rows, cols], cp_ref[rows], fu[rows]]
        ):
            edge_ref[pl.ds((side * 7 + f) * ROWS, ROWS)] = field


def side_tiles(send_a, send_b, recv_a, recv_b, even, packed):
    own_a, own_b, got_a, got_b = send_a[packed], send_b[packed], recv_a[packed], recv_b[packed]
    pick = lambda a, b: jnp.where(even, a, b)
    return pick(own_b, own_a), pick(own_a, own_b), pick(got_b, got_a), pick(got_a, got_b)


def outer_tile(from_west, from_east, f, k):
    lane1 = lane_of(from_west.shape)
    at = 4 * f + 32 * k
    east = pltpu.roll(from_east, (-at) % LANES, 1)
    west = pltpu.roll(from_west, (LANES - HALO - at) % LANES, 1)
    tile = jnp.where(lane1 < HALO, east, jnp.where(lane1 >= LANES - HALO, west, 0.0))
    if f == 3:
        extra = pltpu.roll(from_west, (LANES - HALO - 1 - 4 * 6 - 32 * k) % LANES, 1)
        tile = jnp.where(lane1 == LANES - HALO - 1, extra, tile)
    if f == 4:
        extra = pltpu.roll(from_east, (HALO - 4 * 6 - 1 - 32 * k) % LANES, 1)
        tile = jnp.where(lane1 == HALO, extra, tile)
    return tile


def force_with_sides(partial, mask, sides, k):
    own_west, own_east, from_west, from_east = sides
    lane1 = lane_of(own_west.shape)
    first, last = 4 * 6 + 32 * k, 4 * 6 + 3 + 32 * k
    outer = outer_tile(from_west, from_east, 0, k)
    tail = pltpu.roll(own_east, (-last) % LANES, 1)
    head = pltpu.roll(own_west, (LANES - 1 - first) % LANES, 1)
    change = jnp.where(lane1 == 0, -tail, jnp.where(lane1 == LANES - 1, head, 0.0))
    outer = outer + 0.5 * mask[:, -LANES:] * change
    begin = partial[:, :LANES] - jnp.where(
        lane1 == 0, 0.5 * mask[:, :LANES] * pltpu.roll(from_west, (-last) % LANES, 1), 0.0
    )
    middle = partial[:, LANES:-LANES]
    end = partial[:, -LANES:] + jnp.where(
        lane1 == LANES - 1,
        0.5 * mask[:, -2 * LANES : -LANES] * pltpu.roll(from_east, (LANES - 1 - first) % LANES, 1),
        0.0,
    )
    return jnp.concatenate([begin, middle, end, outer], axis=1)


def own_place():
    return lax.axis_index("blk"), lax.axis_index("sub")


def mask_group(block):
    if isinstance(block, int):
        return pl.ds(block * ROWS, ROWS)
    return pl.ds(pl.multiple_of(block * ROWS, ROWS), ROWS)


def mask_row(ocean, block_row, sub, tiles):
    lane1 = lane_of((1, LANES))
    parts = [jnp.full((1, LANES), ocean_at(ocean, block_row, sub * tiles + t), F32) for t in range(tiles)]
    east = ocean_at(ocean, block_row, (sub + 1) * tiles)
    west = ocean_at(ocean, block_row, sub * tiles - 1)
    parts.append(jnp.where(lane1 < LANES // 2, east, west))
    return jnp.concatenate(parts, axis=1)


def edge_kernel(masks, edges, send_a, send_b, recv_a, recv_b, _, rows_a, rows_b, *, row_count):
    col_count = edges.shape[1]
    tiles = col_count // LANES
    block_rows = row_count // BLOCK
    blk, sub = own_place()
    even_sub, even_blk = (sub % 2) == 0, (blk % 2) == 0
    shape = (ROWS, col_count + LANES)
    row8, lane8 = row_of(shape), lane_of(shape)
    crosses_west = (lane8 == 0) | (lane8 == col_count)
    crosses_east = (lane8 == col_count - 1) | (lane8 == col_count + LANES - 1)
    strips = row_count // (4 * ROWS)
    results = []
    for side, top in enumerate((True, False)):
        k = 0 if top else 3
        packed = pl.ds(0 if top else (strips - 1) * ROWS, ROWS)
        rows = [edges[pl.ds((side * 7 + f) * ROWS, ROWS)] for f in range(7)]
        sides = side_tiles(send_a, send_b, recv_a, recv_b, even_sub, packed)
        mask = masks[mask_group(0 if top else block_rows - 1)]
        fields = [force_with_sides(rows[0], mask, sides, k)]
        for f in range(1, 6):
            fields.append(jnp.concatenate([rows[f], outer_tile(sides[2], sides[3], f, k)], axis=1))
        flux = jnp.concatenate([rows[6], outer_tile(sides[2], sides[3], 7, k)], axis=1)
        if top:
            fields[1] = jnp.where(row8 == 3, pltpu.roll(flux, 3, 0), fields[1])
            half = lambda v: v
        else:
            extra = jnp.where(crosses_west, left(fields[2]) + left(down(fields[3])), 0.0)
            extra = extra + jnp.where(crosses_east, right(down(fields[4])), 0.0)
            fields[5] = fields[5] + jnp.where(row8 == 4, extra, 0.0)
            fields[2] = jnp.where(row8 == 4, pltpu.roll(flux, 5, 0), fields[2])
            half = lambda v: pltpu.roll(v, 4, 0)
        pieces = []
        for pair in range(3):
            one, two = half(fields[2 * pair]), half(fields[2 * pair + 1])
            pieces.append(jnp.where(row8 < 4, one, pltpu.roll(two, 4, 0)))
        results.append(pieces)
    for pair in range(3):
        rows = slice(pair * ROWS, (pair + 1) * ROWS)
        rows_a[rows] = jnp.where(even_blk, results[1][pair], results[0][pair])
        rows_b[rows] = jnp.where(even_blk, results[0][pair], results[1][pair])


def prepare_kernel(fp, cp, masks, ax, ay, axy, axm, bly, nx, nxy, nxm, lxy, rxm, inv, c0):
    row_count, wide = ax.shape[0] - ROWS, ax.shape[1]
    cols = pl.ds(0, wide - LANES)
    lane8 = lane_of((ROWS, wide - LANES))
    end = lane8 == wide - LANES - 1

    def body(g, before):
        rows = pl.ds(pl.multiple_of(g * ROWS, ROWS), ROWS)
        here_xy, here_xm = axy[rows, cols], axm[rows, cols]
        bly[rows, cols] = jnp.where(lane8 == 0, 0.0, left(ay[rows, cols]))
        lxy[rows, cols] = jnp.where(lane8 == 0, 0.0, left(here_xy))
        rxm[rows, cols] = jnp.where(end, 0.0, right(here_xm))
        rolled = tuple(down(v) for v in (ax[rows, cols], here_xy, here_xm))
        for ring, a, b in zip((nx, nxy, nxm), before, rolled):
            ring[rows, cols] = shifted_rows(a, b)
        inverse = masks[mask_group(g * ROWS // BLOCK), cols] * (1.0 / cp[rows])
        inv[rows, cols] = inverse
        c0[rows, cols] = fp[rows] * inverse
        return rolled

    zero = jnp.zeros(lane8.shape, F32)
    lax.fori_loop(0, row_count // ROWS, body, (zero, zero, zero), unroll=4)


def widen_kernel(
    masks, fp, send_a, send_b, recv_a, recv_b,
    ax_in, ay_in, bly_in, nx_in, nxy_in, nxm_in, lxy_in, rxm_in, inv_in, c0_in, center_in,
    outer_center, ax, ay, bly, nx, nxy, nxm, lxy, rxm, inv, c0, center,
):
    row_count, col_count = fp.shape
    tiles = col_count // LANES
    block_rows = row_count // BLOCK
    groups = row_count // ROWS
    blk, sub = own_place()
    even_sub = (sub % 2) == 0
    lane1 = lane_of((ROWS, LANES))
    first, last, outer = pl.ds(0, LANES), pl.ds(col_count - LANES, LANES), pl.ds(col_count, LANES)
    west_edge, east_edge = lane1 == 0, lane1 == LANES - 1

    def at(g):
        return pl.ds(pl.multiple_of(g * ROWS, ROWS), ROWS)

    def widen(p, before):
        sides = side_tiles(send_a, send_b, recv_a, recv_b, even_sub, at(p))
        own_west, own_east, from_west, from_east = sides
        for k in range(4):
            g = 4 * p + k
            rows = at(g)
            new_f, new_x, new_y, new_xy, new_xm, new_c = [outer_tile(from_west, from_east, f, k) for f in range(6)]
            end_y = pltpu.roll(own_east, (-(4 * 2 + 3 + 32 * k)) % LANES, 1)
            end_xy = pltpu.roll(own_east, (-(4 * 3 + 3 + 32 * k)) % LANES, 1)
            begin_xm = pltpu.roll(own_west, (LANES - 1 - 4 * 4 - 32 * k) % LANES, 1)
            left_y, left_xy, right_xm = left(new_y), left(new_xy), right(new_xm)
            outer_y = jnp.where(west_edge, end_y, left_y)
            outer_xy = jnp.where(west_edge, end_xy, left_xy)
            outer_xm = jnp.where(east_edge, begin_xm, right_xm)
            rolled = [down(v) for v in (new_x, new_xy, new_xm, outer_xy, outer_xm, left_xy, right_xm)]
            up_x, up_xy, up_xm, up_outer_xy, up_outer_xm, up_left, up_right = [
                shifted_rows(a, b) for a, b in zip(before, rolled)
            ]
            before = rolled
            ax[rows, outer] = new_x
            ay[rows, outer] = new_y
            bly[rows, outer] = outer_y
            lxy[rows, outer] = outer_xy
            rxm[rows, outer] = outer_xm
            nx[rows, outer] = up_x
            nxy[rows, outer] = up_xy
            nxm[rows, outer] = up_xm
            bly[rows, first] = jnp.where(west_edge, left_y, bly[rows, first])
            lxy[rows, first] = jnp.where(west_edge, left_xy, lxy[rows, first])
            rxm[rows, last] = jnp.where(east_edge, right_xm, rxm[rows, last])
            center_first = center[rows, first] + jnp.where(west_edge, left_y + up_left, 0.0)
            center_last = center[rows, last] + jnp.where(east_edge, up_right, 0.0)
            center_outer = new_c + jnp.where(west_edge, outer_y + up_outer_xy, 0.0)
            center_outer = center_outer + jnp.where(east_edge, up_outer_xm, 0.0)
            center[rows, first] = center_first
            center[rows, last] = center_last
            outer_center[rows] = center_outer
            block = mask_group(g * ROWS // BLOCK)
            mask_first, mask_last, mask_outer = masks[block, first], masks[block, last], masks[block, outer]
            near, far = 4 * 6 + 32 * k, 4 * 6 + 3 + 32 * k
            tail = pltpu.roll(own_east, (-far) % LANES, 1)
            begin = pltpu.roll(own_west, (LANES - 1 - near) % LANES, 1)
            from_w = pltpu.roll(from_west, (-far) % LANES, 1)
            from_e = pltpu.roll(from_east, (LANES - 1 - near) % LANES, 1)
            force_first = fp[rows, first] - jnp.where(west_edge, (0.5 * mask_first) * from_w, 0.0)
            force_last = fp[rows, last] + jnp.where(east_edge, (0.5 * mask_last) * from_e, 0.0)
            change = jnp.where(west_edge, -tail, jnp.where(east_edge, begin, 0.0))
            force_outer = new_f + 0.5 * mask_outer * change
            inverse_first = mask_first * (1.0 / center_first)
            inverse_last = mask_last * (1.0 / center_last)
            inverse_outer = jnp.where(mask_outer > 0.0, 1.0 / jnp.where(center_outer > 0.0, center_outer, 1.0), 0.0)
            inv[rows, first] = inverse_first
            inv[rows, last] = inverse_last
            inv[rows, outer] = inverse_outer
            c0[rows, first] = force_first * inverse_first
            c0[rows, last] = force_last * inverse_last
            c0[rows, outer] = force_outer * inverse_outer
        return tuple(before)

    zero = jnp.zeros((ROWS, LANES), F32)
    lax.fori_loop(0, groups // 4, widen, (zero,) * 7)


def group_rows(g):
    return pl.ds(g * ROWS if isinstance(g, int) else pl.multiple_of(g * ROWS, ROWS), ROWS)


def sides_of(source, g, width):
    value = source[group_rows(g)]
    return left(value)[:, :width], right(value)[:, :width]


def terms(rings, source, g, width, turned):
    ax, ay, bly, nx, nxy, nxm, lxy, rxm = rings
    rows, cols = group_rows(g), pl.ds(0, width)
    west, east = turned
    here = source[rows, cols]
    same = ay[rows, cols] * east + bly[rows, cols] * west
    after = ax[rows, cols] * here + lxy[rows, cols] * west + rxm[rows, cols] * east
    before = nx[rows, cols] * here + nxy[rows, cols] * east + nxm[rows, cols] * west
    return same, down(after), pltpu.roll(before, ROWS - 1, 0)


def sweep(rings, source, start, count, width, finish):
    period = source.shape[0] // ROWS
    at = lambda n: n % period
    ahead, turned, following = [sides_of(source, at(start + d), width) for d in (-1, 0, 1)]
    _, ring_after, _ = terms(rings, source, at(start - 1), width, ahead)
    same, after, own_first = terms(rings, source, at(start), width, turned)
    tail = row_of((ROWS, width)) == ROWS - 1

    def advance(g, previous_group, next_group, carry):
        partial, own, previous, turned = carry
        following = sides_of(source, next_group, width)
        same, after, later = terms(rings, source, g, width, turned)
        finish(previous_group, partial + jnp.where(tail, later, own))
        return same + shifted_rows(previous, after), later, after, following

    carry = (same + shifted_rows(ring_after, after), own_first, after, following)
    if start + count <= period:
        body = lambda g, carry: advance(g, g - 1, jnp.minimum(g + 1, period - 1), carry)
        carry = lax.fori_loop(start + 1, start + count, body, carry, unroll=UNROLL)
    else:
        for n in range(start + 1, start + count):
            carry = advance(at(n), at(n - 1), at(n + 1), carry)
    partial, own, _, turned = carry
    if count == period:
        later = own_first
    else:
        later = terms(rings, source, at(start + count), width, turned)[2]
    finish(at(start + count - 1), partial + jnp.where(tail, later, own))


def step(rings, inv, source, target, start, count, subtract):
    def finish(g, total):
        rows = group_rows(g)
        moved = inv[rows] * total
        target[rows] = source[rows] - moved if subtract else moved

    sweep(rings, source, start, count, source.shape[1], finish)


def early_kernel(ax, ay, bly, nx, nxy, nxm, lxy, rxm, inv, c0, c1, c2):
    groups = c0.shape[0] // ROWS - 1
    rings = (ax, ay, bly, nx, nxy, nxm, lxy, rxm)
    step(rings, inv, c0, c1, 2, groups - 4, True)
    step(rings, inv, c1, c2, 3, groups - 6, False)


def basis_kernel(
    masks, outer_center, edges, send_a, send_b, recv_a, recv_b, rows_a, rows_b,
    ax_in, ay_in, bly_in, nx_in, nxy_in, nxm_in, lxy_in, rxm_in, inv_in, c0_in, center_in, c1_in, c2_in,
    c3, c4, gram_ref, ax, ay, bly, nx, nxy, nxm, lxy, rxm, inv, c0, center, c1, c2,
):
    row_count, col_count = center.shape
    tiles = col_count // LANES
    wide = col_count + LANES
    block_rows = row_count // BLOCK
    groups = row_count // ROWS
    blk, sub = own_place()
    even_sub, even_blk = (sub % 2) == 0, (blk % 2) == 0
    row8, lane8 = row_of((ROWS, wide)), lane_of((ROWS, wide))
    row1, lane1 = row_of((ROWS, LANES)), lane_of((ROWS, LANES))
    first, last, outer = pl.ds(0, LANES), pl.ds(col_count - LANES, LANES), pl.ds(col_count, LANES)
    west_edge, east_edge = lane1 == 0, lane1 == LANES - 1

    def at(g):
        return pl.ds(pl.multiple_of(g * ROWS, ROWS), ROWS)

    pieces = []
    for pair in range(3):
        rows = slice(pair * ROWS, (pair + 1) * ROWS)
        below = jnp.where(even_blk, rows_a[rows], rows_b[rows])
        above = jnp.where(even_blk, rows_b[rows], rows_a[rows])
        pieces.append(jnp.where(row8 < 4, below, pltpu.roll(above, 4, 0)))
        pieces.append(jnp.where(row8 < 4, pltpu.roll(below, 4, 0), above))
    out_f, out_x, out_y, out_xy, out_xm, out_c = pieces
    flux_below, flux_above = out_x[3:4], out_y[4:5]

    def edge_group(side, k):
        strip = 0 if side == 0 else groups // 4 - 1
        sides = side_tiles(send_a, send_b, recv_a, recv_b, even_sub, at(strip))
        get = lambda f: edges[pl.ds((side * 7 + f) * ROWS, ROWS)]
        full = [
            jnp.concatenate([get(e), outer_tile(sides[2], sides[3], f, k)], axis=1)
            for e, f in ((1, 1), (3, 3), (4, 4), (6, 7))
        ]
        mask = masks[mask_group(0 if side == 0 else block_rows - 1)]
        return full, mask, force_with_sides(get(0), mask, sides, k)

    (_, _, _, flux_first), mask_first, force_first = edge_group(0, 0)
    (x_last, xy_last, xm_last, flux_last), mask_last, force_last = edge_group(1, 3)
    mask_below, mask_above = masks[mask_group(block_rows)], masks[mask_group(block_rows + 1)]

    def inverse_of(mask, total):
        return jnp.where(mask > 0.0, 1.0 / jnp.where(total > 0.0, total, 1.0), 0.0)

    head = row8 == 0
    own_first = pl.ds(0, ROWS)
    up = []
    for ring, out in ((nx, out_x), (nxy, out_xy), (nxm, out_xm)):
        moved = jnp.where(head, down(out), ring[own_first])
        ring[own_first] = moved
        up.append(moved)
    total = jnp.concatenate([center[own_first], outer_center[own_first]], axis=1)
    total = total + jnp.where(head, up[0] + left(up[1]) + right(up[2]), 0.0)
    center[own_first] = total[:, :col_count]
    inverse = inverse_of(mask_first, total)
    inv[own_first] = inverse
    c0[own_first] = inverse * (force_first - jnp.where(head, 0.5 * mask_first * flux_above, 0.0))
    own_last = pl.ds(row_count - ROWS, ROWS)
    c0[own_last] = inv[own_last] * (
        force_last + jnp.where(row8 == ROWS - 1, 0.5 * mask_last * flux_below, 0.0)
    )
    ring_rows = pl.ds(row_count, ROWS)
    up = [
        jnp.where(head, down(before), down(out))
        for before, out in ((x_last, out_x), (xy_last, out_xy), (xm_last, out_xm))
    ]
    left_y = left(out_y)
    for ring, value in (
        (ax, out_x), (ay, out_y), (bly, left_y), (nx, up[0]), (nxy, up[1]), (nxm, up[2]),
        (lxy, left(out_xy)), (rxm, right(out_xm)),
    ):
        ring[ring_rows] = value
    crosses_west = (row8 != 4) & ((lane8 == 0) | (lane8 == col_count))
    crosses_east = (row8 != 4) & ((lane8 == col_count - 1) | (lane8 == wide - 1))
    total = out_c + jnp.where(head, up[0], 0.0)
    total = total + jnp.where(crosses_west, left_y, 0.0)
    total = total + jnp.where(head | crosses_west, left(up[1]), 0.0)
    total = total + jnp.where(head | crosses_east, right(up[2]), 0.0)
    inverse = inverse_of(jnp.where(row8 < 4, mask_below, mask_above), total)
    out_f = out_f - jnp.where(head, 0.5 * mask_below * flux_last[ROWS - 1 : ROWS], 0.0)
    out_f = out_f + jnp.where(row8 == ROWS - 1, 0.5 * mask_above * flux_first[0:1], 0.0)
    inv[ring_rows] = inverse
    c0[ring_rows] = inverse * out_f

    rings = (ax, ay, bly, nx, nxy, nxm, lxy, rxm)
    step(rings, inv, c0, c1, groups - 2, 5, True)
    step(rings, inv, c1, c2, groups - 3, 7, False)
    step(rings, inv, c2, c3, 0, groups + 1, False)

    cols = pl.ds(0, col_count)

    def last_finish(g, total):
        c4[at(g)] = inv[at(g), cols] * total

    sweep(rings, c3, 0, groups, col_count, last_finish)

    def add_products(g, sums):
        rows = at(g)
        basis = [ref[rows, cols] for ref in (c0, c1, c2, c3)] + [c4[rows]]
        weight = center[rows]
        weighted = [weight * b for b in basis]
        new = []
        for (i, j), total in zip(PAIRS, sums):
            product = basis[i] * weighted[j]
            part = product[:, :LANES]
            for t in range(1, tiles):
                part = part + product[:, t * LANES : (t + 1) * LANES]
            new.append(total + part)
        return tuple(new)

    zero = jnp.zeros((ROWS, LANES), F32)
    sums = lax.fori_loop(0, groups, add_products, tuple(zero for _ in PAIRS), unroll=2)

    count = len(PAIRS)
    high = jnp.zeros((2 * ROWS, LANES), F32)
    low = high
    place = row_of((2 * ROWS, LANES))
    for index, total in enumerate(sums):
        error = jnp.zeros_like(total)
        for shift in (4, 2, 1):
            total, rounding = two_sum(total, pltpu.roll(total, shift, 0))
            error = error + pltpu.roll(error, shift, 0) + rounding
        high = jnp.where(place == index, total[0:1], high)
        low = jnp.where(place == index, error[0:1], low)
    for shift in (64, 32, 16, 8, 4, 2, 1):
        high, rounding = two_sum(high, pltpu.roll(high, shift, 1))
        low = low + pltpu.roll(low, shift, 1) + rounding
    lane2 = lane_of((2 * ROWS, LANES))
    packed = jnp.where(lane2 == place, high, jnp.where(lane2 == place + LANES // 2, low, 0.0))
    gram_ref[...] = jnp.broadcast_to(jnp.sum(packed, axis=0, keepdims=True), gram_ref.shape)


def finish_kernel(gram_ref, c0, c1, c2, c3, c4, center_ref, height_out, residual_out, height_ref, residual_ref, sems):
    lane1 = lane_of((1, LANES))
    high = gram_ref[...]
    low = jnp.zeros_like(high)
    while high.shape[0] > 1:
        half = high.shape[0] // 2
        high, rounding = two_sum(high[:half], high[half:])
        low = low[:half] + low[half:] + rounding
    entries = high + (low + pltpu.roll(high, LANES // 2, 1))
    size = ITERS + 1
    gram = {}
    for index, (i, j) in enumerate(PAIRS):
        entry = jnp.sum(jnp.where(lane1 == index, entries, 0.0), axis=1, keepdims=True)
        gram[i, j] = entry
        gram[j, i] = entry
    zero = jnp.zeros((1, 1), F32)
    one = jnp.ones((1, 1), F32)

    def image(coefs):
        result = [zero, coefs[0] + coefs[1]]
        for j in range(2, size):
            own = coefs[j] if j < size - 1 else zero
            result.append(own - coefs[j - 1])
        return result

    def form(one_side, products):
        total = zero
        for a, b in zip(one_side, products):
            total = total + a * b
        return total

    scaled = [one] + [zero] * (size - 1)
    search = [zero] * size
    height = [zero] * size
    rho_old, sigma = one, zero
    for iteration in range(ITERS):
        limit = iteration + 1
        products = []
        for j in range(size):
            total = zero
            for i in range(limit):
                total = total + scaled[i] * gram[i, j]
            products.append(total)
        rho = form(scaled[:limit], products)
        curvature = form(image(scaled)[: limit + 1], products)
        beta = rho / rho_old
        sigma = curvature - beta * beta * sigma
        alpha = rho / sigma
        rho_old = rho
        search = [s + beta * q for s, q in zip(scaled, search)]
        height = [h + alpha * q for h, q in zip(height, search)]
        scaled = [s - alpha * q for s, q in zip(scaled, image(search))]

    def combine(g, _):
        rows = pl.ds(pl.multiple_of(g * ROWS, ROWS), ROWS)
        cols = pl.ds(0, center_ref.shape[1])
        basis = [ref[rows, cols] for ref in (c0, c1, c2, c3, c4)]
        total = height[0] * basis[0]
        for j in range(1, size - 1):
            total = total + height[j] * basis[j]
        height_ref[rows] = total
        total = scaled[0] * basis[0]
        for j in range(1, size):
            total = total + scaled[j] * basis[j]
        residual_ref[rows] = center_ref[rows] * total
        return 0

    row_count = center_ref.shape[0]
    part = row_count // PARTS
    copies = []
    for p in range(PARTS):
        lax.fori_loop(p * part // ROWS, (p + 1) * part // ROWS, combine, 0, unroll=4)
        rows = pl.ds(p * part, part)
        for i, (src, dst) in enumerate(((height_ref, height_out), (residual_ref, residual_out))):
            copies.append(pltpu.make_async_copy(src.at[rows], dst.at[rows], sems.at[i, p]))
            copies[-1].start()
    for copy in copies:
        copy.wait()


def swap(value, axis, parity):
    peers = lax.axis_size(axis)
    pairs = []
    for i in range(parity, peers - 1, 2):
        pairs += [(i, i + 1), (i + 1, i)]
    return lax.ppermute(value, axis, pairs)


def body(u_flow, v_flow, thickness, depth_levels, block_ocean, coef_x, coef_y, coef_xy, coef_xm, extra_diagonal):
    levels, row_count, col_count = u_flow.shape
    wide = col_count + LANES
    shape = lambda *dims: pltpu.VMEM(dims, F32)
    final = jax.ShapeDtypeStruct((row_count, col_count), F32)
    far = lambda array: pltpu.with_memory_space_constraint(array, pltpu.HBM)
    plane = shape(row_count, col_count)
    ring = shape(row_count + ROWS, wide)
    strip = shape(row_count // 4, LANES)
    flow = pltpu.VMEM((levels, row_count, col_count), F32)
    field = pltpu.VMEM((row_count, col_count), F32)
    fp, cp, edges, send_a, send_b, *rings, masks = pl.pallas_call(
        flux_kernel,
        out_shape=(plane, plane, shape(14 * ROWS, col_count), strip, strip)
        + (ring,) * 4
        + (shape((row_count // BLOCK + 2) * ROWS, wide),),
        in_specs=[HBM] * 10,
        out_specs=(VMEM,) * 10,
        scratch_shapes=[flow, flow, pltpu.VMEM((row_count, col_count), jnp.int32)]
        + [field] * 3
        + [pltpu.SMEM(thickness.shape, F32), pltpu.SMEM(block_ocean.shape, jnp.int32)]
        + [pltpu.SemaphoreType.DMA((2, row_count // PIECE)), pltpu.SemaphoreType.DMA((6,)), pltpu.SemaphoreType.DMA((2,))],
        compiler_params=pltpu.CompilerParams(vmem_limit_bytes=FLUX_LIMIT),
        name="flux",
    )(
        *[far(a) for a in (thickness, block_ocean, u_flow, v_flow, depth_levels, coef_x, coef_y, coef_xy, coef_xm, extra_diagonal)],
    )
    recv_a, recv_b = swap(send_a, "sub", 0), swap(send_b, "sub", 1)
    ax, ay, axy, axm = rings
    *moved, inv, c0 = pl.pallas_call(
        prepare_kernel,
        out_shape=(ring,) * 8,
        in_specs=[VMEM] * 7,
        out_specs=(VMEM,) * 8,
        compiler_params=pltpu.CompilerParams(vmem_limit_bytes=8 << 20),
        cost_estimate=pl.CostEstimate(flops=10 << 20, bytes_accessed=4 << 20, transcendentals=0),
        name="prepare",
    )(fp, cp, masks, ax, ay, axy, axm)
    edge = shape(3 * ROWS, wide)
    edge_a, edge_b = pl.pallas_call(
        functools.partial(edge_kernel, row_count=row_count),
        out_shape=(edge, edge),
        in_specs=[VMEM] * 7,
        out_specs=(VMEM,) * 2,
        compiler_params=pltpu.CompilerParams(vmem_limit_bytes=8 << 20),
        name="edge",
    )(masks, edges, send_a, send_b, recv_a, recv_b, moved[0])
    rows_a, rows_b = swap(edge_a, "blk", 0), swap(edge_b, "blk", 1)
    outer_center, *rings = pl.pallas_call(
        widen_kernel,
        out_shape=(shape(row_count, LANES),) + (ring,) * 10 + (plane,),
        in_specs=[VMEM] * 17,
        out_specs=(VMEM,) * 12,
        input_output_aliases={6 + i: 1 + i for i in range(11)},
        compiler_params=pltpu.CompilerParams(vmem_limit_bytes=8 << 20),
        cost_estimate=pl.CostEstimate(flops=10 << 20, bytes_accessed=4 << 20, transcendentals=0),
        name="widen",
    )(masks, fp, send_a, send_b, recv_a, recv_b, ax, ay, *moved, inv, c0, cp)
    devices = lax.axis_size("blk") * lax.axis_size("sub")
    early = pl.pallas_call(
        early_kernel,
        out_shape=(ring, ring),
        in_specs=[VMEM] * 10,
        out_specs=(VMEM,) * 2,
        compiler_params=pltpu.CompilerParams(vmem_limit_bytes=8 << 20),
        cost_estimate=pl.CostEstimate(flops=10 << 20, bytes_accessed=4 << 20, transcendentals=0),
        name="early",
    )(*rings[:10])
    c3, c4, gram, *rest = pl.pallas_call(
        basis_kernel,
        out_shape=(ring, plane, shape(devices, LANES)) + (ring,) * 10 + (plane, ring, ring),
        in_specs=[VMEM] * 22,
        out_specs=(VMEM,) * 16,
        input_output_aliases={9 + i: 3 + i for i in range(13)},
        compiler_params=pltpu.CompilerParams(vmem_limit_bytes=8 << 20),
        name="basis",
    )(masks, outer_center, edges, send_a, send_b, recv_a, recv_b, rows_a, rows_b, *rings, *early)
    c0, center, c1, c2 = rest[-4:]
    gram = lax.all_to_all(gram, ("blk", "sub"), 0, 0, tiled=True)
    return pl.pallas_call(
        finish_kernel,
        out_shape=(final, final),
        in_specs=[VMEM] * 7,
        out_specs=(HBM,) * 2,
        scratch_shapes=[field, field, pltpu.SemaphoreType.DMA((2, PARTS))],
        compiler_params=pltpu.CompilerParams(vmem_limit_bytes=8 << 20),
        name="finish",
    )(gram, c0, c1, c2, c3, c4, center)


def solution(mesh):
    placed = (
        P(None, "blk", "sub"),
        P(None, "blk", "sub"),
        P(),
        P("blk", "sub"),
        P(),
        P("blk", "sub"),
        P("blk", "sub"),
        P("blk", "sub"),
        P("blk", "sub"),
        P("blk", "sub"),
    )
    return jax.shard_map(
        body,
        mesh=mesh,
        in_specs=placed,
        out_specs=(P("blk", "sub"), P("blk", "sub")),
        check_vma=False,
    )
```

```python
import functools

import jax
import jax.numpy as jnp
from jax import lax
from jax.experimental import pallas as pl
from jax.experimental.pallas import tpu as pltpu
from jax.sharding import PartitionSpec as P

BLOCK = 128
ITERS = 4
HALO = ITERS
LANES = 128
ROWS = 8
CHUNK = 32
PIECE = 16
AHEAD = 6
UNROLL = 8
PARTS = 4
F32 = jnp.float32
FLUX_LIMIT = 40 << 20
VMEM = pl.BlockSpec(memory_space=pltpu.VMEM)
HBM = pl.BlockSpec(memory_space=pltpu.HBM)
PAIRS = [(i, j) for i in range(ITERS) for j in range(i, ITERS + 1)]


def lane_of(shape):
    return lax.broadcasted_iota(jnp.int32, shape, len(shape) - 1)


def row_of(shape):
    return lax.broadcasted_iota(jnp.int32, shape, len(shape) - 2)


def shifted_rows(before, here):
    return jnp.where(row_of(here.shape) == 0, before, here)


def left(value):
    return pltpu.roll(value, 1, 1)


def right(value):
    return pltpu.roll(value, value.shape[1] - 1, 1)


def down(value):
    return pltpu.roll(value, 1, 0)


def two_sum(a, b):
    total = a + b
    other = total - a
    return total, (a - (total - other)) + (b - other)


def ocean_at(ocean_ref, row, col):
    block_rows, block_cols = ocean_ref.shape
    inside = (row >= 0) & (row < block_rows) & (col >= 0) & (col < block_cols)
    entry = ocean_ref[jnp.clip(row, 0, block_rows - 1), jnp.clip(col, 0, block_cols - 1)]
    return jnp.where(inside & (entry == 1), 1.0, 0.0).astype(F32)


def flux_kernel(
    thick_hbm, ocean_hbm, u_hbm, v_hbm, depth_hbm, cx_hbm, cy_hbm, cxy_hbm, cxm_hbm, ex_hbm,
    fu, fv, ex, edge_ref, pack_a, pack_b, ax, ay, axy, axm, masks,
    u_buf, v_buf, depth, thick, ocean, sems, coef_sem, small_sem,
):
    levels, row_count, col_count = u_buf.shape
    tiles = col_count // LANES
    chunks = row_count // CHUNK
    pieces = row_count // PIECE
    groups = row_count // ROWS
    steps = CHUNK // ROWS
    blk, sub = own_place()
    block_rows = row_count // BLOCK
    own = (pl.ds(0, row_count), pl.ds(0, col_count))
    coef_copies = [
        pltpu.make_async_copy(src, dst, coef_sem.at[i])
        for i, (src, dst) in enumerate(
            [
                (depth_hbm, depth), (ex_hbm, ex), (cx_hbm, ax.at[own]), (cy_hbm, ay.at[own]),
                (cxy_hbm, axy.at[own]), (cxm_hbm, axm.at[own]),
            ]
        )
    ]

    def flow_copies(c):
        rows = pl.ds(pl.multiple_of(c * PIECE, PIECE), PIECE)
        return (
            pltpu.make_async_copy(u_hbm.at[:, rows, :], u_buf.at[:, rows, :], sems.at[0, c]),
            pltpu.make_async_copy(v_hbm.at[:, rows, :], v_buf.at[:, rows, :], sems.at[1, c]),
        )

    small_copies = [
        pltpu.make_async_copy(src, dst, small_sem.at[i])
        for i, (src, dst) in enumerate([(thick_hbm, thick), (ocean_hbm, ocean)])
    ]
    for copy in small_copies:
        copy.start()
    coef_copies[0].start()
    for copy in flow_copies(0):
        copy.start()
    for copy in coef_copies[1:]:
        copy.start()
    for c in range(1, AHEAD):
        for copy in flow_copies(c):
            copy.start()
    for copy in small_copies:
        copy.wait()
    for place in range(block_rows + 2):
        block_row = blk * block_rows + (place if place <= block_rows else -1)
        masks[mask_group(place)] = jnp.broadcast_to(
            mask_row(ocean, block_row, sub, tiles), (ROWS, col_count + LANES)
        )
    coef_copies[0].wait()

    row8 = row_of((ROWS, 2 * LANES))
    lane8 = lane_of((ROWS, 2 * LANES))
    lane1 = lane_of((ROWS, LANES))
    first, final = pl.ds(0, LANES), pl.ds(col_count - LANES, LANES)
    even = (sub % 2) == 0

    def ends(ref, rows):
        return jnp.concatenate([ref[rows, first], ref[rows, final]], axis=1)

    def at(g):
        return pl.ds(pl.multiple_of(g * ROWS, ROWS), ROWS)

    def west_of(value):
        return jnp.where(lane8 == 0, 0.0, left(value))

    def east_of(value):
        return jnp.where(lane8 == 2 * LANES - 1, 0.0, right(value))

    def rolled_fields(rows):
        return [
            down(v) for v in (ends(ax, rows), west_of(ends(axy, rows)), east_of(ends(axm, rows)), ends(fu, rows))
        ]

    def sum_group(g):
        rows = at(g)
        for t in range(tiles):
            lanes = pl.ds(t * LANES, LANES)
            mask = masks[mask_group(g * ROWS // BLOCK), lanes]
            deep = depth[rows, lanes]
            total_u = jnp.zeros((ROWS, LANES), F32)
            total_v = total_u
            for k in range(levels):
                active = jnp.where(deep > k, thick[k], 0.0)
                total_u = total_u + active * u_buf[k, rows, lanes]
                total_v = total_v + active * v_buf[k, rows, lanes]
            fu[rows, lanes] = mask * total_u
            fv[rows, lanes] = mask * total_v

    def group_work(g, k, before):
        rows = at(g)
        here_x, here_y, here_xy, here_xm, here_u, here_v = [ends(ref, rows) for ref in (ax, ay, axy, axm, fu, fv)]
        west_xy, east_xm, west_y = west_of(here_xy), east_of(here_xm), west_of(here_y)
        rolled = [down(v) for v in (here_x, west_xy, east_xm, here_u)]
        up_x, up_west, up_east, up_u = [shifted_rows(a, b) for a, b in zip(before, rolled)]
        total = ends(ex, rows) + here_x
        total = total + up_x
        total = total + here_y
        total = total + west_y
        total = total + here_xy
        total = total + up_west
        total = total + here_xm
        total = total + up_east
        after = ends(fu, at(jnp.minimum(g + 1, groups - 1)))
        after = jnp.where(g + 1 < groups, pltpu.roll(after, ROWS - 1, 0), 0.0)
        below = jnp.where(row8 == ROWS - 1, after, pltpu.roll(here_u, ROWS - 1, 0))
        change = 0.5 * ((below - up_u) + (east_of(here_v) - west_of(here_v)))
        mask = ends(masks, mask_group(g * ROWS // BLOCK))
        partial = mask * change
        fields = [partial, here_x, here_y, here_xy, here_xm, total, here_v, here_u]
        to_west = jnp.zeros((ROWS, LANES), F32)
        to_east = to_west
        for f, field in enumerate(fields):
            lane = 4 * f + 32 * k
            chosen = (lane1 >= lane) & (lane1 < lane + HALO)
            to_west = jnp.where(chosen, pltpu.roll(field[:, :LANES], lane, 1), to_west)
            to_east = jnp.where(chosen, pltpu.roll(field[:, -LANES:], (lane + HALO) % LANES, 1), to_east)
        lane = 4 * 6 + 32 * k
        extra = pltpu.roll(here_xm[:, :LANES], (lane + 1 - HALO) % LANES, 1)
        to_west = jnp.where(lane1 == lane + 1, extra, to_west)
        extra = pltpu.roll(here_xy[:, -LANES:], (lane + HALO + 1) % LANES, 1)
        to_east = jnp.where(lane1 == lane, extra, to_east)
        packed = at(g // 4)
        for_a = jnp.where(even, to_east, to_west)
        for_b = jnp.where(even, to_west, to_east)
        if k == 0:
            pack_a[packed] = for_a
            pack_b[packed] = for_b
        else:
            pack_a[packed] = pack_a[packed] + for_a
            pack_b[packed] = pack_b[packed] + for_b
        return rolled

    def work_from(g, k):
        before = rolled_fields(at(jnp.maximum(g - 1, 0)))
        return group_work(g, k, [jnp.where(g > 0, b, 0.0) for b in before])

    def chunk(c, _):
        def piece(i, _):
            p = c * (CHUNK // PIECE) + i
            for copy in flow_copies(p):
                copy.wait()

            @pl.when(p + AHEAD < pieces)
            def _():
                for copy in flow_copies(p + AHEAD):
                    copy.start()

            for j in range(PIECE // ROWS):
                sum_group(p * (PIECE // ROWS) + j)
            return 0

        lax.fori_loop(0, CHUNK // PIECE, piece, 0)

        @pl.when(c == 0)
        def _():
            for copy in coef_copies[1:]:
                copy.wait()

        @pl.when(c > 0)
        def _():
            work_from(c * steps - 1, 3)

        carry = work_from(c * steps, 0)
        for k in range(1, steps - 1):
            carry = group_work(c * steps + k, k, carry)
        return 0

    lax.fori_loop(0, chunks, chunk, 0)
    work_from(groups - 1, 3)
    for side, base in enumerate((0, row_count - ROWS)):
        rows = pl.ds(base, ROWS)
        for f, field in enumerate(
            [ax[rows, own[1]], ay[rows, own[1]], axy[rows, own[1]], axm[rows, own[1]], fu[rows]]
        ):
            edge_ref[pl.ds((side * 5 + f) * ROWS, ROWS)] = field


def side_tiles(send_a, send_b, recv_a, recv_b, even, packed):
    own_a, own_b, got_a, got_b = send_a[packed], send_b[packed], recv_a[packed], recv_b[packed]
    pick = lambda a, b: jnp.where(even, a, b)
    return pick(own_b, own_a), pick(own_a, own_b), pick(got_b, got_a), pick(got_a, got_b)


def outer_tile(from_west, from_east, f, k):
    lane1 = lane_of(from_west.shape)
    at = 4 * f + 32 * k
    east = pltpu.roll(from_east, (-at) % LANES, 1)
    west = pltpu.roll(from_west, (LANES - HALO - at) % LANES, 1)
    tile = jnp.where(lane1 < HALO, east, jnp.where(lane1 >= LANES - HALO, west, 0.0))
    if f == 3:
        extra = pltpu.roll(from_west, (LANES - HALO - 1 - 4 * 6 - 32 * k) % LANES, 1)
        tile = jnp.where(lane1 == LANES - HALO - 1, extra, tile)
    if f == 4:
        extra = pltpu.roll(from_east, (HALO - 4 * 6 - 1 - 32 * k) % LANES, 1)
        tile = jnp.where(lane1 == HALO, extra, tile)
    return tile


def force_with_sides(partial, mask, sides, k):
    own_west, own_east, from_west, from_east = sides
    lane1 = lane_of(own_west.shape)
    first, last = 4 * 6 + 32 * k, 4 * 6 + 3 + 32 * k
    outer = outer_tile(from_west, from_east, 0, k)
    tail = pltpu.roll(own_east, (-last) % LANES, 1)
    head = pltpu.roll(own_west, (LANES - 1 - first) % LANES, 1)
    change = jnp.where(lane1 == 0, -tail, jnp.where(lane1 == LANES - 1, head, 0.0))
    outer = outer + 0.5 * mask[:, -LANES:] * change
    begin = partial[:, :LANES] - jnp.where(
        lane1 == 0, 0.5 * mask[:, :LANES] * pltpu.roll(from_west, (-last) % LANES, 1), 0.0
    )
    middle = partial[:, LANES:-LANES]
    end = partial[:, -LANES:] + jnp.where(
        lane1 == LANES - 1,
        0.5 * mask[:, -2 * LANES : -LANES] * pltpu.roll(from_east, (LANES - 1 - first) % LANES, 1),
        0.0,
    )
    return jnp.concatenate([begin, middle, end, outer], axis=1)


def own_place():
    return lax.axis_index("blk"), lax.axis_index("sub")


def mask_group(block):
    if isinstance(block, int):
        return pl.ds(block * ROWS, ROWS)
    return pl.ds(pl.multiple_of(block * ROWS, ROWS), ROWS)


def mask_row(ocean, block_row, sub, tiles):
    lane1 = lane_of((1, LANES))
    parts = [jnp.full((1, LANES), ocean_at(ocean, block_row, sub * tiles + t), F32) for t in range(tiles)]
    east = ocean_at(ocean, block_row, (sub + 1) * tiles)
    west = ocean_at(ocean, block_row, sub * tiles - 1)
    parts.append(jnp.where(lane1 < LANES // 2, east, west))
    return jnp.concatenate(parts, axis=1)


def edge_kernel(masks, edges, made, send_a, send_b, recv_a, recv_b, rows_a, rows_b, *, row_count):
    col_count = edges.shape[1]
    tiles = col_count // LANES
    block_rows = row_count // BLOCK
    blk, sub = own_place()
    even_sub, even_blk = (sub % 2) == 0, (blk % 2) == 0
    shape = (ROWS, col_count + LANES)
    row8, lane8 = row_of(shape), lane_of(shape)
    crosses_west = (lane8 == 0) | (lane8 == col_count)
    crosses_east = (lane8 == col_count - 1) | (lane8 == col_count + LANES - 1)
    strips = row_count // (4 * ROWS)
    results = []
    for side, top in enumerate((True, False)):
        k = 0 if top else 3
        packed = pl.ds(0 if top else (strips - 1) * ROWS, ROWS)
        rows = [edges[pl.ds((side * 5 + f) * ROWS, ROWS)] for f in range(5)]
        rows = [made[pl.ds(2 * side * ROWS, ROWS)], *rows[:4], made[pl.ds((2 * side + 1) * ROWS, ROWS)], rows[4]]
        sides = side_tiles(send_a, send_b, recv_a, recv_b, even_sub, packed)
        mask = masks[mask_group(0 if top else block_rows - 1)]
        fields = [force_with_sides(rows[0], mask, sides, k)]
        for f in range(1, 6):
            fields.append(jnp.concatenate([rows[f], outer_tile(sides[2], sides[3], f, k)], axis=1))
        flux = jnp.concatenate([rows[6], outer_tile(sides[2], sides[3], 7, k)], axis=1)
        if top:
            fields[1] = jnp.where(row8 == 3, pltpu.roll(flux, 3, 0), fields[1])
            half = lambda v: v
        else:
            extra = jnp.where(crosses_west, left(fields[2]) + left(down(fields[3])), 0.0)
            extra = extra + jnp.where(crosses_east, right(down(fields[4])), 0.0)
            fields[5] = fields[5] + jnp.where(row8 == 4, extra, 0.0)
            fields[2] = jnp.where(row8 == 4, pltpu.roll(flux, 5, 0), fields[2])
            half = lambda v: pltpu.roll(v, 4, 0)
        pieces = []
        for pair in range(3):
            one, two = half(fields[2 * pair]), half(fields[2 * pair + 1])
            pieces.append(jnp.where(row8 < 4, one, pltpu.roll(two, 4, 0)))
        results.append(pieces)
    for pair in range(3):
        rows = slice(pair * ROWS, (pair + 1) * ROWS)
        rows_a[rows] = jnp.where(even_blk, results[1][pair], results[0][pair])
        rows_b[rows] = jnp.where(even_blk, results[0][pair], results[1][pair])


def prepare_kernel(
    fu, fv, ex, masks, ax, ay, axy, axm,
    fp, cp, edge_ref, bly, nx, nxy, nxm, lxy, rxm, inv, c0,
):
    row_count, col_count = fp.shape
    groups = row_count // ROWS
    cols = pl.ds(0, col_count)
    row8, lane8 = row_of((ROWS, col_count)), lane_of((ROWS, col_count))
    begin, end = lane8 == 0, lane8 == col_count - 1
    head, tail = row8 == 0, row8 == ROWS - 1

    def body(g, before):
        rows = group_rows(g)
        here_x, here_y, here_xy, here_xm = [ref[rows, cols] for ref in (ax, ay, axy, axm)]
        here_u, here_v = fu[rows], fv[rows]
        west_y = jnp.where(begin, 0.0, left(here_y))
        west_xy = jnp.where(begin, 0.0, left(here_xy))
        east_xm = jnp.where(end, 0.0, right(here_xm))
        rolled = tuple(down(v) for v in (here_x, here_xy, here_xm, west_xy, east_xm, here_u))
        up_x, up_xy, up_xm, up_west, up_east, up_u = [jnp.where(head, a, b) for a, b in zip(before, rolled)]
        total = ex[rows] + here_x
        total = total + up_x
        total = total + here_y
        total = total + west_y
        total = total + here_xy
        total = total + up_west
        total = total + here_xm
        total = total + up_east
        cp[rows] = total
        for ring, value in ((bly, west_y), (nx, up_x), (nxy, up_xy), (nxm, up_xm), (lxy, west_xy), (rxm, east_xm)):
            ring[rows, cols] = value
        after = pltpu.roll(fu[group_rows(jnp.minimum(g + 1, groups - 1))], ROWS - 1, 0)
        below = jnp.where(tail, jnp.where(g + 1 < groups, after, 0.0), pltpu.roll(here_u, ROWS - 1, 0))
        across = jnp.where(end, 0.0, right(here_v)) - jnp.where(begin, 0.0, left(here_v))
        mask = masks[mask_group(g * ROWS // BLOCK), cols]
        partial = mask * (0.5 * ((below - up_u) + across))
        fp[rows] = partial
        inverse = mask * (1.0 / total)
        inv[rows, cols] = inverse
        c0[rows, cols] = partial * inverse
        return rolled

    zero = jnp.zeros((ROWS, col_count), F32)
    lax.fori_loop(0, groups, body, (zero,) * 6, unroll=4)
    for side, base in enumerate((0, row_count - ROWS)):
        rows = pl.ds(base, ROWS)
        edge_ref[pl.ds(2 * side * ROWS, ROWS)] = fp[rows]
        edge_ref[pl.ds((2 * side + 1) * ROWS, ROWS)] = cp[rows]


def widen_kernel(
    masks, fp, send_a, send_b, recv_a, recv_b,
    ax_in, ay_in, bly_in, nx_in, nxy_in, nxm_in, lxy_in, rxm_in, inv_in, c0_in, center_in,
    outer_center, ax, ay, bly, nx, nxy, nxm, lxy, rxm, inv, c0, center,
):
    row_count, col_count = fp.shape
    tiles = col_count // LANES
    block_rows = row_count // BLOCK
    groups = row_count // ROWS
    blk, sub = own_place()
    even_sub = (sub % 2) == 0
    lane1 = lane_of((ROWS, LANES))
    first, last, outer = pl.ds(0, LANES), pl.ds(col_count - LANES, LANES), pl.ds(col_count, LANES)
    west_edge, east_edge = lane1 == 0, lane1 == LANES - 1

    def at(g):
        return pl.ds(pl.multiple_of(g * ROWS, ROWS), ROWS)

    def widen(p, before):
        sides = side_tiles(send_a, send_b, recv_a, recv_b, even_sub, at(p))
        own_west, own_east, from_west, from_east = sides
        for k in range(4):
            g = 4 * p + k
            rows = at(g)
            new_f, new_x, new_y, new_xy, new_xm, new_c = [outer_tile(from_west, from_east, f, k) for f in range(6)]
            end_y = pltpu.roll(own_east, (-(4 * 2 + 3 + 32 * k)) % LANES, 1)
            end_xy = pltpu.roll(own_east, (-(4 * 3 + 3 + 32 * k)) % LANES, 1)
            begin_xm = pltpu.roll(own_west, (LANES - 1 - 4 * 4 - 32 * k) % LANES, 1)
            left_y, left_xy, right_xm = left(new_y), left(new_xy), right(new_xm)
            outer_y = jnp.where(west_edge, end_y, left_y)
            outer_xy = jnp.where(west_edge, end_xy, left_xy)
            outer_xm = jnp.where(east_edge, begin_xm, right_xm)
            rolled = [down(v) for v in (new_x, new_xy, new_xm, outer_xy, outer_xm, left_xy, right_xm)]
            up_x, up_xy, up_xm, up_outer_xy, up_outer_xm, up_left, up_right = [
                shifted_rows(a, b) for a, b in zip(before, rolled)
            ]
            before = rolled
            ax[rows, outer] = new_x
            ay[rows, outer] = new_y
            bly[rows, outer] = outer_y
            lxy[rows, outer] = outer_xy
            rxm[rows, outer] = outer_xm
            nx[rows, outer] = up_x
            nxy[rows, outer] = up_xy
            nxm[rows, outer] = up_xm
            bly[rows, first] = jnp.where(west_edge, left_y, bly[rows, first])
            lxy[rows, first] = jnp.where(west_edge, left_xy, lxy[rows, first])
            rxm[rows, last] = jnp.where(east_edge, right_xm, rxm[rows, last])
            center_first = center[rows, first] + jnp.where(west_edge, left_y + up_left, 0.0)
            center_last = center[rows, last] + jnp.where(east_edge, up_right, 0.0)
            center_outer = new_c + jnp.where(west_edge, outer_y + up_outer_xy, 0.0)
            center_outer = center_outer + jnp.where(east_edge, up_outer_xm, 0.0)
            center[rows, first] = center_first
            center[rows, last] = center_last
            outer_center[rows] = center_outer
            block = mask_group(g * ROWS // BLOCK)
            mask_first, mask_last, mask_outer = masks[block, first], masks[block, last], masks[block, outer]
            near, far = 4 * 6 + 32 * k, 4 * 6 + 3 + 32 * k
            tail = pltpu.roll(own_east, (-far) % LANES, 1)
            begin = pltpu.roll(own_west, (LANES - 1 - near) % LANES, 1)
            from_w = pltpu.roll(from_west, (-far) % LANES, 1)
            from_e = pltpu.roll(from_east, (LANES - 1 - near) % LANES, 1)
            force_first = fp[rows, first] - jnp.where(west_edge, (0.5 * mask_first) * from_w, 0.0)
            force_last = fp[rows, last] + jnp.where(east_edge, (0.5 * mask_last) * from_e, 0.0)
            change = jnp.where(west_edge, -tail, jnp.where(east_edge, begin, 0.0))
            force_outer = new_f + 0.5 * mask_outer * change
            inverse_first = mask_first * (1.0 / center_first)
            inverse_last = mask_last * (1.0 / center_last)
            inverse_outer = jnp.where(mask_outer > 0.0, 1.0 / jnp.where(center_outer > 0.0, center_outer, 1.0), 0.0)
            inv[rows, first] = inverse_first
            inv[rows, last] = inverse_last
            inv[rows, outer] = inverse_outer
            c0[rows, first] = force_first * inverse_first
            c0[rows, last] = force_last * inverse_last
            c0[rows, outer] = force_outer * inverse_outer
        return tuple(before)

    zero = jnp.zeros((ROWS, LANES), F32)
    lax.fori_loop(0, groups // 4, widen, (zero,) * 7)


def group_rows(g):
    return pl.ds(g * ROWS if isinstance(g, int) else pl.multiple_of(g * ROWS, ROWS), ROWS)


def sides_of(source, g, width):
    value = source[group_rows(g)]
    return left(value)[:, :width], right(value)[:, :width]


def terms(rings, source, g, width, turned):
    ax, ay, bly, nx, nxy, nxm, lxy, rxm = rings
    rows, cols = group_rows(g), pl.ds(0, width)
    west, east = turned
    here = source[rows, cols]
    same = ay[rows, cols] * east + bly[rows, cols] * west
    after = ax[rows, cols] * here + lxy[rows, cols] * west + rxm[rows, cols] * east
    before = nx[rows, cols] * here + nxy[rows, cols] * east + nxm[rows, cols] * west
    return same, down(after), pltpu.roll(before, ROWS - 1, 0)


def sweep(rings, source, start, count, width, finish):
    period = source.shape[0] // ROWS
    at = lambda n: n % period
    ahead, turned, following = [sides_of(source, at(start + d), width) for d in (-1, 0, 1)]
    _, ring_after, _ = terms(rings, source, at(start - 1), width, ahead)
    same, after, own_first = terms(rings, source, at(start), width, turned)
    tail = row_of((ROWS, width)) == ROWS - 1

    def advance(g, previous_group, next_group, carry):
        partial, own, previous, turned = carry
        following = sides_of(source, next_group, width)
        same, after, later = terms(rings, source, g, width, turned)
        finish(previous_group, partial + jnp.where(tail, later, own))
        return same + shifted_rows(previous, after), later, after, following

    carry = (same + shifted_rows(ring_after, after), own_first, after, following)
    if start + count <= period:
        body = lambda g, carry: advance(g, g - 1, jnp.minimum(g + 1, period - 1), carry)
        carry = lax.fori_loop(start + 1, start + count, body, carry, unroll=UNROLL)
    else:
        for n in range(start + 1, start + count):
            carry = advance(at(n), at(n - 1), at(n + 1), carry)
    partial, own, _, turned = carry
    if count == period:
        later = own_first
    else:
        later = terms(rings, source, at(start + count), width, turned)[2]
    finish(at(start + count - 1), partial + jnp.where(tail, later, own))


def step(rings, inv, source, target, start, count, subtract):
    def finish(g, total):
        rows = group_rows(g)
        moved = inv[rows] * total
        target[rows] = source[rows] - moved if subtract else moved

    sweep(rings, source, start, count, source.shape[1], finish)


def early_kernel(ax, ay, bly, nx, nxy, nxm, lxy, rxm, inv, c0, c1, c2):
    groups = c0.shape[0] // ROWS - 1
    rings = (ax, ay, bly, nx, nxy, nxm, lxy, rxm)
    step(rings, inv, c0, c1, 2, groups - 4, True)
    step(rings, inv, c1, c2, 3, groups - 6, False)


def basis_kernel(
    masks, outer_center, edges, made, send_a, send_b, recv_a, recv_b, rows_a, rows_b,
    ax_in, ay_in, bly_in, nx_in, nxy_in, nxm_in, lxy_in, rxm_in, inv_in, c0_in, center_in, c1_in, c2_in,
    c3, c4, gram_ref, ax, ay, bly, nx, nxy, nxm, lxy, rxm, inv, c0, center, c1, c2,
):
    row_count, col_count = center.shape
    tiles = col_count // LANES
    wide = col_count + LANES
    block_rows = row_count // BLOCK
    groups = row_count // ROWS
    blk, sub = own_place()
    even_sub, even_blk = (sub % 2) == 0, (blk % 2) == 0
    row8, lane8 = row_of((ROWS, wide)), lane_of((ROWS, wide))
    row1, lane1 = row_of((ROWS, LANES)), lane_of((ROWS, LANES))
    first, last, outer = pl.ds(0, LANES), pl.ds(col_count - LANES, LANES), pl.ds(col_count, LANES)
    west_edge, east_edge = lane1 == 0, lane1 == LANES - 1

    def at(g):
        return pl.ds(pl.multiple_of(g * ROWS, ROWS), ROWS)

    pieces = []
    for pair in range(3):
        rows = slice(pair * ROWS, (pair + 1) * ROWS)
        below = jnp.where(even_blk, rows_a[rows], rows_b[rows])
        above = jnp.where(even_blk, rows_b[rows], rows_a[rows])
        pieces.append(jnp.where(row8 < 4, below, pltpu.roll(above, 4, 0)))
        pieces.append(jnp.where(row8 < 4, pltpu.roll(below, 4, 0), above))
    out_f, out_x, out_y, out_xy, out_xm, out_c = pieces
    flux_below, flux_above = out_x[3:4], out_y[4:5]

    def edge_group(side, k):
        strip = 0 if side == 0 else groups // 4 - 1
        sides = side_tiles(send_a, send_b, recv_a, recv_b, even_sub, at(strip))
        get = lambda f: edges[pl.ds((side * 5 + f) * ROWS, ROWS)]
        full = [
            jnp.concatenate([get(e), outer_tile(sides[2], sides[3], f, k)], axis=1)
            for e, f in ((0, 1), (2, 3), (3, 4), (4, 7))
        ]
        mask = masks[mask_group(0 if side == 0 else block_rows - 1)]
        return full, mask, force_with_sides(made[pl.ds(2 * side * ROWS, ROWS)], mask, sides, k)

    (_, _, _, flux_first), mask_first, force_first = edge_group(0, 0)
    (x_last, xy_last, xm_last, flux_last), mask_last, force_last = edge_group(1, 3)
    mask_below, mask_above = masks[mask_group(block_rows)], masks[mask_group(block_rows + 1)]

    def inverse_of(mask, total):
        return jnp.where(mask > 0.0, 1.0 / jnp.where(total > 0.0, total, 1.0), 0.0)

    head = row8 == 0
    own_first = pl.ds(0, ROWS)
    up = []
    for ring, out in ((nx, out_x), (nxy, out_xy), (nxm, out_xm)):
        moved = jnp.where(head, down(out), ring[own_first])
        ring[own_first] = moved
        up.append(moved)
    total = jnp.concatenate([center[own_first], outer_center[own_first]], axis=1)
    total = total + jnp.where(head, up[0] + left(up[1]) + right(up[2]), 0.0)
    center[own_first] = total[:, :col_count]
    inverse = inverse_of(mask_first, total)
    inv[own_first] = inverse
    c0[own_first] = inverse * (force_first - jnp.where(head, 0.5 * mask_first * flux_above, 0.0))
    own_last = pl.ds(row_count - ROWS, ROWS)
    c0[own_last] = inv[own_last] * (
        force_last + jnp.where(row8 == ROWS - 1, 0.5 * mask_last * flux_below, 0.0)
    )
    ring_rows = pl.ds(row_count, ROWS)
    up = [
        jnp.where(head, down(before), down(out))
        for before, out in ((x_last, out_x), (xy_last, out_xy), (xm_last, out_xm))
    ]
    left_y = left(out_y)
    for ring, value in (
        (ax, out_x), (ay, out_y), (bly, left_y), (nx, up[0]), (nxy, up[1]), (nxm, up[2]),
        (lxy, left(out_xy)), (rxm, right(out_xm)),
    ):
        ring[ring_rows] = value
    crosses_west = (row8 != 4) & ((lane8 == 0) | (lane8 == col_count))
    crosses_east = (row8 != 4) & ((lane8 == col_count - 1) | (lane8 == wide - 1))
    total = out_c + jnp.where(head, up[0], 0.0)
    total = total + jnp.where(crosses_west, left_y, 0.0)
    total = total + jnp.where(head | crosses_west, left(up[1]), 0.0)
    total = total + jnp.where(head | crosses_east, right(up[2]), 0.0)
    inverse = inverse_of(jnp.where(row8 < 4, mask_below, mask_above), total)
    out_f = out_f - jnp.where(head, 0.5 * mask_below * flux_last[ROWS - 1 : ROWS], 0.0)
    out_f = out_f + jnp.where(row8 == ROWS - 1, 0.5 * mask_above * flux_first[0:1], 0.0)
    inv[ring_rows] = inverse
    c0[ring_rows] = inverse * out_f

    rings = (ax, ay, bly, nx, nxy, nxm, lxy, rxm)
    step(rings, inv, c0, c1, groups - 2, 5, True)
    step(rings, inv, c1, c2, groups - 3, 7, False)
    step(rings, inv, c2, c3, 0, groups + 1, False)

    cols = pl.ds(0, col_count)

    def last_finish(g, total):
        c4[at(g)] = inv[at(g), cols] * total

    sweep(rings, c3, 0, groups, col_count, last_finish)

    def add_products(g, sums):
        rows = at(g)
        basis = [ref[rows, cols] for ref in (c0, c1, c2, c3)] + [c4[rows]]
        weight = center[rows]
        weighted = [weight * b for b in basis]
        new = []
        for (i, j), total in zip(PAIRS, sums):
            product = basis[i] * weighted[j]
            part = product[:, :LANES]
            for t in range(1, tiles):
                part = part + product[:, t * LANES : (t + 1) * LANES]
            new.append(total + part)
        return tuple(new)

    zero = jnp.zeros((ROWS, LANES), F32)
    sums = lax.fori_loop(0, groups, add_products, tuple(zero for _ in PAIRS), unroll=2)

    count = len(PAIRS)
    high = jnp.zeros((2 * ROWS, LANES), F32)
    low = high
    place = row_of((2 * ROWS, LANES))
    for index, total in enumerate(sums):
        error = jnp.zeros_like(total)
        for shift in (4, 2, 1):
            total, rounding = two_sum(total, pltpu.roll(total, shift, 0))
            error = error + pltpu.roll(error, shift, 0) + rounding
        high = jnp.where(place == index, total[0:1], high)
        low = jnp.where(place == index, error[0:1], low)
    scale = (2.0 * LANES) * jnp.max(jnp.abs(high), axis=1, keepdims=True)
    coarse = (high + scale) - scale
    low = jnp.sum(low + (high - coarse), axis=1, keepdims=True)
    high = jnp.sum(coarse, axis=1, keepdims=True)
    lane2 = lane_of((2 * ROWS, LANES))
    packed = jnp.where(lane2 == place, high, jnp.where(lane2 == place + LANES // 2, low, 0.0))
    gram_ref[...] = jnp.broadcast_to(jnp.sum(packed, axis=0, keepdims=True), gram_ref.shape)


def finish_kernel(gram_ref, c0, c1, c2, c3, c4, center_ref, height_out, residual_out, height_ref, residual_ref, sems):
    lane1 = lane_of((1, LANES))
    high = gram_ref[...]
    low = jnp.zeros_like(high)
    while high.shape[0] > 1:
        half = high.shape[0] // 2
        high, rounding = two_sum(high[:half], high[half:])
        low = low[:half] + low[half:] + rounding
    entries = high + (low + pltpu.roll(high, LANES // 2, 1))
    size = ITERS + 1
    gram = {}
    for index, (i, j) in enumerate(PAIRS):
        entry = jnp.sum(jnp.where(lane1 == index, entries, 0.0), axis=1, keepdims=True)
        gram[i, j] = entry
        gram[j, i] = entry
    zero = jnp.zeros((1, 1), F32)
    one = jnp.ones((1, 1), F32)

    def image(coefs):
        result = [zero, coefs[0] + coefs[1]]
        for j in range(2, size):
            own = coefs[j] if j < size - 1 else zero
            result.append(own - coefs[j - 1])
        return result

    def form(one_side, products):
        total = zero
        for a, b in zip(one_side, products):
            total = total + a * b
        return total

    scaled = [one] + [zero] * (size - 1)
    search = [zero] * size
    height = [zero] * size
    rho_old, sigma = one, zero
    for iteration in range(ITERS):
        limit = iteration + 1
        products = []
        for j in range(size):
            total = zero
            for i in range(limit):
                total = total + scaled[i] * gram[i, j]
            products.append(total)
        rho = form(scaled[:limit], products)
        curvature = form(image(scaled)[: limit + 1], products)
        beta = rho / rho_old
        sigma = curvature - beta * beta * sigma
        alpha = rho / sigma
        rho_old = rho
        search = [s + beta * q for s, q in zip(scaled, search)]
        height = [h + alpha * q for h, q in zip(height, search)]
        scaled = [s - alpha * q for s, q in zip(scaled, image(search))]

    def combine(g, _):
        rows = pl.ds(pl.multiple_of(g * ROWS, ROWS), ROWS)
        cols = pl.ds(0, center_ref.shape[1])
        basis = [ref[rows, cols] for ref in (c0, c1, c2, c3, c4)]
        total = height[0] * basis[0]
        for j in range(1, size - 1):
            total = total + height[j] * basis[j]
        height_ref[rows] = total
        total = scaled[0] * basis[0]
        for j in range(1, size):
            total = total + scaled[j] * basis[j]
        residual_ref[rows] = center_ref[rows] * total
        return 0

    row_count = center_ref.shape[0]
    part = row_count // PARTS
    copies = []
    for p in range(PARTS):
        lax.fori_loop(p * part // ROWS, (p + 1) * part // ROWS, combine, 0, unroll=4)
        rows = pl.ds(p * part, part)
        for i, (src, dst) in enumerate(((height_ref, height_out), (residual_ref, residual_out))):
            copies.append(pltpu.make_async_copy(src.at[rows], dst.at[rows], sems.at[i, p]))
            copies[-1].start()
    for copy in copies:
        copy.wait()


def swap(value, axis, parity):
    peers = lax.axis_size(axis)
    pairs = []
    for i in range(parity, peers - 1, 2):
        pairs += [(i, i + 1), (i + 1, i)]
    return lax.ppermute(value, axis, pairs)


def body(u_flow, v_flow, thickness, depth_levels, block_ocean, coef_x, coef_y, coef_xy, coef_xm, extra_diagonal):
    levels, row_count, col_count = u_flow.shape
    wide = col_count + LANES
    shape = lambda *dims: pltpu.VMEM(dims, F32)
    final = jax.ShapeDtypeStruct((row_count, col_count), F32)
    far = lambda array: pltpu.with_memory_space_constraint(array, pltpu.HBM)
    plane = shape(row_count, col_count)
    ring = shape(row_count + ROWS, wide)
    strip = shape(row_count // 4, LANES)
    flow = pltpu.VMEM((levels, row_count, col_count), F32)
    field = pltpu.VMEM((row_count, col_count), F32)
    flux_u, flux_v, extra, edges, send_a, send_b, *rings, masks = pl.pallas_call(
        flux_kernel,
        out_shape=(plane, plane, plane, shape(10 * ROWS, col_count), strip, strip)
        + (ring,) * 4
        + (shape((row_count // BLOCK + 2) * ROWS, wide),),
        in_specs=[HBM] * 10,
        out_specs=(VMEM,) * 11,
        scratch_shapes=[flow, flow, pltpu.VMEM((row_count, col_count), jnp.int32)]
        + [pltpu.SMEM(thickness.shape, F32), pltpu.SMEM(block_ocean.shape, jnp.int32)]
        + [pltpu.SemaphoreType.DMA((2, row_count // PIECE)), pltpu.SemaphoreType.DMA((6,)), pltpu.SemaphoreType.DMA((2,))],
        compiler_params=pltpu.CompilerParams(vmem_limit_bytes=FLUX_LIMIT),
        name="flux",
    )(
        *[far(a) for a in (thickness, block_ocean, u_flow, v_flow, depth_levels, coef_x, coef_y, coef_xy, coef_xm, extra_diagonal)],
    )
    recv_a, recv_b = swap(send_a, "sub", 0), swap(send_b, "sub", 1)
    ax, ay, axy, axm = rings
    fp, cp, made, *moved, inv, c0 = pl.pallas_call(
        prepare_kernel,
        out_shape=(plane, plane, shape(4 * ROWS, col_count)) + (ring,) * 8,
        in_specs=[VMEM] * 8,
        out_specs=(VMEM,) * 11,
        compiler_params=pltpu.CompilerParams(vmem_limit_bytes=8 << 20),
        cost_estimate=pl.CostEstimate(flops=10 << 20, bytes_accessed=4 << 20, transcendentals=0),
        name="prepare",
    )(flux_u, flux_v, extra, masks, ax, ay, axy, axm)
    edge = shape(3 * ROWS, wide)
    edge_a, edge_b = pl.pallas_call(
        functools.partial(edge_kernel, row_count=row_count),
        out_shape=(edge, edge),
        in_specs=[VMEM] * 7,
        out_specs=(VMEM,) * 2,
        compiler_params=pltpu.CompilerParams(vmem_limit_bytes=8 << 20),
        name="edge",
    )(masks, edges, made, send_a, send_b, recv_a, recv_b)
    rows_a, rows_b = swap(edge_a, "blk", 0), swap(edge_b, "blk", 1)
    outer_center, *rings = pl.pallas_call(
        widen_kernel,
        out_shape=(shape(row_count, LANES),) + (ring,) * 10 + (plane,),
        in_specs=[VMEM] * 17,
        out_specs=(VMEM,) * 12,
        input_output_aliases={6 + i: 1 + i for i in range(11)},
        compiler_params=pltpu.CompilerParams(vmem_limit_bytes=8 << 20),
        cost_estimate=pl.CostEstimate(flops=10 << 20, bytes_accessed=4 << 20, transcendentals=0),
        name="widen",
    )(masks, fp, send_a, send_b, recv_a, recv_b, ax, ay, *moved, inv, c0, cp)
    devices = lax.axis_size("blk") * lax.axis_size("sub")
    early = pl.pallas_call(
        early_kernel,
        out_shape=(ring, ring),
        in_specs=[VMEM] * 10,
        out_specs=(VMEM,) * 2,
        compiler_params=pltpu.CompilerParams(vmem_limit_bytes=8 << 20),
        cost_estimate=pl.CostEstimate(flops=10 << 20, bytes_accessed=4 << 20, transcendentals=0),
        name="early",
    )(*rings[:10])
    c3, c4, gram, *rest = pl.pallas_call(
        basis_kernel,
        out_shape=(ring, plane, shape(devices, LANES)) + (ring,) * 10 + (plane, ring, ring),
        in_specs=[VMEM] * 23,
        out_specs=(VMEM,) * 16,
        input_output_aliases={10 + i: 3 + i for i in range(13)},
        compiler_params=pltpu.CompilerParams(vmem_limit_bytes=8 << 20),
        name="basis",
    )(masks, outer_center, edges, made, send_a, send_b, recv_a, recv_b, rows_a, rows_b, *rings, *early)
    c0, center, c1, c2 = rest[-4:]
    gram = lax.all_to_all(gram, ("blk", "sub"), 0, 0, tiled=True)
    return pl.pallas_call(
        finish_kernel,
        out_shape=(final, final),
        in_specs=[VMEM] * 7,
        out_specs=(HBM,) * 2,
        scratch_shapes=[field, field, pltpu.SemaphoreType.DMA((2, PARTS))],
        compiler_params=pltpu.CompilerParams(vmem_limit_bytes=8 << 20),
        name="finish",
    )(gram, c0, c1, c2, c3, c4, center)


def solution(mesh):
    placed = (
        P(None, "blk", "sub"),
        P(None, "blk", "sub"),
        P(),
        P("blk", "sub"),
        P(),
        P("blk", "sub"),
        P("blk", "sub"),
        P("blk", "sub"),
        P("blk", "sub"),
        P("blk", "sub"),
    )
    return jax.shard_map(
        body,
        mesh=mesh,
        in_specs=placed,
        out_specs=(P("blk", "sub"), P("blk", "sub")),
        check_vma=False,
    )
```

```python
import functools

import jax
import jax.numpy as jnp
from jax import lax
from jax.experimental import pallas as pl
from jax.experimental.pallas import tpu as pltpu
from jax.sharding import PartitionSpec as P

BLOCK = 128
ITERS = 4
HALO = ITERS
LANES = 128
ROWS = 8
CHUNK = 32
PIECE = 32
AHEAD = 3
UNROLL = 8
PARTS = 4
F32 = jnp.float32
FLUX_LIMIT = 40 << 20
VMEM = pl.BlockSpec(memory_space=pltpu.VMEM)
HBM = pl.BlockSpec(memory_space=pltpu.HBM)
PAIRS = [(i, j) for i in range(ITERS) for j in range(i, ITERS + 1)]


def lane_of(shape):
    return lax.broadcasted_iota(jnp.int32, shape, len(shape) - 1)


def row_of(shape):
    return lax.broadcasted_iota(jnp.int32, shape, len(shape) - 2)


def shifted_rows(before, here):
    return jnp.where(row_of(here.shape) == 0, before, here)


def left(value):
    return pltpu.roll(value, 1, 1)


def right(value):
    return pltpu.roll(value, value.shape[1] - 1, 1)


def down(value):
    return pltpu.roll(value, 1, 0)


def two_sum(a, b):
    total = a + b
    other = total - a
    return total, (a - (total - other)) + (b - other)


def ocean_at(ocean_ref, row, col):
    block_rows, block_cols = ocean_ref.shape
    inside = (row >= 0) & (row < block_rows) & (col >= 0) & (col < block_cols)
    entry = ocean_ref[jnp.clip(row, 0, block_rows - 1), jnp.clip(col, 0, block_cols - 1)]
    return jnp.where(inside & (entry == 1), 1.0, 0.0).astype(F32)


def flux_kernel(
    thick_hbm, ocean_hbm, u_hbm, v_hbm, depth_hbm, cx_hbm, cy_hbm, cxy_hbm, cxm_hbm, ex_hbm,
    fu, fv, ex, edge_ref, pack_a, pack_b, ax, ay, axy, axm, masks,
    u_buf, v_buf, depth, thick, ocean, sems, coef_sem, small_sem,
):
    levels, row_count, col_count = u_buf.shape
    tiles = col_count // LANES
    chunks = row_count // CHUNK
    pieces = row_count // PIECE
    groups = row_count // ROWS
    steps = CHUNK // ROWS
    blk, sub = own_place()
    block_rows = row_count // BLOCK
    own = (pl.ds(0, row_count), pl.ds(0, col_count))
    coef_copies = [
        pltpu.make_async_copy(src, dst, coef_sem.at[i])
        for i, (src, dst) in enumerate(
            [
                (depth_hbm, depth), (ex_hbm, ex), (cx_hbm, ax.at[own]), (cy_hbm, ay.at[own]),
                (cxy_hbm, axy.at[own]), (cxm_hbm, axm.at[own]),
            ]
        )
    ]

    def flow_copies(c):
        rows = pl.ds(pl.multiple_of(c * PIECE, PIECE), PIECE)
        return (
            pltpu.make_async_copy(u_hbm.at[:, rows, :], u_buf.at[:, rows, :], sems.at[0, c]),
            pltpu.make_async_copy(v_hbm.at[:, rows, :], v_buf.at[:, rows, :], sems.at[1, c]),
        )

    small_copies = [
        pltpu.make_async_copy(src, dst, small_sem.at[i])
        for i, (src, dst) in enumerate([(thick_hbm, thick), (ocean_hbm, ocean)])
    ]
    for copy in small_copies:
        copy.start()
    coef_copies[0].start()
    for copy in flow_copies(0):
        copy.start()
    for copy in coef_copies[1:]:
        copy.start()
    for c in range(1, AHEAD):
        for copy in flow_copies(c):
            copy.start()
    for copy in small_copies:
        copy.wait()
    for place in range(block_rows + 2):
        block_row = blk * block_rows + (place if place <= block_rows else -1)
        masks[mask_group(place)] = jnp.broadcast_to(
            mask_row(ocean, block_row, sub, tiles), (ROWS, col_count + LANES)
        )
    coef_copies[0].wait()

    row8 = row_of((ROWS, 2 * LANES))
    lane8 = lane_of((ROWS, 2 * LANES))
    lane1 = lane_of((ROWS, LANES))
    first, final = pl.ds(0, LANES), pl.ds(col_count - LANES, LANES)
    even = (sub % 2) == 0

    def ends(ref, rows):
        return jnp.concatenate([ref[rows, first], ref[rows, final]], axis=1)

    def at(g):
        return pl.ds(pl.multiple_of(g * ROWS, ROWS), ROWS)

    def west_of(value):
        return jnp.where(lane8 == 0, 0.0, left(value))

    def east_of(value):
        return jnp.where(lane8 == 2 * LANES - 1, 0.0, right(value))

    def rolled_fields(rows):
        return [
            down(v) for v in (ends(ax, rows), west_of(ends(axy, rows)), east_of(ends(axm, rows)), ends(fu, rows))
        ]

    def sum_group(g):
        rows = at(g)
        for t in range(tiles):
            lanes = pl.ds(t * LANES, LANES)
            mask = masks[mask_group(g * ROWS // BLOCK), lanes]
            deep = depth[rows, lanes]
            total_u = jnp.zeros((ROWS, LANES), F32)
            total_v = total_u
            for k in range(levels):
                active = jnp.where(deep > k, thick[k], 0.0)
                total_u = total_u + active * u_buf[k, rows, lanes]
                total_v = total_v + active * v_buf[k, rows, lanes]
            fu[rows, lanes] = mask * total_u
            fv[rows, lanes] = mask * total_v

    def group_work(g, k, before):
        rows = at(g)
        here_x, here_y, here_xy, here_xm, here_u, here_v = [ends(ref, rows) for ref in (ax, ay, axy, axm, fu, fv)]
        west_xy, east_xm, west_y = west_of(here_xy), east_of(here_xm), west_of(here_y)
        rolled = [down(v) for v in (here_x, west_xy, east_xm, here_u)]
        up_x, up_west, up_east, up_u = [shifted_rows(a, b) for a, b in zip(before, rolled)]
        total = ends(ex, rows) + here_x
        total = total + up_x
        total = total + here_y
        total = total + west_y
        total = total + here_xy
        total = total + up_west
        total = total + here_xm
        total = total + up_east
        after = ends(fu, at(jnp.minimum(g + 1, groups - 1)))
        after = jnp.where(g + 1 < groups, pltpu.roll(after, ROWS - 1, 0), 0.0)
        below = jnp.where(row8 == ROWS - 1, after, pltpu.roll(here_u, ROWS - 1, 0))
        change = 0.5 * ((below - up_u) + (east_of(here_v) - west_of(here_v)))
        mask = ends(masks, mask_group(g * ROWS // BLOCK))
        partial = mask * change
        fields = [partial, here_x, here_y, here_xy, here_xm, total, here_v, here_u]
        to_west = jnp.zeros((ROWS, LANES), F32)
        to_east = to_west
        for f, field in enumerate(fields):
            lane = 4 * f + 32 * k
            chosen = (lane1 >= lane) & (lane1 < lane + HALO)
            to_west = jnp.where(chosen, pltpu.roll(field[:, :LANES], lane, 1), to_west)
            to_east = jnp.where(chosen, pltpu.roll(field[:, -LANES:], (lane + HALO) % LANES, 1), to_east)
        lane = 4 * 6 + 32 * k
        extra = pltpu.roll(here_xm[:, :LANES], (lane + 1 - HALO) % LANES, 1)
        to_west = jnp.where(lane1 == lane + 1, extra, to_west)
        extra = pltpu.roll(here_xy[:, -LANES:], (lane + HALO + 1) % LANES, 1)
        to_east = jnp.where(lane1 == lane, extra, to_east)
        packed = at(g // 4)
        for_a = jnp.where(even, to_east, to_west)
        for_b = jnp.where(even, to_west, to_east)
        if k == 0:
            pack_a[packed] = for_a
            pack_b[packed] = for_b
        else:
            pack_a[packed] = pack_a[packed] + for_a
            pack_b[packed] = pack_b[packed] + for_b
        return rolled

    def work_from(g, k):
        before = rolled_fields(at(jnp.maximum(g - 1, 0)))
        return group_work(g, k, [jnp.where(g > 0, b, 0.0) for b in before])

    def chunk(c, _):
        def piece(i, _):
            p = c * (CHUNK // PIECE) + i
            for copy in flow_copies(p):
                copy.wait()

            @pl.when(p + AHEAD < pieces)
            def _():
                for copy in flow_copies(p + AHEAD):
                    copy.start()

            for j in range(PIECE // ROWS):
                sum_group(p * (PIECE // ROWS) + j)
            return 0

        lax.fori_loop(0, CHUNK // PIECE, piece, 0)

        @pl.when(c == 0)
        def _():
            for copy in coef_copies[1:]:
                copy.wait()

        @pl.when(c > 0)
        def _():
            work_from(c * steps - 1, 3)

        carry = work_from(c * steps, 0)
        for k in range(1, steps - 1):
            carry = group_work(c * steps + k, k, carry)
        return 0

    lax.fori_loop(0, chunks, chunk, 0)
    work_from(groups - 1, 3)
    for side, base in enumerate((0, row_count - ROWS)):
        rows = pl.ds(base, ROWS)
        for f, field in enumerate(
            [ax[rows, own[1]], ay[rows, own[1]], axy[rows, own[1]], axm[rows, own[1]], fu[rows]]
        ):
            edge_ref[pl.ds((side * 5 + f) * ROWS, ROWS)] = field


def side_tiles(send_a, send_b, recv_a, recv_b, even, packed):
    own_a, own_b, got_a, got_b = send_a[packed], send_b[packed], recv_a[packed], recv_b[packed]
    pick = lambda a, b: jnp.where(even, a, b)
    return pick(own_b, own_a), pick(own_a, own_b), pick(got_b, got_a), pick(got_a, got_b)


def outer_tile(from_west, from_east, f, k):
    lane1 = lane_of(from_west.shape)
    at = 4 * f + 32 * k
    east = pltpu.roll(from_east, (-at) % LANES, 1)
    west = pltpu.roll(from_west, (LANES - HALO - at) % LANES, 1)
    tile = jnp.where(lane1 < HALO, east, jnp.where(lane1 >= LANES - HALO, west, 0.0))
    if f == 3:
        extra = pltpu.roll(from_west, (LANES - HALO - 1 - 4 * 6 - 32 * k) % LANES, 1)
        tile = jnp.where(lane1 == LANES - HALO - 1, extra, tile)
    if f == 4:
        extra = pltpu.roll(from_east, (HALO - 4 * 6 - 1 - 32 * k) % LANES, 1)
        tile = jnp.where(lane1 == HALO, extra, tile)
    return tile


def force_with_sides(partial, mask, sides, k):
    own_west, own_east, from_west, from_east = sides
    lane1 = lane_of(own_west.shape)
    first, last = 4 * 6 + 32 * k, 4 * 6 + 3 + 32 * k
    outer = outer_tile(from_west, from_east, 0, k)
    tail = pltpu.roll(own_east, (-last) % LANES, 1)
    head = pltpu.roll(own_west, (LANES - 1 - first) % LANES, 1)
    change = jnp.where(lane1 == 0, -tail, jnp.where(lane1 == LANES - 1, head, 0.0))
    outer = outer + 0.5 * mask[:, -LANES:] * change
    begin = partial[:, :LANES] - jnp.where(
        lane1 == 0, 0.5 * mask[:, :LANES] * pltpu.roll(from_west, (-last) % LANES, 1), 0.0
    )
    middle = partial[:, LANES:-LANES]
    end = partial[:, -LANES:] + jnp.where(
        lane1 == LANES - 1,
        0.5 * mask[:, -2 * LANES : -LANES] * pltpu.roll(from_east, (LANES - 1 - first) % LANES, 1),
        0.0,
    )
    return jnp.concatenate([begin, middle, end, outer], axis=1)


def own_place():
    return lax.axis_index("blk"), lax.axis_index("sub")


def mask_group(block):
    if isinstance(block, int):
        return pl.ds(block * ROWS, ROWS)
    return pl.ds(pl.multiple_of(block * ROWS, ROWS), ROWS)


def mask_row(ocean, block_row, sub, tiles):
    lane1 = lane_of((1, LANES))
    parts = [jnp.full((1, LANES), ocean_at(ocean, block_row, sub * tiles + t), F32) for t in range(tiles)]
    east = ocean_at(ocean, block_row, (sub + 1) * tiles)
    west = ocean_at(ocean, block_row, sub * tiles - 1)
    parts.append(jnp.where(lane1 < LANES // 2, east, west))
    return jnp.concatenate(parts, axis=1)


def edge_kernel(masks, edges, made, send_a, send_b, recv_a, recv_b, rows_a, rows_b, *, row_count):
    col_count = edges.shape[1]
    tiles = col_count // LANES
    block_rows = row_count // BLOCK
    blk, sub = own_place()
    even_sub, even_blk = (sub % 2) == 0, (blk % 2) == 0
    shape = (ROWS, col_count + LANES)
    row8, lane8 = row_of(shape), lane_of(shape)
    crosses_west = (lane8 == 0) | (lane8 == col_count)
    crosses_east = (lane8 == col_count - 1) | (lane8 == col_count + LANES - 1)
    strips = row_count // (4 * ROWS)
    results = []
    for side, top in enumerate((True, False)):
        k = 0 if top else 3
        packed = pl.ds(0 if top else (strips - 1) * ROWS, ROWS)
        rows = [edges[pl.ds((side * 5 + f) * ROWS, ROWS)] for f in range(5)]
        rows = [made[pl.ds(2 * side * ROWS, ROWS)], *rows[:4], made[pl.ds((2 * side + 1) * ROWS, ROWS)], rows[4]]
        sides = side_tiles(send_a, send_b, recv_a, recv_b, even_sub, packed)
        mask = masks[mask_group(0 if top else block_rows - 1)]
        fields = [force_with_sides(rows[0], mask, sides, k)]
        for f in range(1, 6):
            fields.append(jnp.concatenate([rows[f], outer_tile(sides[2], sides[3], f, k)], axis=1))
        flux = jnp.concatenate([rows[6], outer_tile(sides[2], sides[3], 7, k)], axis=1)
        if top:
            fields[1] = jnp.where(row8 == 3, pltpu.roll(flux, 3, 0), fields[1])
            half = lambda v: v
        else:
            extra = jnp.where(crosses_west, left(fields[2]) + left(down(fields[3])), 0.0)
            extra = extra + jnp.where(crosses_east, right(down(fields[4])), 0.0)
            fields[5] = fields[5] + jnp.where(row8 == 4, extra, 0.0)
            fields[2] = jnp.where(row8 == 4, pltpu.roll(flux, 5, 0), fields[2])
            half = lambda v: pltpu.roll(v, 4, 0)
        pieces = []
        for pair in range(3):
            one, two = half(fields[2 * pair]), half(fields[2 * pair + 1])
            pieces.append(jnp.where(row8 < 4, one, pltpu.roll(two, 4, 0)))
        results.append(pieces)
    for pair in range(3):
        rows = slice(pair * ROWS, (pair + 1) * ROWS)
        rows_a[rows] = jnp.where(even_blk, results[1][pair], results[0][pair])
        rows_b[rows] = jnp.where(even_blk, results[0][pair], results[1][pair])


def prepare_kernel(
    fu, fv, ex, masks, ax, ay, axy, axm,
    fp, cp, edge_ref, bly, nx, nxy, nxm, lxy, rxm, inv, c0,
):
    row_count, col_count = fp.shape
    groups = row_count // ROWS
    cols = pl.ds(0, col_count)
    row8, lane8 = row_of((ROWS, col_count)), lane_of((ROWS, col_count))
    begin, end = lane8 == 0, lane8 == col_count - 1
    head, tail = row8 == 0, row8 == ROWS - 1

    def body(g, before):
        rows = group_rows(g)
        here_x, here_y, here_xy, here_xm = [ref[rows, cols] for ref in (ax, ay, axy, axm)]
        here_u, here_v = fu[rows], fv[rows]
        west_y = jnp.where(begin, 0.0, left(here_y))
        west_xy = jnp.where(begin, 0.0, left(here_xy))
        east_xm = jnp.where(end, 0.0, right(here_xm))
        rolled = tuple(down(v) for v in (here_x, here_xy, here_xm, west_xy, east_xm, here_u))
        up_x, up_xy, up_xm, up_west, up_east, up_u = [jnp.where(head, a, b) for a, b in zip(before, rolled)]
        total = ex[rows] + here_x
        total = total + up_x
        total = total + here_y
        total = total + west_y
        total = total + here_xy
        total = total + up_west
        total = total + here_xm
        total = total + up_east
        cp[rows] = total
        for ring, value in ((bly, west_y), (nx, up_x), (nxy, up_xy), (nxm, up_xm), (lxy, west_xy), (rxm, east_xm)):
            ring[rows, cols] = value
        after = pltpu.roll(fu[group_rows(jnp.minimum(g + 1, groups - 1))], ROWS - 1, 0)
        below = jnp.where(tail, jnp.where(g + 1 < groups, after, 0.0), pltpu.roll(here_u, ROWS - 1, 0))
        across = jnp.where(end, 0.0, right(here_v)) - jnp.where(begin, 0.0, left(here_v))
        mask = masks[mask_group(g * ROWS // BLOCK), cols]
        partial = mask * (0.5 * ((below - up_u) + across))
        fp[rows] = partial
        inverse = mask * (1.0 / total)
        inv[rows, cols] = inverse
        c0[rows, cols] = partial * inverse
        return rolled

    zero = jnp.zeros((ROWS, col_count), F32)
    lax.fori_loop(0, groups, body, (zero,) * 6, unroll=4)
    for side, base in enumerate((0, row_count - ROWS)):
        rows = pl.ds(base, ROWS)
        edge_ref[pl.ds(2 * side * ROWS, ROWS)] = fp[rows]
        edge_ref[pl.ds((2 * side + 1) * ROWS, ROWS)] = cp[rows]


def widen_kernel(
    masks, fp, send_a, send_b, recv_a, recv_b,
    ax_in, ay_in, bly_in, nx_in, nxy_in, nxm_in, lxy_in, rxm_in, inv_in, c0_in, center_in,
    outer_center, ax, ay, bly, nx, nxy, nxm, lxy, rxm, inv, c0, center,
):
    row_count, col_count = fp.shape
    tiles = col_count // LANES
    block_rows = row_count // BLOCK
    groups = row_count // ROWS
    blk, sub = own_place()
    even_sub = (sub % 2) == 0
    lane1 = lane_of((ROWS, LANES))
    first, last, outer = pl.ds(0, LANES), pl.ds(col_count - LANES, LANES), pl.ds(col_count, LANES)
    west_edge, east_edge = lane1 == 0, lane1 == LANES - 1

    def at(g):
        return pl.ds(pl.multiple_of(g * ROWS, ROWS), ROWS)

    def widen(p, before):
        sides = side_tiles(send_a, send_b, recv_a, recv_b, even_sub, at(p))
        own_west, own_east, from_west, from_east = sides
        for k in range(4):
            g = 4 * p + k
            rows = at(g)
            new_f, new_x, new_y, new_xy, new_xm, new_c = [outer_tile(from_west, from_east, f, k) for f in range(6)]
            end_y = pltpu.roll(own_east, (-(4 * 2 + 3 + 32 * k)) % LANES, 1)
            end_xy = pltpu.roll(own_east, (-(4 * 3 + 3 + 32 * k)) % LANES, 1)
            begin_xm = pltpu.roll(own_west, (LANES - 1 - 4 * 4 - 32 * k) % LANES, 1)
            left_y, left_xy, right_xm = left(new_y), left(new_xy), right(new_xm)
            outer_y = jnp.where(west_edge, end_y, left_y)
            outer_xy = jnp.where(west_edge, end_xy, left_xy)
            outer_xm = jnp.where(east_edge, begin_xm, right_xm)
            rolled = [down(v) for v in (new_x, new_xy, new_xm, outer_xy, outer_xm, left_xy, right_xm)]
            up_x, up_xy, up_xm, up_outer_xy, up_outer_xm, up_left, up_right = [
                shifted_rows(a, b) for a, b in zip(before, rolled)
            ]
            before = rolled
            ax[rows, outer] = new_x
            ay[rows, outer] = new_y
            bly[rows, outer] = outer_y
            lxy[rows, outer] = outer_xy
            rxm[rows, outer] = outer_xm
            nx[rows, outer] = up_x
            nxy[rows, outer] = up_xy
            nxm[rows, outer] = up_xm
            bly[rows, first] = jnp.where(west_edge, left_y, bly[rows, first])
            lxy[rows, first] = jnp.where(west_edge, left_xy, lxy[rows, first])
            rxm[rows, last] = jnp.where(east_edge, right_xm, rxm[rows, last])
            center_first = center[rows, first] + jnp.where(west_edge, left_y + up_left, 0.0)
            center_last = center[rows, last] + jnp.where(east_edge, up_right, 0.0)
            center_outer = new_c + jnp.where(west_edge, outer_y + up_outer_xy, 0.0)
            center_outer = center_outer + jnp.where(east_edge, up_outer_xm, 0.0)
            center[rows, first] = center_first
            center[rows, last] = center_last
            outer_center[rows] = center_outer
            block = mask_group(g * ROWS // BLOCK)
            mask_first, mask_last, mask_outer = masks[block, first], masks[block, last], masks[block, outer]
            near, far = 4 * 6 + 32 * k, 4 * 6 + 3 + 32 * k
            tail = pltpu.roll(own_east, (-far) % LANES, 1)
            begin = pltpu.roll(own_west, (LANES - 1 - near) % LANES, 1)
            from_w = pltpu.roll(from_west, (-far) % LANES, 1)
            from_e = pltpu.roll(from_east, (LANES - 1 - near) % LANES, 1)
            force_first = fp[rows, first] - jnp.where(west_edge, (0.5 * mask_first) * from_w, 0.0)
            force_last = fp[rows, last] + jnp.where(east_edge, (0.5 * mask_last) * from_e, 0.0)
            change = jnp.where(west_edge, -tail, jnp.where(east_edge, begin, 0.0))
            force_outer = new_f + 0.5 * mask_outer * change
            inverse_first = mask_first * (1.0 / center_first)
            inverse_last = mask_last * (1.0 / center_last)
            inverse_outer = jnp.where(mask_outer > 0.0, 1.0 / jnp.where(center_outer > 0.0, center_outer, 1.0), 0.0)
            inv[rows, first] = inverse_first
            inv[rows, last] = inverse_last
            inv[rows, outer] = inverse_outer
            c0[rows, first] = force_first * inverse_first
            c0[rows, last] = force_last * inverse_last
            c0[rows, outer] = force_outer * inverse_outer
        return tuple(before)

    zero = jnp.zeros((ROWS, LANES), F32)
    lax.fori_loop(0, groups // 4, widen, (zero,) * 7)


def group_rows(g):
    return pl.ds(g * ROWS if isinstance(g, int) else pl.multiple_of(g * ROWS, ROWS), ROWS)


def sides_of(source, g, width):
    value = source[group_rows(g)]
    return left(value)[:, :width], right(value)[:, :width]


def terms(rings, source, g, width, turned):
    ax, ay, bly, nx, nxy, nxm, lxy, rxm = rings
    rows, cols = group_rows(g), pl.ds(0, width)
    west, east = turned
    here = source[rows, cols]
    same = ay[rows, cols] * east + bly[rows, cols] * west
    after = ax[rows, cols] * here + lxy[rows, cols] * west + rxm[rows, cols] * east
    before = nx[rows, cols] * here + nxy[rows, cols] * east + nxm[rows, cols] * west
    return same, down(after), pltpu.roll(before, ROWS - 1, 0)


def sweep(rings, source, start, count, width, finish):
    period = source.shape[0] // ROWS
    at = lambda n: n % period
    ahead, turned, following = [sides_of(source, at(start + d), width) for d in (-1, 0, 1)]
    _, ring_after, _ = terms(rings, source, at(start - 1), width, ahead)
    same, after, own_first = terms(rings, source, at(start), width, turned)
    tail = row_of((ROWS, width)) == ROWS - 1

    def advance(g, previous_group, next_group, carry):
        partial, own, previous, turned = carry
        following = sides_of(source, next_group, width)
        same, after, later = terms(rings, source, g, width, turned)
        finish(previous_group, partial + jnp.where(tail, later, own))
        return same + shifted_rows(previous, after), later, after, following

    carry = (same + shifted_rows(ring_after, after), own_first, after, following)
    if start + count <= period:
        body = lambda g, carry: advance(g, g - 1, jnp.minimum(g + 1, period - 1), carry)
        carry = lax.fori_loop(start + 1, start + count, body, carry, unroll=UNROLL)
    else:
        for n in range(start + 1, start + count):
            carry = advance(at(n), at(n - 1), at(n + 1), carry)
    partial, own, _, turned = carry
    if count == period:
        later = own_first
    else:
        later = terms(rings, source, at(start + count), width, turned)[2]
    finish(at(start + count - 1), partial + jnp.where(tail, later, own))


def step(rings, inv, source, target, start, count, subtract):
    def finish(g, total):
        rows = group_rows(g)
        moved = inv[rows] * total
        target[rows] = source[rows] - moved if subtract else moved

    sweep(rings, source, start, count, source.shape[1], finish)


def early_kernel(ax, ay, bly, nx, nxy, nxm, lxy, rxm, inv, c0, c1, c2):
    groups = c0.shape[0] // ROWS - 1
    rings = (ax, ay, bly, nx, nxy, nxm, lxy, rxm)
    step(rings, inv, c0, c1, 2, groups - 4, True)
    step(rings, inv, c1, c2, 3, groups - 6, False)


def basis_kernel(
    masks, outer_center, edges, made, send_a, send_b, recv_a, recv_b, rows_a, rows_b,
    ax_in, ay_in, bly_in, nx_in, nxy_in, nxm_in, lxy_in, rxm_in, inv_in, c0_in, center_in, c1_in, c2_in,
    c3, c4, gram_ref, ax, ay, bly, nx, nxy, nxm, lxy, rxm, inv, c0, center, c1, c2,
):
    row_count, col_count = center.shape
    tiles = col_count // LANES
    wide = col_count + LANES
    block_rows = row_count // BLOCK
    groups = row_count // ROWS
    blk, sub = own_place()
    even_sub, even_blk = (sub % 2) == 0, (blk % 2) == 0
    row8, lane8 = row_of((ROWS, wide)), lane_of((ROWS, wide))
    row1, lane1 = row_of((ROWS, LANES)), lane_of((ROWS, LANES))
    first, last, outer = pl.ds(0, LANES), pl.ds(col_count - LANES, LANES), pl.ds(col_count, LANES)
    west_edge, east_edge = lane1 == 0, lane1 == LANES - 1

    def at(g):
        return pl.ds(pl.multiple_of(g * ROWS, ROWS), ROWS)

    pieces = []
    for pair in range(3):
        rows = slice(pair * ROWS, (pair + 1) * ROWS)
        below = jnp.where(even_blk, rows_a[rows], rows_b[rows])
        above = jnp.where(even_blk, rows_b[rows], rows_a[rows])
        pieces.append(jnp.where(row8 < 4, below, pltpu.roll(above, 4, 0)))
        pieces.append(jnp.where(row8 < 4, pltpu.roll(below, 4, 0), above))
    out_f, out_x, out_y, out_xy, out_xm, out_c = pieces
    flux_below, flux_above = out_x[3:4], out_y[4:5]

    def edge_group(side, k):
        strip = 0 if side == 0 else groups // 4 - 1
        sides = side_tiles(send_a, send_b, recv_a, recv_b, even_sub, at(strip))
        get = lambda f: edges[pl.ds((side * 5 + f) * ROWS, ROWS)]
        full = [
            jnp.concatenate([get(e), outer_tile(sides[2], sides[3], f, k)], axis=1)
            for e, f in ((0, 1), (2, 3), (3, 4), (4, 7))
        ]
        mask = masks[mask_group(0 if side == 0 else block_rows - 1)]
        return full, mask, force_with_sides(made[pl.ds(2 * side * ROWS, ROWS)], mask, sides, k)

    (_, _, _, flux_first), mask_first, force_first = edge_group(0, 0)
    (x_last, xy_last, xm_last, flux_last), mask_last, force_last = edge_group(1, 3)
    mask_below, mask_above = masks[mask_group(block_rows)], masks[mask_group(block_rows + 1)]

    def inverse_of(mask, total):
        return jnp.where(mask > 0.0, 1.0 / jnp.where(total > 0.0, total, 1.0), 0.0)

    head = row8 == 0
    own_first = pl.ds(0, ROWS)
    up = []
    for ring, out in ((nx, out_x), (nxy, out_xy), (nxm, out_xm)):
        moved = jnp.where(head, down(out), ring[own_first])
        ring[own_first] = moved
        up.append(moved)
    total = jnp.concatenate([center[own_first], outer_center[own_first]], axis=1)
    total = total + jnp.where(head, up[0] + left(up[1]) + right(up[2]), 0.0)
    center[own_first] = total[:, :col_count]
    inverse = inverse_of(mask_first, total)
    inv[own_first] = inverse
    c0[own_first] = inverse * (force_first - jnp.where(head, 0.5 * mask_first * flux_above, 0.0))
    own_last = pl.ds(row_count - ROWS, ROWS)
    c0[own_last] = inv[own_last] * (
        force_last + jnp.where(row8 == ROWS - 1, 0.5 * mask_last * flux_below, 0.0)
    )
    ring_rows = pl.ds(row_count, ROWS)
    up = [
        jnp.where(head, down(before), down(out))
        for before, out in ((x_last, out_x), (xy_last, out_xy), (xm_last, out_xm))
    ]
    left_y = left(out_y)
    for ring, value in (
        (ax, out_x), (ay, out_y), (bly, left_y), (nx, up[0]), (nxy, up[1]), (nxm, up[2]),
        (lxy, left(out_xy)), (rxm, right(out_xm)),
    ):
        ring[ring_rows] = value
    crosses_west = (row8 != 4) & ((lane8 == 0) | (lane8 == col_count))
    crosses_east = (row8 != 4) & ((lane8 == col_count - 1) | (lane8 == wide - 1))
    total = out_c + jnp.where(head, up[0], 0.0)
    total = total + jnp.where(crosses_west, left_y, 0.0)
    total = total + jnp.where(head | crosses_west, left(up[1]), 0.0)
    total = total + jnp.where(head | crosses_east, right(up[2]), 0.0)
    inverse = inverse_of(jnp.where(row8 < 4, mask_below, mask_above), total)
    out_f = out_f - jnp.where(head, 0.5 * mask_below * flux_last[ROWS - 1 : ROWS], 0.0)
    out_f = out_f + jnp.where(row8 == ROWS - 1, 0.5 * mask_above * flux_first[0:1], 0.0)
    inv[ring_rows] = inverse
    c0[ring_rows] = inverse * out_f

    rings = (ax, ay, bly, nx, nxy, nxm, lxy, rxm)
    step(rings, inv, c0, c1, groups - 2, 5, True)
    step(rings, inv, c1, c2, groups - 3, 7, False)
    step(rings, inv, c2, c3, 0, groups + 1, False)

    cols = pl.ds(0, col_count)

    def last_finish(g, total):
        c4[at(g)] = inv[at(g), cols] * total

    sweep(rings, c3, 0, groups, col_count, last_finish)

    def add_products(g, sums):
        rows = at(g)
        basis = [ref[rows, cols] for ref in (c0, c1, c2, c3)] + [c4[rows]]
        weight = center[rows]
        weighted = [weight * b for b in basis]
        new = []
        for (i, j), total in zip(PAIRS, sums):
            product = basis[i] * weighted[j]
            part = product[:, :LANES]
            for t in range(1, tiles):
                part = part + product[:, t * LANES : (t + 1) * LANES]
            new.append(total + part)
        return tuple(new)

    zero = jnp.zeros((ROWS, LANES), F32)
    sums = lax.fori_loop(0, groups, add_products, tuple(zero for _ in PAIRS), unroll=2)

    count = len(PAIRS)
    high = jnp.zeros((2 * ROWS, LANES), F32)
    low = high
    place = row_of((2 * ROWS, LANES))
    for index, total in enumerate(sums):
        error = jnp.zeros_like(total)
        for shift in (4, 2, 1):
            total, rounding = two_sum(total, pltpu.roll(total, shift, 0))
            error = error + pltpu.roll(error, shift, 0) + rounding
        high = jnp.where(place == index, total[0:1], high)
        low = jnp.where(place == index, error[0:1], low)
    scale = (2.0 * LANES) * jnp.max(jnp.abs(high), axis=1, keepdims=True)
    coarse = (high + scale) - scale
    low = jnp.sum(low + (high - coarse), axis=1, keepdims=True)
    high = jnp.sum(coarse, axis=1, keepdims=True)
    lane2 = lane_of((2 * ROWS, LANES))
    packed = jnp.where(lane2 == place, high, jnp.where(lane2 == place + LANES // 2, low, 0.0))
    gram_ref[...] = jnp.broadcast_to(jnp.sum(packed, axis=0, keepdims=True), gram_ref.shape)


def finish_kernel(gram_ref, c0, c1, c2, c3, c4, center_ref, height_out, residual_out, height_ref, residual_ref, sems):
    lane1 = lane_of((1, LANES))
    high = gram_ref[...]
    low = jnp.zeros_like(high)
    while high.shape[0] > 1:
        half = high.shape[0] // 2
        high, rounding = two_sum(high[:half], high[half:])
        low = low[:half] + low[half:] + rounding
    entries = high + (low + pltpu.roll(high, LANES // 2, 1))
    size = ITERS + 1
    gram = {}
    for index, (i, j) in enumerate(PAIRS):
        entry = jnp.sum(jnp.where(lane1 == index, entries, 0.0), axis=1, keepdims=True)
        gram[i, j] = entry
        gram[j, i] = entry
    zero = jnp.zeros((1, 1), F32)
    one = jnp.ones((1, 1), F32)

    def image(coefs):
        result = [zero, coefs[0] + coefs[1]]
        for j in range(2, size):
            own = coefs[j] if j < size - 1 else zero
            result.append(own - coefs[j - 1])
        return result

    def form(one_side, products):
        total = zero
        for a, b in zip(one_side, products):
            total = total + a * b
        return total

    scaled = [one] + [zero] * (size - 1)
    search = [zero] * size
    height = [zero] * size
    rho_old, sigma = one, zero
    for iteration in range(ITERS):
        limit = iteration + 1
        products = []
        for j in range(size):
            total = zero
            for i in range(limit):
                total = total + scaled[i] * gram[i, j]
            products.append(total)
        rho = form(scaled[:limit], products)
        curvature = form(image(scaled)[: limit + 1], products)
        beta = rho / rho_old
        sigma = curvature - beta * beta * sigma
        alpha = rho / sigma
        rho_old = rho
        search = [s + beta * q for s, q in zip(scaled, search)]
        height = [h + alpha * q for h, q in zip(height, search)]
        scaled = [s - alpha * q for s, q in zip(scaled, image(search))]

    def combine(g, _):
        rows = pl.ds(pl.multiple_of(g * ROWS, ROWS), ROWS)
        cols = pl.ds(0, center_ref.shape[1])
        basis = [ref[rows, cols] for ref in (c0, c1, c2, c3, c4)]
        total = height[0] * basis[0]
        for j in range(1, size - 1):
            total = total + height[j] * basis[j]
        height_ref[rows] = total
        total = scaled[0] * basis[0]
        for j in range(1, size):
            total = total + scaled[j] * basis[j]
        residual_ref[rows] = center_ref[rows] * total
        return 0

    row_count = center_ref.shape[0]
    part = row_count // PARTS
    copies = []
    for p in range(PARTS):
        lax.fori_loop(p * part // ROWS, (p + 1) * part // ROWS, combine, 0, unroll=4)
        rows = pl.ds(p * part, part)
        for i, (src, dst) in enumerate(((height_ref, height_out), (residual_ref, residual_out))):
            copies.append(pltpu.make_async_copy(src.at[rows], dst.at[rows], sems.at[i, p]))
            copies[-1].start()
    for copy in copies:
        copy.wait()


def swap(value, axis, parity):
    peers = lax.axis_size(axis)
    pairs = []
    for i in range(parity, peers - 1, 2):
        pairs += [(i, i + 1), (i + 1, i)]
    return lax.ppermute(value, axis, pairs)


def body(u_flow, v_flow, thickness, depth_levels, block_ocean, coef_x, coef_y, coef_xy, coef_xm, extra_diagonal):
    levels, row_count, col_count = u_flow.shape
    wide = col_count + LANES
    shape = lambda *dims: pltpu.VMEM(dims, F32)
    final = jax.ShapeDtypeStruct((row_count, col_count), F32)
    far = lambda array: pltpu.with_memory_space_constraint(array, pltpu.HBM)
    plane = shape(row_count, col_count)
    ring = shape(row_count + ROWS, wide)
    strip = shape(row_count // 4, LANES)
    flow = pltpu.VMEM((levels, row_count, col_count), F32)
    field = pltpu.VMEM((row_count, col_count), F32)
    flux_u, flux_v, extra, edges, send_a, send_b, *rings, masks = pl.pallas_call(
        flux_kernel,
        out_shape=(plane, plane, plane, shape(10 * ROWS, col_count), strip, strip)
        + (ring,) * 4
        + (shape((row_count // BLOCK + 2) * ROWS, wide),),
        in_specs=[HBM] * 10,
        out_specs=(VMEM,) * 11,
        scratch_shapes=[flow, flow, pltpu.VMEM((row_count, col_count), jnp.int32)]
        + [pltpu.SMEM(thickness.shape, F32), pltpu.SMEM(block_ocean.shape, jnp.int32)]
        + [pltpu.SemaphoreType.DMA((2, row_count // PIECE)), pltpu.SemaphoreType.DMA((6,)), pltpu.SemaphoreType.DMA((2,))],
        compiler_params=pltpu.CompilerParams(vmem_limit_bytes=FLUX_LIMIT),
        name="flux",
    )(
        *[far(a) for a in (thickness, block_ocean, u_flow, v_flow, depth_levels, coef_x, coef_y, coef_xy, coef_xm, extra_diagonal)],
    )
    recv_a, recv_b = swap(send_a, "sub", 0), swap(send_b, "sub", 1)
    ax, ay, axy, axm = rings
    fp, cp, made, *moved, inv, c0 = pl.pallas_call(
        prepare_kernel,
        out_shape=(plane, plane, shape(4 * ROWS, col_count)) + (ring,) * 8,
        in_specs=[VMEM] * 8,
        out_specs=(VMEM,) * 11,
        compiler_params=pltpu.CompilerParams(vmem_limit_bytes=8 << 20),
        cost_estimate=pl.CostEstimate(flops=10 << 20, bytes_accessed=4 << 20, transcendentals=0),
        name="prepare",
    )(flux_u, flux_v, extra, masks, ax, ay, axy, axm)
    edge = shape(3 * ROWS, wide)
    edge_a, edge_b = pl.pallas_call(
        functools.partial(edge_kernel, row_count=row_count),
        out_shape=(edge, edge),
        in_specs=[VMEM] * 7,
        out_specs=(VMEM,) * 2,
        compiler_params=pltpu.CompilerParams(vmem_limit_bytes=8 << 20),
        name="edge",
    )(masks, edges, made, send_a, send_b, recv_a, recv_b)
    rows_a, rows_b = swap(edge_a, "blk", 0), swap(edge_b, "blk", 1)
    outer_center, *rings = pl.pallas_call(
        widen_kernel,
        out_shape=(shape(row_count, LANES),) + (ring,) * 10 + (plane,),
        in_specs=[VMEM] * 17,
        out_specs=(VMEM,) * 12,
        input_output_aliases={6 + i: 1 + i for i in range(11)},
        compiler_params=pltpu.CompilerParams(vmem_limit_bytes=8 << 20),
        cost_estimate=pl.CostEstimate(flops=10 << 20, bytes_accessed=4 << 20, transcendentals=0),
        name="widen",
    )(masks, fp, send_a, send_b, recv_a, recv_b, ax, ay, *moved, inv, c0, cp)
    devices = lax.axis_size("blk") * lax.axis_size("sub")
    early = pl.pallas_call(
        early_kernel,
        out_shape=(ring, ring),
        in_specs=[VMEM] * 10,
        out_specs=(VMEM,) * 2,
        compiler_params=pltpu.CompilerParams(vmem_limit_bytes=8 << 20),
        cost_estimate=pl.CostEstimate(flops=10 << 20, bytes_accessed=4 << 20, transcendentals=0),
        name="early",
    )(*rings[:10])
    c3, c4, gram, *rest = pl.pallas_call(
        basis_kernel,
        out_shape=(ring, plane, shape(devices, LANES)) + (ring,) * 10 + (plane, ring, ring),
        in_specs=[VMEM] * 23,
        out_specs=(VMEM,) * 16,
        input_output_aliases={10 + i: 3 + i for i in range(13)},
        compiler_params=pltpu.CompilerParams(vmem_limit_bytes=8 << 20),
        name="basis",
    )(masks, outer_center, edges, made, send_a, send_b, recv_a, recv_b, rows_a, rows_b, *rings, *early)
    c0, center, c1, c2 = rest[-4:]
    gram = lax.all_to_all(gram, ("blk", "sub"), 0, 0, tiled=True)
    return pl.pallas_call(
        finish_kernel,
        out_shape=(final, final),
        in_specs=[VMEM] * 7,
        out_specs=(HBM,) * 2,
        scratch_shapes=[field, field, pltpu.SemaphoreType.DMA((2, PARTS))],
        compiler_params=pltpu.CompilerParams(vmem_limit_bytes=8 << 20),
        name="finish",
    )(gram, c0, c1, c2, c3, c4, center)


def solution(mesh):
    placed = (
        P(None, "blk", "sub"),
        P(None, "blk", "sub"),
        P(),
        P("blk", "sub"),
        P(),
        P("blk", "sub"),
        P("blk", "sub"),
        P("blk", "sub"),
        P("blk", "sub"),
        P("blk", "sub"),
    )
    return jax.shard_map(
        body,
        mesh=mesh,
        in_specs=placed,
        out_specs=(P("blk", "sub"), P("blk", "sub")),
        check_vma=False,
    )
```
